128 devices in a mesh: gx: 8 (over x, core), gy: 16 (over z, y).
Axes of the slice: x: 4, y: 4, z: 4, core: 2. Of those that a mesh axis runs over, the one named last changes fastest.
Arguments:
- samples: float32 [16384, 2, 128], P(('gx', 'gy')), may hold values from -6 to 6
- kernel: float32 [16384, 3, 4, 128], P(('gx', 'gy')), may hold values from 0.1 to 1
- offsets: int32 [16384, 3, 128], P(('gx', 'gy')), may hold values from 0 to 4
- owners: int32 [16384, 1], P(('gx', 'gy')), may hold values from 0 to 127; in each aligned block of 128 rows (0 to 127, 128 to 255, ...) at most 2 rows name the same one
- tile_ids: int32 [16384], P(('gx', 'gy')), may hold values from 0 to 863
- deapod_first: float32 [192], replicated, may hold values from 1 to 3
- deapod_second: float32 [192], P('gx'), may hold values from 1 to 3
- deapod_third: float32 [192], P('gy'), may hold values from 1 to 3
Outputs:
- image: float32 [2, 192, 192, 192], P(None, 'gy', 'gx')
The draws below stay inside these ranges and needn't reach their ends.
Inputs may be any that keep to these rules, and one draw needn't show every extreme that they name: `owners`: among the 128 blocks of one device no owner is named more than 2 times, and in some device one owner is named exactly 2 times. `tile_ids`: tiles are numbered row, column, depth over the owner's 6 x 3 x 48 tiles. `offsets`: each sample's kernel lies inside its block's tile.
All inputs are finite; a program needn't handle non-finite values.
Results may differ from the reference program's by a relative error of at most 0.0003.
Values sent between devices are 32-bit elements; how exact they have to be, the bound alone decides.
A program may use at most 128 MiB of HBM per device.

```python
import math
import jax
import jax.numpy as jnp
import numpy as np
from jax import lax

NX = 384
NY = 384
NZ = 384
TILE = 8
KW = 4
SPB = 128
B_DEV = 128
CAP = 2
BLOCKS = 16384
TILES_DEV = 864
IX = 192
IY = 192
IZ = 192
N_GX = 8
N_GY = 16
DEVICES = 128


def with_ends(drawn, rng, least, largest):
    index_at = [jax.random.randint(jax.random.fold_in(rng, axis), (), 0, length) for axis, length in enumerate(drawn.shape)]
    longest = drawn.shape.index(max(drawn.shape))
    beside = index_at[:longest] + [(index_at[longest] + 1) % drawn.shape[longest]] + index_at[longest + 1:]
    return drawn.at[tuple(index_at)].set(least).at[tuple(beside)].set(largest)


def block_levels(own_key, extent, cuts, smallest, top_value):
    factor_of = 1.0
    for dim, blocks in cuts:
        draws = jax.random.uniform(jax.random.fold_in(jax.random.fold_in(own_key, 6), dim), (blocks,), jnp.float32, smallest / len(cuts), top_value / len(cuts))
        factor_of = factor_of * jnp.repeat(jnp.exp(draws), extent[dim] // blocks).reshape((-1,) + (1,) * (len(extent) - 1 - dim))
    return factor_of


def routed_block(key, own, number, rows, count, top, most, lean):
    order = jax.random.permutation(key, count)
    crowded, common = portions_of(count, rows * top, most, lean, True), portions_of(count, rows * top, most, lean, False)
    places = jnp.arange(count)

    def named(tallies, offset_by):
        used = int((tallies > 0).sum())
        fixed = max(1, used // 4)
        moved = fixed + (places - fixed + offset_by * (used - fixed)) % max(1, count - fixed)
        return jnp.zeros((count,), jnp.int32).at[order[jnp.where(places < fixed, places, moved)]].set(jnp.asarray(tallies, jnp.int32))

    tallies = jnp.where(number % 4 == 0, named(crowded, number // 4), named(common, number - number // 4 - 1))
    mixed = jax.random.permutation(jax.random.fold_in(own, 3), count)
    source_of, sink = mixed[0:count // 2 * 2:2], mixed[1:count // 2 * 2:2]
    margin = jnp.minimum(tallies[source_of] - 1, most - tallies[sink]) // 2
    margin = jnp.where((source_of == order[0]) | (sink == order[0]) | (tallies[sink] == 0), 0, jnp.maximum(margin, 0))
    moved = jax.random.randint(jax.random.fold_in(own, 4), (count // 2,), 0, 1 << 20) % (margin + 1)
    tallies = tallies.at[source_of].add(-moved).at[sink].add(moved)
    members = jnp.searchsorted(jnp.cumsum(tallies), jnp.arange(rows * top), side="right").astype(jnp.int32)
    listing = members.reshape(top, rows).T
    listing = listing[jax.random.permutation(jax.random.fold_in(own, 1), rows)]
    offset_by = jax.random.randint(jax.random.fold_in(own, 2), (rows, 1), 0, top)
    return jnp.take_along_axis(listing, (jnp.arange(top)[None, :] + offset_by) % top, axis=1)


def portions_of(amount, total, limit, lean, full):
    weights = [(1 << 20) // math.isqrt(grade ** lean) + 1 for grade in range(1, amount + 1)]
    largest = limit if full else min(limit, max(-(-total // amount), total * weights[0] // sum(weights)))
    least = 1 if total - largest >= amount - 1 else 0
    holding, rest = [largest] + [least] * (amount - 1), total - largest - least * (amount - 1)
    while rest > 0:
        free = [i for i in range(1, amount) if holding[i] < largest] or [i for i in range(1, amount) if holding[i] < limit]
        whole, left = sum([weights[i] for i in free]), rest
        for i in free:
            addition = min(limit - holding[i], max(1, left * weights[i] // whole), rest)
            holding[i] = holding[i] + addition
            rest = rest - addition
    return np.array(holding)


def normal_values(stream_key, shape, scale, reach, split=(), held_as=jnp.bfloat16):
    entries = jax.random.normal(stream_key, shape, jnp.float32) * scale
    if len(split) > 0:
        entries = block_levels(stream_key, shape, split, -0.22, 0.18) * entries
    return jnp.clip(entries, min=-reach, max=reach).astype(held_as)


def setup_inputs(seed: int = 0) -> dict:
    key_of = jax.random.split(jax.random.key(seed), 9)
    samples = normal_values(key_of[0], (BLOCKS, 2, SPB), 1.0, 6.0, ((0, 128),), jnp.float32)
    kernel = jnp.clip(jnp.exp(math.log(1.0) - 2.3025851 * jax.random.uniform(key_of[1], (BLOCKS, 3, KW, SPB), jnp.float32) ** block_levels(key_of[1], (BLOCKS, 3, KW, SPB), ((0, 128),), -0.2, 0.2)), 0.1, 1.0)
    offsets = with_ends(jax.random.randint(key_of[2], (BLOCKS, 3, SPB), 0, TILE - KW + 1), jax.random.fold_in(key_of[2], 1), 0, TILE - KW).astype(jnp.int32)
    owners_keys = jax.random.split(jax.random.fold_in(key_of[3], 1), BLOCKS // B_DEV)
    owners_turns = jax.random.permutation(jax.random.fold_in(key_of[3], 3), BLOCKS // B_DEV)
    owners = jax.vmap(lambda own, number: routed_block(jax.random.fold_in(key_of[3], 2), own, number, B_DEV, DEVICES, 1, CAP, 2))(owners_keys, owners_turns).reshape((BLOCKS, 1))
    tile_ids = with_ends(jax.random.randint(key_of[4], (BLOCKS,), 0, TILES_DEV), jax.random.fold_in(key_of[4], 1), 0, TILES_DEV - 1).astype(jnp.int32)
    deapod_first = jnp.clip(jnp.exp(jax.random.uniform(key_of[5], (IX,), jnp.float32, math.log(1.0), math.log(3.0))), 1.0, 3.0)
    deapod_second = jnp.clip(jnp.exp(math.log(3.0) - 1.0986123 * jax.random.uniform(key_of[6], (IY,), jnp.float32) ** block_levels(key_of[6], (IY,), ((0, 8),), -0.2, 0.2)), 1.0, 3.0)
    deapod_third = jnp.clip(jnp.exp(math.log(3.0) - 1.0986123 * jax.random.uniform(key_of[7], (IZ,), jnp.float32) ** block_levels(key_of[7], (IZ,), ((0, 16),), -0.2, 0.2)), 1.0, 3.0)
    return {"samples": samples, "kernel": kernel, "offsets": offsets, "owners": owners, "tile_ids": tile_ids, "deapod_first": deapod_first, "deapod_second": deapod_second, "deapod_third": deapod_third}


def fourier_table(length, outputs):
    freq = jnp.arange(length, dtype=jnp.int32) - length // 2
    image_pos = jnp.arange(outputs, dtype=jnp.int32) - outputs // 2
    phase_steps = jnp.mod(freq[:, None] * image_pos[None, :], length)
    phases = phase_steps.astype(jnp.float32) * (2.0 * math.pi / length)
    norming = 1.0 / math.sqrt(length)
    return (jnp.cos(phases) * norming, jnp.sin(phases) * norming)

def complex_apply(real_part, imag_part, cos_table, sin_table, pattern):
    highest = lax.Precision.HIGHEST
    real_cos = jnp.einsum(pattern, real_part, cos_table, precision=highest)
    real_sin = jnp.einsum(pattern, real_part, sin_table, precision=highest)
    imag_cos = jnp.einsum(pattern, imag_part, cos_table, precision=highest)
    imag_sin = jnp.einsum(pattern, imag_part, sin_table, precision=highest)
    return jnp.stack((real_cos - imag_sin, real_sin + imag_cos))

def spread(values, kernel, starts, tile_width):
    kernel_taps = jnp.arange(kernel.shape[2], dtype=jnp.float32)
    cell_axis = jnp.arange(tile_width, dtype=jnp.float32)
    matches = (cell_axis[None, None, :, None, None] == starts[:, :, None, None, :] + kernel_taps[None, None, None, :, None]).astype(jnp.float32)
    placed = lax.optimization_barrier(jnp.sum(matches * kernel[:, :, None, :, :], axis=3))
    plane_weight = placed[:, 0][:, :, None, :] * placed[:, 1][:, None, :, :]
    depth_weight = values[:, :, None, :] * placed[:, 2][:, None, :, :]
    return jnp.einsum('nijs,ncls->ncijl', plane_weight, depth_weight, precision=lax.Precision.HIGHEST)

def reference(samples, kernel, offsets, owners, tile_ids, deapod_first, deapod_second, deapod_third):
    device_count = N_GX * N_GY
    per_device = samples.shape[0] // device_count
    block_width = samples.shape[2]
    kernel_taps = kernel.shape[2]

    def spread_group(operands):
        return spread(operands[0], operands[1], operands[2], TILE)
    pieces = lax.map(spread_group, (samples.reshape(device_count, per_device, 2, block_width), kernel.reshape(device_count, per_device, 3, kernel_taps, block_width), offsets.astype(jnp.float32).reshape(device_count, per_device, 3, block_width)))
    pieces = pieces.reshape(-1, 2, TILE, TILE, TILE)
    tile_rows = NX // (TILE * N_GX)
    tile_cols = NY // (TILE * N_GY)
    tile_depth = NZ // TILE
    target = owners[:, 0]
    global_row = target // N_GY * tile_rows + tile_ids // (tile_cols * tile_depth)
    global_col = target % N_GY * tile_cols + tile_ids // tile_depth % tile_cols
    slab_slot = global_col * tile_depth + tile_ids % tile_depth
    slab_tiles = NY // TILE * tile_depth
    cos_z, sin_z = fourier_table(NZ, NZ // 2)
    cos_y, sin_y = fourier_table(NY, NY // 2)
    cos_x, sin_x = fourier_table(NX, NX // 2)

    def add_row(accumulated, tile_row):
        chosen = jnp.where(global_row == tile_row, slab_slot, slab_tiles)
        slab = jnp.zeros((slab_tiles, 2, TILE, TILE, TILE), jnp.float32).at[chosen].add(pieces, mode='drop')
        slab = slab.reshape(NY // TILE, tile_depth, 2, TILE, TILE, TILE).transpose(2, 3, 0, 4, 1, 5).reshape(2, TILE, NY, NZ)
        along_z = complex_apply(slab[0], slab[1], cos_z, sin_z, 'xyk,km->xym')
        along_y = complex_apply(along_z[0], along_z[1], cos_y, sin_y, 'xym,yq->xqm')
        rows_cos = lax.dynamic_slice_in_dim(cos_x, tile_row * TILE, TILE, 0)
        rows_sin = lax.dynamic_slice_in_dim(sin_x, tile_row * TILE, TILE, 0)
        along_x = complex_apply(along_y[0], along_y[1], rows_cos, rows_sin, 'xqm,xp->mqp')
        return (accumulated + along_x, None)
    start = jnp.zeros((2, NZ // 2, NY // 2, NX // 2), jnp.float32)
    accumulated, _ = lax.scan(add_row, start, jnp.arange(NX // TILE, dtype=jnp.int32))
    return accumulated * deapod_third[None, :, None, None] * deapod_second[None, None, :, None] * deapod_first[None, None, None, :]
```

```python
import math

import jax
import jax.numpy as jnp
import ml_dtypes
import numpy as np
from jax import lax
from jax.experimental import pallas as pl
from jax.experimental.pallas import tpu as pltpu
from jax.sharding import PartitionSpec as P

N = 384
M = 192
DEVICES = 128
ROWS, COLS = 8, 16
BLOCKS = 128
TILES = 864
SLOT_ROWS = 17
ROUNDS = 3
MESH = pl.DeviceIdType.MESH
F32 = jnp.float32
BF16 = jnp.bfloat16


def angles(cells, images):
    steps = np.mod((cells[:, None] - N // 2) * (images[None, :] - M // 2), N)
    phases = steps.astype(np.float64) * (2.0 * math.pi / N)
    return np.cos(phases) / math.sqrt(N), np.sin(phases) / math.sqrt(N)


def halves(table):
    table = table.astype(np.float32)
    high = table.astype(ml_dtypes.bfloat16)
    low = (table - high.astype(np.float32)).astype(ml_dtypes.bfloat16)
    return high, low


def left_table(cells, images):
    cos, sin = angles(cells, images)
    high, low = halves(np.concatenate((cos.T, sin.T)))
    return np.concatenate((high, low, high), axis=1)


def tables():
    every = np.arange(M)
    a, pair, side, low = np.meshgrid(np.arange(3), np.arange(8), np.arange(2), np.arange(4), indexing="ij")
    order = (12 * (2 * pair + side) + 4 * a + low).reshape(-1)
    third = left_table(np.arange(N), order)
    q, g, j = np.meshgrid(np.arange(3), np.arange(COLS), np.arange(8), indexing="ij")
    second = left_table((g * 24 + q * 8 + j).reshape(-1), every)
    turn, lane = np.meshgrid(np.arange(ROUNDS), np.arange(128), indexing="ij")
    source = (lane >> 6) * 4 + (lane & 3)
    cells = source * 48 + (2 * turn + ((lane >> 2) & 1)) * 8 + ((lane >> 3) & 7)
    firsts = []
    for part in angles(cells.reshape(-1), every):
        high, low = halves(part)
        firsts.append(np.concatenate((high, low, high), axis=0))
    return third, second, firsts[0], firsts[1]


def split(value):
    high = value.astype(BF16)
    return high, (value - high.astype(F32)).astype(BF16)


def exchange_bit(value, axis_low, lane_bit):
    count, rows, lanes = value.shape
    shift = 1 << lane_bit
    pairs = value.reshape(count // (2 * axis_low), 2, axis_low * rows, lanes)
    first = pairs[:, 0].reshape(-1, lanes)
    second = pairs[:, 1].reshape(-1, lanes)
    lane = lax.broadcasted_iota(jnp.int32, first.shape, 1)
    upper = (lane & shift) != 0
    new_first = jnp.where(upper, pltpu.roll(second, shift, 1), first)
    new_second = jnp.where(upper, second, pltpu.roll(first, lanes - shift, 1))
    shape = (count // (2 * axis_low), axis_low * rows, lanes)
    out = jnp.stack((new_first.reshape(shape), new_second.reshape(shape)), axis=1)
    return out.reshape(value.shape)


def combine(product):
    rows = product.shape[0] // 2
    lane = lax.broadcasted_iota(jnp.int32, (rows, 128), 1)
    turned = pltpu.roll(product[rows:], 64, 1)
    return product[:rows] + jnp.where(lane < 64, -turned, turned)


NT = (((1,), (1,)), ((), ()))


def spread_kernel(owners, tile_ids, samples, kernel, offsets, out, table):
    out[...] = jnp.zeros_like(out)

    @pl.loop(0, DEVICES)
    def _(d):
        table[0, d] = TILES
        table[1, d] = TILES

    cell = lax.broadcasted_iota(jnp.int32, (8, 128), 0)

    def place(n, dim):
        away = cell - offsets[n, pl.ds(dim, 1), :]
        total = jnp.zeros((8, 128), F32)
        for k in range(4):
            total = jnp.where(away == k, kernel[n, dim, pl.ds(k, 1), :], total)
        return total

    def one(n):
        first, second, third = place(n, 0), place(n, 1), place(n, 2)
        real = samples[n, pl.ds(0, 1), :] * first
        imag = samples[n, pl.ds(1, 1), :] * first
        plane = jnp.concatenate((real, imag), axis=0)
        weight = (plane[:, None, :] * second[None, :, :]).reshape(128, 128)
        high, low = split(weight)
        depth_high, depth_low = split(third)
        left = jnp.concatenate(
            (
                jnp.concatenate((depth_high, depth_high), axis=1),
                jnp.concatenate((depth_low, jnp.zeros_like(depth_low)), axis=1),
            ),
            axis=0,
        )
        right = jnp.concatenate((high, low), axis=1)
        both = lax.dot_general(left, right, NT, preferred_element_type=F32)
        piece = both[:8] + both[8:]
        dest = owners[n]
        seen = (table[0, dest] != TILES).astype(jnp.int32)
        table[seen, dest] = tile_ids[n]
        out[dest, pl.ds(pl.multiple_of(seen * 8, 8), 8), :] = piece

    @pl.loop(0, BLOCKS // 4)
    def _(step):
        for u in range(4):
            one(step * 4 + u)

    lane = lax.broadcasted_iota(jnp.int32, (1, 128), 1)

    @pl.loop(0, DEVICES)
    def _(d):
        out[d, pl.ds(16, 1), :] = jnp.where(lane < 64, table[0, d], table[1, d]).astype(F32)


def spread(owners, tile_ids, samples, kernel, offsets):
    vmem = pl.BlockSpec(memory_space=pltpu.VMEM)
    smem = pl.BlockSpec(memory_space=pltpu.SMEM)
    return pl.pallas_call(
        spread_kernel,
        out_shape=jax.ShapeDtypeStruct((DEVICES, SLOT_ROWS, 128), F32),
        in_specs=[smem, smem, vmem, vmem, vmem],
        out_specs=vmem,
        scratch_shapes=[pltpu.SMEM((2, DEVICES), jnp.int32)],
        compiler_params=pltpu.CompilerParams(vmem_limit_bytes=32 << 20),
        name="spread",
    )(owners, tile_ids, samples, kernel, offsets)


def route_kernel(x, out, send_sem, recv_sem, local_sem):
    gx, gy = lax.axis_index("gx"), lax.axis_index("gy")
    me = gx * COLS + gy
    own = pltpu.make_async_copy(x.at[me], out.at[me], local_sem)
    own.start()

    def copy(peer, lands):
        return pltpu.make_async_remote_copy(
            src_ref=x.at[peer],
            dst_ref=out.at[lands],
            send_sem=send_sem.at[peer],
            recv_sem=recv_sem.at[lands],
            device_id=(peer // COLS, lax.rem(peer, COLS)),
            device_id_type=MESH,
        )

    @pl.loop(1, DEVICES)
    def _(k):
        copy(lax.rem(me + k, DEVICES), me).start()

    own.wait()

    @pl.loop(1, DEVICES)
    def _(k):
        peer = lax.rem(me + DEVICES - k, DEVICES)
        copy(peer, peer).wait_recv()

    @pl.loop(1, DEVICES)
    def _(k):
        peer = lax.rem(me + k, DEVICES)
        copy(peer, me).wait_send()


def route(outbox):
    return pl.pallas_call(
        route_kernel,
        out_shape=jax.ShapeDtypeStruct(outbox.shape, outbox.dtype),
        in_specs=[pl.BlockSpec(memory_space=pltpu.VMEM)],
        out_specs=pl.BlockSpec(memory_space=pltpu.VMEM),
        scratch_shapes=[
            pltpu.SemaphoreType.DMA((DEVICES,)),
            pltpu.SemaphoreType.DMA((DEVICES,)),
            pltpu.SemaphoreType.DMA,
        ],
        compiler_params=pltpu.CompilerParams(has_side_effects=True, vmem_limit_bytes=32 << 20),
        name="route",
    )(outbox)


def gather_kernel(inbox, grid, ids, slots, sem):
    marks = inbox[:, 16, :]
    lane = lax.broadcasted_iota(jnp.int32, (DEVICES, 128), 1)
    source = lax.broadcasted_iota(jnp.int32, (DEVICES, 128), 0)
    marks = jnp.where((lane & 63) == (source & 63), marks, 0.0)
    ids[pl.ds(0, 1), :] = jnp.sum(marks[:64], axis=0, keepdims=True).astype(jnp.int32)
    ids[pl.ds(1, 1), :] = jnp.sum(marks[64:], axis=0, keepdims=True).astype(jnp.int32)
    copy = pltpu.make_async_copy(ids, slots, sem)
    copy.start()
    grid[...] = jnp.zeros_like(grid)
    copy.wait()
    for half in range(2):

        @pl.loop(0, 64 // 4)
        def _(step):
            for u in range(4):
                s = step * 4 + u
                for slot in range(2):
                    t = slots[half, slot * 64 + s]
                    grid[t] = grid[t] + inbox[half * 64 + s, pl.ds(slot * 8, 8), :]


def gather(inbox):
    vmem = pl.BlockSpec(memory_space=pltpu.VMEM)
    return pl.pallas_call(
        gather_kernel,
        out_shape=jax.ShapeDtypeStruct((TILES + 1, 8, 128), F32),
        in_specs=[vmem],
        out_specs=vmem,
        scratch_shapes=[
            pltpu.VMEM((8, 128), jnp.int32),
            pltpu.SMEM((8, 128), jnp.int32),
            pltpu.SemaphoreType.DMA,
        ],
        compiler_params=pltpu.CompilerParams(vmem_limit_bytes=32 << 20),
        name="gather",
    )(inbox)


def transform_kernel(
    grid,
    third,
    second,
    first_cos,
    first_sin,
    out,
    out_z,
    in_y,
    rows_y,
    out_y,
    in_x,
    rows_x,
    z_send,
    z_recv,
    y_send,
    y_recv,
    own_sem,
):
    gx, gy = lax.axis_index("gx"), lax.axis_index("gy")

    def send_z(turn, peer, lands):
        return pltpu.make_async_remote_copy(
            src_ref=out_z.at[turn, peer // 2, lax.rem(peer, 2)],
            dst_ref=in_y.at[turn, lands],
            send_sem=z_send.at[turn, peer],
            recv_sem=z_recv.at[turn, lands],
            device_id=(gx, peer),
            device_id_type=MESH,
        )

    def own_z(turn):
        return pltpu.make_async_copy(
            out_z.at[turn, gy // 2, lax.rem(gy, 2)], in_y.at[turn, gy], own_sem.at[0, turn]
        )

    def send_y(turn, peer, lands):
        return pltpu.make_async_remote_copy(
            src_ref=out_y.at[turn, peer],
            dst_ref=in_x.at[turn, lands],
            send_sem=y_send.at[turn, peer],
            recv_sem=y_recv.at[turn, lands],
            device_id=(peer, gy),
            device_id_type=MESH,
        )

    def own_y(turn):
        return pltpu.make_async_copy(out_y.at[turn, gx], in_x.at[turn, gx], own_sem.at[1, turn])

    row = lax.broadcasted_iota(jnp.int32, (24, 8, 128), 1)
    for turn in range(ROUNDS):
        for q in range(3):
            cells = jnp.concatenate(
                [
                    grid[pl.ds(((2 * turn + r) * 3 + q) * 48, 48)].reshape(N, 128)
                    for r in range(2)
                ],
                axis=1,
            )
            high, low = split(cells)
            product = jnp.dot(
                third[...], jnp.concatenate((high, high, low), axis=0), preferred_element_type=F32
            )
            near = combine(product[:, :128]).reshape(24, 8, 128)
            far = combine(product[:, 128:]).reshape(24, 8, 128)
            even = jnp.where(row < 4, near, pltpu.roll(far, 4, 1))
            odd = jnp.where(row < 4, pltpu.roll(near, 4, 1), far)
            for a in range(3):
                out_z[turn, :, 0, q * 3 + a] = even[a * 8 : a * 8 + 8]
                out_z[turn, :, 1, q * 3 + a] = odd[a * 8 : a * 8 + 8]
        own_z(turn).start()

        @pl.loop(1, COLS)
        def _(k):
            send_z(turn, lax.rem(gy + k, COLS), gy).start()

    for turn in range(ROUNDS):
        own_z(turn).wait()

        @pl.loop(1, COLS)
        def _(k):
            peer = lax.rem(gy + COLS - k, COLS)
            send_z(turn, peer, peer).wait_recv()

        for a in range(3):
            for q in range(3):
                value = in_y[turn, :, q * 3 + a]
                for bit in range(4):
                    value = exchange_bit(value, 1 << bit, 3 + bit)
                high, low = split(value.reshape(128, 128))
                rows_y[pl.ds(a * 128, 128), pl.ds(q * 128, 128)] = high
                rows_y[pl.ds(a * 128, 128), pl.ds(N + q * 128, 128)] = high
                rows_y[pl.ds(a * 128, 128), pl.ds(2 * N + q * 128, 128)] = low
        product = lax.dot_general(second[...], rows_y[...], NT, preferred_element_type=F32)
        for a in range(3):
            part = combine(product[:, a * 128 : a * 128 + 128])
            out_y[turn, :, a] = part.reshape(ROWS, 24, 128)
        own_y(turn).start()

        @pl.loop(1, ROWS)
        def _(k):
            send_y(turn, lax.rem(gx + k, ROWS), gx).start()

    for turn in range(ROUNDS):
        own_y(turn).wait()

        @pl.loop(1, ROWS)
        def _(k):
            peer = lax.rem(gx + ROWS - k, ROWS)
            send_y(turn, peer, peer).wait_recv()

        value = in_x[turn].reshape(ROWS, 72, 128)
        value = exchange_bit(value, 4, 6)
        value = exchange_bit(value, 2, 1)
        value = exchange_bit(value, 1, 0)
        high, low = split(value.reshape(576, 128))
        rows_x[:, pl.ds(turn * 128, 128)] = high
        rows_x[:, pl.ds(N + turn * 128, 128)] = high
        rows_x[:, pl.ds(2 * N + turn * 128, 128)] = low

    cos = jnp.dot(rows_x[...], first_cos[...], preferred_element_type=F32)
    sin = jnp.dot(rows_x[...], first_sin[...], preferred_element_type=F32)
    real = (cos[:288] - sin[288:]).reshape(4, 3, 24, M)
    imag = (sin[:288] + cos[288:]).reshape(4, 3, 24, M)
    for b in range(4):
        for a in range(3):
            out[0, a * 4 + b] = real[b, a]
            out[1, a * 4 + b] = imag[b, a]

    for turn in range(ROUNDS):

        @pl.loop(1, COLS)
        def _(k):
            send_z(turn, lax.rem(gy + k, COLS), gy).wait_send()

        @pl.loop(1, ROWS)
        def _(k):
            send_y(turn, lax.rem(gx + k, ROWS), gx).wait_send()


def transform(grid, third, second, first_cos, first_sin):
    vmem = pl.BlockSpec(memory_space=pltpu.VMEM)
    return pl.pallas_call(
        transform_kernel,
        out_shape=jax.ShapeDtypeStruct((2, 12, 24, M), F32),
        in_specs=[vmem] * 5,
        out_specs=vmem,
        scratch_shapes=[
            pltpu.VMEM((ROUNDS, 8, 2, 9, 8, 128), F32),
            pltpu.VMEM((ROUNDS, COLS, 9, 8, 128), F32),
            pltpu.VMEM((N, 3 * N), BF16),
            pltpu.VMEM((ROUNDS, ROWS, 3, 24, 128), F32),
            pltpu.VMEM((ROUNDS, ROWS, 3, 24, 128), F32),
            pltpu.VMEM((576, 3 * N), BF16),
            pltpu.SemaphoreType.DMA((ROUNDS, COLS)),
            pltpu.SemaphoreType.DMA((ROUNDS, COLS)),
            pltpu.SemaphoreType.DMA((ROUNDS, ROWS)),
            pltpu.SemaphoreType.DMA((ROUNDS, ROWS)),
            pltpu.SemaphoreType.DMA((2, ROUNDS)),
        ],
        compiler_params=pltpu.CompilerParams(has_side_effects=True, vmem_limit_bytes=48 << 20),
        name="transform",
    )(grid, third, second, first_cos, first_sin)


def solution(mesh):
    third, second, first_cos, first_sin = tables()

    def on_device(samples, kernel, offsets, owners, tile_ids, deapod_first, deapod_second, deapod_third):
        outbox = spread(owners[:, 0], tile_ids, samples, kernel, offsets)
        grid = gather(route(outbox))
        along_x = transform(grid, third, second, first_cos, first_sin)
        return (
            along_x
            * deapod_third[None, :, None, None]
            * deapod_second[None, None, :, None]
            * deapod_first[None, None, None, :]
        )

    in_specs = (
        P(("gx", "gy"), None, None),
        P(("gx", "gy"), None, None, None),
        P(("gx", "gy"), None, None),
        P(("gx", "gy"), None),
        P(("gx", "gy")),
        P(),
        P("gx"),
        P("gy"),
    )
    return jax.shard_map(
        on_device, mesh=mesh, in_specs=in_specs, out_specs=P(None, "gy", "gx", None), check_vma=False
    )
```

```python
import math

import jax
import jax.numpy as jnp
import ml_dtypes
import numpy as np
from jax import lax
from jax.experimental import pallas as pl
from jax.experimental.pallas import tpu as pltpu
from jax.sharding import PartitionSpec as P

N = 384
M = 192
DEVICES = 128
ROWS, COLS = 8, 16
BLOCKS = 128
TILES = 864
SLOT_ROWS = 17
ROUNDS = 3
MESH = pl.DeviceIdType.MESH
F32 = jnp.float32
BF16 = jnp.bfloat16


def angles(cells, images):
    steps = np.mod((cells[:, None] - N // 2) * (images[None, :] - M // 2), N)
    phases = steps.astype(np.float64) * (2.0 * math.pi / N)
    return np.cos(phases) / math.sqrt(N), np.sin(phases) / math.sqrt(N)


def halves(table):
    table = table.astype(np.float32)
    high = table.astype(ml_dtypes.bfloat16)
    low = (table - high.astype(np.float32)).astype(ml_dtypes.bfloat16)
    return high, low


def left_table(cells, images):
    cos, sin = angles(cells, images)
    high, low = halves(np.concatenate((cos.T, sin.T)))
    return np.concatenate((high, low, high), axis=1)


def tables():
    every = np.arange(M)
    a, pair, side, low = np.meshgrid(np.arange(3), np.arange(8), np.arange(2), np.arange(4), indexing="ij")
    order = (12 * (2 * pair + side) + 4 * a + low).reshape(-1)
    l, d = np.meshgrid(np.arange(8), np.arange(48), indexing="ij")
    third = left_table((d * 8 + l).reshape(-1), order)
    q, g, j = np.meshgrid(np.arange(3), np.arange(COLS), np.arange(8), indexing="ij")
    second = left_table((g * 24 + q * 8 + j).reshape(-1), every)
    turn, lane = np.meshgrid(np.arange(ROUNDS), np.arange(128), indexing="ij")
    source = (lane >> 6) * 4 + (lane & 3)
    cells = source * 48 + (2 * turn + ((lane >> 2) & 1)) * 8 + ((lane >> 3) & 7)
    firsts = []
    for part in angles(cells.reshape(-1), every):
        high, low = halves(part)
        firsts.append(np.concatenate((high, low, high), axis=0))
    return third, second, firsts[0], firsts[1]


def split(value):
    high = value.astype(BF16)
    return high, (value - high.astype(F32)).astype(BF16)


def exchange_bit(value, axis_low, lane_bit):
    count, rows, lanes = value.shape
    shift = 1 << lane_bit
    pairs = value.reshape(count // (2 * axis_low), 2, axis_low * rows, lanes)
    first = pairs[:, 0].reshape(-1, lanes)
    second = pairs[:, 1].reshape(-1, lanes)
    lane = lax.broadcasted_iota(jnp.int32, first.shape, 1)
    upper = (lane & shift) != 0
    new_first = jnp.where(upper, pltpu.roll(second, shift, 1), first)
    new_second = jnp.where(upper, second, pltpu.roll(first, lanes - shift, 1))
    shape = (count // (2 * axis_low), axis_low * rows, lanes)
    out = jnp.stack((new_first.reshape(shape), new_second.reshape(shape)), axis=1)
    return out.reshape(value.shape)


def combine(product):
    rows = product.shape[0] // 2
    lane = lax.broadcasted_iota(jnp.int32, (rows, 128), 1)
    turned = pltpu.roll(product[rows:], 64, 1)
    return product[:rows] + jnp.where(lane < 64, -turned, turned)


NT = (((1,), (1,)), ((), ()))


def whole_kernel(
    owners_in,
    tile_ids_in,
    samples_in,
    kernel_in,
    offsets_in,
    third_in,
    second_in,
    first_cos_in,
    first_sin_in,
    out,
    owners,
    tile_ids,
    samples,
    kernel,
    offsets,
    third,
    second,
    first_cos,
    first_sin,
    pieces,
    ids,
    source_of,
    slots,
    outbox,
    inbox,
    marks,
    arrived,
    cells,
    out_z,
    in_y,
    rows_y,
    out_y,
    in_x,
    rows_x,
    load_sem,
    slot_sem,
    p_send,
    p_recv,
    z_send,
    z_recv,
    y_send,
    y_recv,
    own_sem,
):
    gx, gy = lax.axis_index("gx"), lax.axis_index("gy")
    me = gx * COLS + gy

    loads = [
        pltpu.make_async_copy(source, target, load_sem.at[i])
        for i, (source, target) in enumerate(
            (
                (owners_in, owners),
                (tile_ids_in, tile_ids),
                (offsets_in, offsets),
                (samples_in, samples),
                (kernel_in, kernel),
                (third_in, third),
                (second_in, second),
                (first_cos_in, first_cos),
                (first_sin_in, first_sin),
            )
        )
    ]
    for load in loads:
        load.start()
    barrier = pltpu.get_barrier_semaphore()

    def greet(k):
        peer = lax.rem(me + k, DEVICES)
        pl.semaphore_signal(
            barrier, inc=1, device_id=(peer // COLS, lax.rem(peer, COLS)), device_id_type=MESH
        )

    loads[0].wait()
    loads[1].wait()
    lane = lax.broadcasted_iota(jnp.int32, (128, 128), 1)
    block = lax.broadcasted_iota(jnp.int32, (128, 128), 0)
    named = jnp.transpose(jnp.broadcast_to(owners[...], (128, 128))) == lane
    tiles = jnp.transpose(jnp.broadcast_to(tile_ids[...], (128, 128)))
    first = jnp.min(jnp.where(named, block, BLOCKS), axis=0, keepdims=True)
    last = jnp.max(jnp.where(named, block, -1), axis=0, keepdims=True)
    last = jnp.where(last > first, last, BLOCKS)
    source_of[pl.ds(0, 1), :] = first
    source_of[pl.ds(1, 1), :] = last
    place_slots = pltpu.make_async_copy(source_of, slots, slot_sem)
    place_slots.start()
    found = []
    for chosen in (first, last):
        tile = jnp.sum(jnp.where(named & (block == chosen), tiles, 0), axis=0, keepdims=True)
        found.append(jnp.where(chosen < BLOCKS, tile, TILES).astype(F32))
    low_lane = lax.broadcasted_iota(jnp.int32, (1, 128), 1) < 64
    ids[pl.ds(0, 1), :] = jnp.where(low_lane, found[0], pltpu.roll(found[1], 64, 1))
    ids[pl.ds(1, 1), :] = jnp.where(low_lane, pltpu.roll(found[0], 64, 1), found[1])

    for load in loads[2:5]:
        load.wait()
    pieces[BLOCKS] = jnp.zeros((8, 128), F32)
    cell = lax.broadcasted_iota(jnp.int32, (8, 128), 0)

    @pl.loop(0, BLOCKS // 8)
    def _(step):
        starts = [offsets[dim, pl.ds(pl.multiple_of(step * 8, 8), 8), :] for dim in range(3)]
        for u in range(8):
            n = step * 8 + u

            @pl.when(n > 0)
            def _():
                greet(n)

            placed = []
            for dim in range(3):
                away = cell - starts[dim][u : u + 1]
                total = jnp.zeros((8, 128), F32)
                for k in range(4):
                    total = jnp.where(away == k, kernel[n, dim, pl.ds(k, 1), :], total)
                placed.append(total)
            real = samples[n, pl.ds(0, 1), :] * placed[0]
            imag = samples[n, pl.ds(1, 1), :] * placed[0]
            plane = jnp.concatenate((real, imag), axis=0)
            weight = (plane[:, None, :] * placed[1][None, :, :]).reshape(128, 128)
            high, low = split(weight)
            depth_high, depth_low = split(placed[2])
            left = jnp.concatenate(
                (
                    jnp.concatenate((depth_high, depth_high), axis=1),
                    jnp.concatenate((depth_low, jnp.zeros_like(depth_low)), axis=1),
                ),
                axis=0,
            )
            right = jnp.concatenate((high, low), axis=1)
            both = lax.dot_general(left, right, NT, preferred_element_type=F32)
            pieces[n] = both[:8] + both[8:]

    place_slots.wait()
    pl.semaphore_wait(barrier, DEVICES - 1)

    def send_piece(peer, lands):
        return pltpu.make_async_remote_copy(
            src_ref=outbox.at[peer],
            dst_ref=inbox.at[lands],
            send_sem=p_send.at[peer],
            recv_sem=p_recv.at[lands],
            device_id=(peer // COLS, lax.rem(peer, COLS)),
            device_id_type=MESH,
        )

    def fill(box, place, peer):
        box[place, pl.ds(0, 8), :] = pieces[slots[0, peer]]
        box[place, pl.ds(8, 8), :] = pieces[slots[1, peer]]
        box[place, pl.ds(16, 1), :] = ids[pl.ds(peer // 64, 1), :]

    @pl.loop(1, DEVICES)
    def _(k):
        peer = lax.rem(me + k, DEVICES)
        fill(outbox, peer, peer)
        send_piece(peer, me).start()

    fill(inbox, me, me)

    @pl.loop(0, ROWS)
    def _(t):
        group = lax.rem(gx + ROWS - t, ROWS)

        @pl.loop(0, COLS)
        def _(u):
            peer = group * COLS + u

            @pl.when(peer != me)
            def _():
                send_piece(peer, peer).wait_recv()

        base = pl.multiple_of(group * COLS, COLS)
        for slot in range(2):
            for l in range(8):
                high, low = split(inbox[pl.ds(base, COLS), slot * 8 + l, :])
                arrived[pl.ds(pl.multiple_of(base + slot * 128, 16), COLS), pl.ds(l * 128, 128)] = high
                arrived[pl.ds(pl.multiple_of(base + 256 + slot * 128, 16), COLS), pl.ds(l * 128, 128)] = low

    marks[...] = jnp.transpose(inbox[:, 16, :])
    mine = lax.rem(me, 64)
    tile_rows = [marks[pl.ds(mine + 64 * slot, 1), :] for slot in range(2)]
    for load in loads[5:]:
        load.wait()

    def send_z(turn, peer, lands):
        return pltpu.make_async_remote_copy(
            src_ref=out_z.at[turn, peer // 2, lax.rem(peer, 2)],
            dst_ref=in_y.at[turn, lands],
            send_sem=z_send.at[turn, peer],
            recv_sem=z_recv.at[turn, lands],
            device_id=(gx, peer),
            device_id_type=MESH,
        )

    def own_z(turn):
        return pltpu.make_async_copy(
            out_z.at[turn, gy // 2, lax.rem(gy, 2)], in_y.at[turn, gy], own_sem.at[0, turn]
        )

    def send_y(turn, peer, lands):
        return pltpu.make_async_remote_copy(
            src_ref=out_y.at[turn, peer],
            dst_ref=in_x.at[turn, lands],
            send_sem=y_send.at[turn, peer],
            recv_sem=y_recv.at[turn, lands],
            device_id=(peer, gy),
            device_id_type=MESH,
        )

    def own_y(turn):
        return pltpu.make_async_copy(out_y.at[turn, gx], in_x.at[turn, gx], own_sem.at[1, turn])

    row = lax.broadcasted_iota(jnp.int32, (24, 8, 128), 1)
    share = TILES // ROUNDS
    tile_of = lax.broadcasted_iota(jnp.int32, (share, 128), 0)
    for turn in range(ROUNDS):
        hits = [
            jnp.where((tile_of + turn * share).astype(F32) == tile_row, 1.0, 0.0).astype(BF16)
            for tile_row in tile_rows
        ]
        hits = jnp.concatenate(hits + hits, axis=1)
        for pair in range(4):
            added = jnp.dot(hits, arrived[:, pl.ds(pair * 256, 256)], preferred_element_type=F32)
            for half, value in enumerate(split(added)):
                for l in range(2):
                    for column in range(6):
                        cells[half, column, pl.ds((2 * pair + l) * 48, 48), :] = value[
                            column * 48 : column * 48 + 48, l * 128 : l * 128 + 128
                        ]
        for q in range(3):
            high, low = [
                jnp.concatenate((cells[half, q], cells[half, 3 + q]), axis=1) for half in range(2)
            ]
            product = jnp.dot(
                third[...], jnp.concatenate((high, high, low), axis=0), preferred_element_type=F32
            )
            near = combine(product[:, :128]).reshape(24, 8, 128)
            far = combine(product[:, 128:]).reshape(24, 8, 128)
            even = jnp.where(row < 4, near, pltpu.roll(far, 4, 1))
            odd = jnp.where(row < 4, pltpu.roll(near, 4, 1), far)
            for a in range(3):
                out_z[turn, :, 0, q * 3 + a] = even[a * 8 : a * 8 + 8]
                out_z[turn, :, 1, q * 3 + a] = odd[a * 8 : a * 8 + 8]
        own_z(turn).start()

        @pl.loop(1, COLS)
        def _(k):
            send_z(turn, lax.rem(gy + k, COLS), gy).start()

    for turn in range(ROUNDS):
        own_z(turn).wait()

        @pl.loop(1, COLS)
        def _(k):
            peer = lax.rem(gy + COLS - k, COLS)
            send_z(turn, peer, peer).wait_recv()

        for a in range(3):
            for q in range(3):
                value = in_y[turn, :, q * 3 + a]
                for bit in range(4):
                    value = exchange_bit(value, 1 << bit, 3 + bit)
                high, low = split(value.reshape(128, 128))
                rows_y[pl.ds(a * 128, 128), pl.ds(q * 128, 128)] = high
                rows_y[pl.ds(a * 128, 128), pl.ds(N + q * 128, 128)] = high
                rows_y[pl.ds(a * 128, 128), pl.ds(2 * N + q * 128, 128)] = low
        product = lax.dot_general(second[...], rows_y[...], NT, preferred_element_type=F32)
        for a in range(3):
            part = combine(product[:, a * 128 : a * 128 + 128])
            out_y[turn, :, a] = part.reshape(ROWS, 24, 128)
        own_y(turn).start()

        @pl.loop(1, ROWS)
        def _(k):
            send_y(turn, lax.rem(gx + k, ROWS), gx).start()

    for turn in range(ROUNDS):
        own_y(turn).wait()

        @pl.loop(1, ROWS)
        def _(k):
            peer = lax.rem(gx + ROWS - k, ROWS)
            send_y(turn, peer, peer).wait_recv()

        value = in_x[turn].reshape(ROWS, 72, 128)
        value = exchange_bit(value, 4, 6)
        value = exchange_bit(value, 2, 1)
        value = exchange_bit(value, 1, 0)
        high, low = split(value.reshape(576, 128))
        rows_x[:, pl.ds(turn * 128, 128)] = high
        rows_x[:, pl.ds(N + turn * 128, 128)] = high
        rows_x[:, pl.ds(2 * N + turn * 128, 128)] = low

    cos = jnp.dot(rows_x[...], first_cos[...], preferred_element_type=F32)
    sin = jnp.dot(rows_x[...], first_sin[...], preferred_element_type=F32)
    real = (cos[:288] - sin[288:]).reshape(4, 3, 24, M)
    imag = (sin[:288] + cos[288:]).reshape(4, 3, 24, M)
    for b in range(4):
        for a in range(3):
            out[0, a * 4 + b] = real[b, a]
            out[1, a * 4 + b] = imag[b, a]

    for turn in range(ROUNDS):

        @pl.loop(1, COLS)
        def _(k):
            send_z(turn, lax.rem(gy + k, COLS), gy).wait_send()

        @pl.loop(1, ROWS)
        def _(k):
            send_y(turn, lax.rem(gx + k, ROWS), gx).wait_send()


    @pl.loop(1, DEVICES)
    def _(k):
        send_piece(lax.rem(me + k, DEVICES), me).wait_send()


def whole(owners, tile_ids, samples, kernel, offsets, third, second, first_cos, first_sin):
    operands = (owners, tile_ids, samples, kernel, offsets, third, second, first_cos, first_sin)
    held = [pltpu.VMEM(x.shape, x.dtype) for x in operands]
    return pl.pallas_call(
        whole_kernel,
        out_shape=jax.ShapeDtypeStruct((2, 12, 24, M), F32),
        in_specs=[pl.BlockSpec(memory_space=pl.ANY)] * len(operands),
        out_specs=pl.BlockSpec(memory_space=pltpu.VMEM),
        scratch_shapes=held
        + [
            pltpu.VMEM((BLOCKS + 1, 8, 128), F32),
            pltpu.VMEM((8, 128), F32),
            pltpu.VMEM((8, 128), jnp.int32),
            pltpu.SMEM((8, 128), jnp.int32),
            pltpu.VMEM((DEVICES, SLOT_ROWS, 128), F32),
            pltpu.VMEM((DEVICES, SLOT_ROWS, 128), F32),
            pltpu.VMEM((128, 128), F32),
            pltpu.VMEM((512, 1024), BF16),
            pltpu.VMEM((2, 6, N, 128), BF16),
            pltpu.VMEM((ROUNDS, 8, 2, 9, 8, 128), F32),
            pltpu.VMEM((ROUNDS, COLS, 9, 8, 128), F32),
            pltpu.VMEM((N, 3 * N), BF16),
            pltpu.VMEM((ROUNDS, ROWS, 3, 24, 128), F32),
            pltpu.VMEM((ROUNDS, ROWS, 3, 24, 128), F32),
            pltpu.VMEM((576, 3 * N), BF16),
            pltpu.SemaphoreType.DMA((len(operands),)),
            pltpu.SemaphoreType.DMA,
            pltpu.SemaphoreType.DMA((DEVICES,)),
            pltpu.SemaphoreType.DMA((DEVICES,)),
            pltpu.SemaphoreType.DMA((ROUNDS, COLS)),
            pltpu.SemaphoreType.DMA((ROUNDS, COLS)),
            pltpu.SemaphoreType.DMA((ROUNDS, ROWS)),
            pltpu.SemaphoreType.DMA((ROUNDS, ROWS)),
            pltpu.SemaphoreType.DMA((2, ROUNDS)),
        ],
        compiler_params=pltpu.CompilerParams(
            collective_id=0, has_side_effects=True, vmem_limit_bytes=48 << 20
        ),
        name="whole",
    )(*operands)


def solution(mesh):
    third, second, first_cos, first_sin = tables()

    def on_device(samples, kernel, offsets, owners, tile_ids, deapod_first, deapod_second, deapod_third):
        along_x = whole(
            owners.reshape(1, BLOCKS),
            tile_ids.reshape(1, BLOCKS),
            samples,
            kernel,
            offsets.transpose(1, 0, 2),
            third,
            second,
            first_cos,
            first_sin,
        )
        return (
            along_x
            * deapod_third[None, :, None, None]
            * deapod_second[None, None, :, None]
            * deapod_first[None, None, None, :]
        )

    in_specs = (
        P(("gx", "gy"), None, None),
        P(("gx", "gy"), None, None, None),
        P(("gx", "gy"), None, None),
        P(("gx", "gy"), None),
        P(("gx", "gy")),
        P(),
        P("gx"),
        P("gy"),
    )
    return jax.shard_map(
        on_device, mesh=mesh, in_specs=in_specs, out_specs=P(None, "gy", "gx", None), check_vma=False
    )
```

```python
import math

import jax
import jax.numpy as jnp
import ml_dtypes
import numpy as np
from jax import lax
from jax.experimental import pallas as pl
from jax.experimental.pallas import tpu as pltpu
from jax.sharding import PartitionSpec as P

N = 384
M = 192
DEVICES = 128
ROWS, COLS = 8, 16
BLOCKS = 128
TILES = 864
SLOT_ROWS = 17
ROUNDS = 3
MESH = pl.DeviceIdType.MESH
F32 = jnp.float32
BF16 = jnp.bfloat16


def angles(cells, images):
    steps = np.mod((cells[:, None] - N // 2) * (images[None, :] - M // 2), N)
    phases = steps.astype(np.float64) * (2.0 * math.pi / N)
    return np.cos(phases) / math.sqrt(N), np.sin(phases) / math.sqrt(N)


def halves(table):
    table = table.astype(np.float32)
    high = table.astype(ml_dtypes.bfloat16)
    low = (table - high.astype(np.float32)).astype(ml_dtypes.bfloat16)
    return high, low


def left_table(cells, images):
    cos, sin = angles(cells, images)
    high, low = halves(np.concatenate((cos.T, sin.T)))
    return np.concatenate((high, low, high), axis=1)


def tables():
    every = np.arange(M)
    a, pair, side, low = np.meshgrid(np.arange(3), np.arange(8), np.arange(2), np.arange(4), indexing="ij")
    order = (12 * (2 * pair + side) + 4 * a + low).reshape(-1)
    l, d = np.meshgrid(np.arange(8), np.arange(48), indexing="ij")
    third = left_table((d * 8 + l).reshape(-1), order)
    q, g, j = np.meshgrid(np.arange(3), np.arange(COLS), np.arange(8), indexing="ij")
    second = left_table((g * 24 + q * 8 + j).reshape(-1), every)
    turn, lane = np.meshgrid(np.arange(ROUNDS), np.arange(128), indexing="ij")
    source = (lane >> 6) * 4 + (lane & 3)
    cells = source * 48 + (2 * turn + ((lane >> 2) & 1)) * 8 + ((lane >> 3) & 7)
    firsts = []
    for part in angles(cells.reshape(-1), every):
        high, low = halves(part)
        firsts.append(np.concatenate((high, low, high), axis=0))
    return third, second, firsts[0], firsts[1]


def split(value):
    high = value.astype(BF16)
    return high, (value - high.astype(F32)).astype(BF16)


def exchange_bit(value, axis_low, lane_bit):
    count, rows, lanes = value.shape
    shift = 1 << lane_bit
    pairs = value.reshape(count // (2 * axis_low), 2, axis_low * rows, lanes)
    first = pairs[:, 0].reshape(-1, lanes)
    second = pairs[:, 1].reshape(-1, lanes)
    lane = lax.broadcasted_iota(jnp.int32, first.shape, 1)
    upper = (lane & shift) != 0
    new_first = jnp.where(upper, pltpu.roll(second, shift, 1), first)
    new_second = jnp.where(upper, second, pltpu.roll(first, lanes - shift, 1))
    shape = (count // (2 * axis_low), axis_low * rows, lanes)
    out = jnp.stack((new_first.reshape(shape), new_second.reshape(shape)), axis=1)
    return out.reshape(value.shape)


def combine(product):
    rows = product.shape[0] // 2
    lane = lax.broadcasted_iota(jnp.int32, (rows, 128), 1)
    turned = pltpu.roll(product[rows:], 64, 1)
    return product[:rows] + jnp.where(lane < 64, -turned, turned)


NT = (((1,), (1,)), ((), ()))


def whole_kernel(
    owners_in,
    tile_ids_in,
    samples_in,
    kernel_in,
    offsets_in,
    third_in,
    second_in,
    first_cos_in,
    first_sin_in,
    out,
    owners,
    tile_ids,
    samples,
    kernel,
    offsets,
    third,
    second,
    first_cos,
    first_sin,
    pieces,
    ids,
    source_of,
    slots,
    outbox,
    inbox,
    marks,
    arrived,
    cells,
    out_z,
    in_y,
    rows_y,
    out_y,
    in_x,
    rows_x,
    load_sem,
    slot_sem,
    p_send,
    p_recv,
    z_send,
    z_recv,
    y_send,
    y_recv,
    own_sem,
):
    gx, gy = lax.axis_index("gx"), lax.axis_index("gy")
    me = gx * COLS + gy

    loads = [
        pltpu.make_async_copy(source, target, load_sem.at[i])
        for i, (source, target) in enumerate(
            (
                (owners_in, owners),
                (tile_ids_in, tile_ids),
                (offsets_in, offsets),
                (samples_in, samples),
                (kernel_in, kernel),
                (third_in, third),
                (second_in, second),
                (first_cos_in, first_cos),
                (first_sin_in, first_sin),
            )
        )
    ]
    for load in loads:
        load.start()
    barrier = pltpu.get_barrier_semaphore()

    @pl.loop(1, DEVICES)
    def _(k):
        peer = lax.rem(me + k, DEVICES)
        pl.semaphore_signal(
            barrier, inc=1, device_id=(peer // COLS, lax.rem(peer, COLS)), device_id_type=MESH
        )

    loads[0].wait()
    loads[1].wait()
    lane = lax.broadcasted_iota(jnp.int32, (128, 128), 1)
    block = lax.broadcasted_iota(jnp.int32, (128, 128), 0)
    named = jnp.transpose(jnp.broadcast_to(owners[...], (128, 128))) == lane
    tiles = jnp.transpose(jnp.broadcast_to(tile_ids[...], (128, 128)))
    first = jnp.min(jnp.where(named, block, BLOCKS), axis=0, keepdims=True)
    last = jnp.max(jnp.where(named, block, -1), axis=0, keepdims=True)
    last = jnp.where(last > first, last, BLOCKS)
    source_of[pl.ds(0, 1), :] = first
    source_of[pl.ds(1, 1), :] = last
    place_slots = pltpu.make_async_copy(source_of, slots, slot_sem)
    place_slots.start()
    found = []
    for chosen in (first, last):
        tile = jnp.sum(jnp.where(named & (block == chosen), tiles, 0), axis=0, keepdims=True)
        found.append(jnp.where(chosen < BLOCKS, tile, TILES).astype(F32))
    low_lane = lax.broadcasted_iota(jnp.int32, (1, 128), 1) < 64
    ids[pl.ds(0, 1), :] = jnp.where(low_lane, found[0], pltpu.roll(found[1], 64, 1))
    ids[pl.ds(1, 1), :] = jnp.where(low_lane, pltpu.roll(found[0], 64, 1), found[1])

    for load in loads[2:5]:
        load.wait()
    pieces[BLOCKS] = jnp.zeros((8, 128), F32)
    cell = lax.broadcasted_iota(jnp.int32, (8, 128), 0)

    @pl.loop(0, BLOCKS // 8)
    def _(step):
        starts = [offsets[dim, pl.ds(pl.multiple_of(step * 8, 8), 8), :] for dim in range(3)]
        for u in range(8):
            n = step * 8 + u

            placed = []
            for dim in range(3):
                away = cell - starts[dim][u : u + 1]
                total = jnp.zeros((8, 128), F32)
                for k in range(4):
                    total = jnp.where(away == k, kernel[n, dim, pl.ds(k, 1), :], total)
                placed.append(total)
            real = samples[n, pl.ds(0, 1), :] * placed[0]
            imag = samples[n, pl.ds(1, 1), :] * placed[0]
            plane = jnp.concatenate((real, imag), axis=0)
            weight = (plane[:, None, :] * placed[1][None, :, :]).reshape(128, 128)
            high, low = split(weight)
            depth_high, depth_low = split(placed[2])
            left = jnp.concatenate(
                (
                    jnp.concatenate((depth_high, depth_high), axis=1),
                    jnp.concatenate((depth_low, jnp.zeros_like(depth_low)), axis=1),
                ),
                axis=0,
            )
            right = jnp.concatenate((high, low), axis=1)
            both = lax.dot_general(left, right, NT, preferred_element_type=F32)
            pieces[n] = both[:8] + both[8:]

    place_slots.wait()
    pl.semaphore_wait(barrier, DEVICES - 1)

    def send_piece(peer, lands):
        return pltpu.make_async_remote_copy(
            src_ref=outbox.at[peer],
            dst_ref=inbox.at[lands],
            send_sem=p_send.at[peer],
            recv_sem=p_recv.at[lands],
            device_id=(peer // COLS, lax.rem(peer, COLS)),
            device_id_type=MESH,
        )

    def fill(box, place, peer):
        box[place, pl.ds(0, 8), :] = pieces[slots[0, peer]]
        box[place, pl.ds(8, 8), :] = pieces[slots[1, peer]]
        box[place, pl.ds(16, 1), :] = ids[pl.ds(peer // 64, 1), :]

    @pl.loop(1, DEVICES)
    def _(k):
        peer = lax.rem(me + k, DEVICES)
        fill(outbox, peer, peer)
        send_piece(peer, me).start()

    fill(inbox, me, me)

    @pl.loop(0, ROWS)
    def _(t):
        group = lax.rem(gx + ROWS - t, ROWS)

        @pl.loop(0, COLS)
        def _(u):
            peer = group * COLS + u

            @pl.when(peer != me)
            def _():
                send_piece(peer, peer).wait_recv()

        base = pl.multiple_of(group * COLS, COLS)
        for slot in range(2):
            for l in range(8):
                high, low = split(inbox[pl.ds(base, COLS), slot * 8 + l, :])
                arrived[pl.ds(pl.multiple_of(base + slot * 128, 16), COLS), pl.ds(l * 128, 128)] = high
                arrived[pl.ds(pl.multiple_of(base + 256 + slot * 128, 16), COLS), pl.ds(l * 128, 128)] = low

    marks[...] = jnp.transpose(inbox[:, 16, :])
    mine = lax.rem(me, 64)
    tile_rows = [marks[pl.ds(mine + 64 * slot, 1), :] for slot in range(2)]
    for load in loads[5:]:
        load.wait()

    def send_z(turn, peer, lands):
        return pltpu.make_async_remote_copy(
            src_ref=out_z.at[turn, peer // 2, lax.rem(peer, 2)],
            dst_ref=in_y.at[turn, lands],
            send_sem=z_send.at[turn, peer],
            recv_sem=z_recv.at[turn, lands],
            device_id=(gx, peer),
            device_id_type=MESH,
        )

    def own_z(turn):
        return pltpu.make_async_copy(
            out_z.at[turn, gy // 2, lax.rem(gy, 2)], in_y.at[turn, gy], own_sem.at[0, turn]
        )

    def send_y(turn, peer, lands):
        return pltpu.make_async_remote_copy(
            src_ref=out_y.at[turn, peer],
            dst_ref=in_x.at[turn, lands],
            send_sem=y_send.at[turn, peer],
            recv_sem=y_recv.at[turn, lands],
            device_id=(peer, gy),
            device_id_type=MESH,
        )

    def own_y(turn):
        return pltpu.make_async_copy(out_y.at[turn, gx], in_x.at[turn, gx], own_sem.at[1, turn])

    row = lax.broadcasted_iota(jnp.int32, (24, 8, 128), 1)
    share = TILES // ROUNDS
    tile_of = lax.broadcasted_iota(jnp.int32, (share, 128), 0)
    for turn in range(ROUNDS):
        hits = [
            jnp.where((tile_of + turn * share).astype(F32) == tile_row, 1.0, 0.0).astype(BF16)
            for tile_row in tile_rows
        ]
        hits = jnp.concatenate(hits + hits, axis=1)
        for pair in range(4):
            added = jnp.dot(hits, arrived[:, pl.ds(pair * 256, 256)], preferred_element_type=F32)
            for half, value in enumerate(split(added)):
                for l in range(2):
                    for column in range(6):
                        cells[half, column, pl.ds((2 * pair + l) * 48, 48), :] = value[
                            column * 48 : column * 48 + 48, l * 128 : l * 128 + 128
                        ]
        for q in range(3):
            high, low = [
                jnp.concatenate((cells[half, q], cells[half, 3 + q]), axis=1) for half in range(2)
            ]
            product = jnp.dot(
                third[...], jnp.concatenate((high, high, low), axis=0), preferred_element_type=F32
            )
            near = combine(product[:, :128]).reshape(24, 8, 128)
            far = combine(product[:, 128:]).reshape(24, 8, 128)
            even = jnp.where(row < 4, near, pltpu.roll(far, 4, 1))
            odd = jnp.where(row < 4, pltpu.roll(near, 4, 1), far)
            for a in range(3):
                out_z[turn, :, 0, q * 3 + a] = even[a * 8 : a * 8 + 8]
                out_z[turn, :, 1, q * 3 + a] = odd[a * 8 : a * 8 + 8]
        own_z(turn).start()

        @pl.loop(1, COLS)
        def _(k):
            send_z(turn, lax.rem(gy + k, COLS), gy).start()

    for turn in range(ROUNDS):
        own_z(turn).wait()

        @pl.loop(1, COLS)
        def _(k):
            peer = lax.rem(gy + COLS - k, COLS)
            send_z(turn, peer, peer).wait_recv()

        for a in range(3):
            for q in range(3):
                value = in_y[turn, :, q * 3 + a]
                for bit in range(4):
                    value = exchange_bit(value, 1 << bit, 3 + bit)
                high, low = split(value.reshape(128, 128))
                rows_y[pl.ds(a * 128, 128), pl.ds(q * 128, 128)] = high
                rows_y[pl.ds(a * 128, 128), pl.ds(N + q * 128, 128)] = high
                rows_y[pl.ds(a * 128, 128), pl.ds(2 * N + q * 128, 128)] = low
        product = lax.dot_general(second[...], rows_y[...], NT, preferred_element_type=F32)
        for a in range(3):
            part = combine(product[:, a * 128 : a * 128 + 128])
            out_y[turn, :, a] = part.reshape(ROWS, 24, 128)
        own_y(turn).start()

        @pl.loop(1, ROWS)
        def _(k):
            send_y(turn, lax.rem(gx + k, ROWS), gx).start()

    for turn in range(ROUNDS):
        own_y(turn).wait()

        @pl.loop(1, ROWS)
        def _(k):
            peer = lax.rem(gx + ROWS - k, ROWS)
            send_y(turn, peer, peer).wait_recv()

        value = in_x[turn].reshape(ROWS, 72, 128)
        value = exchange_bit(value, 4, 6)
        value = exchange_bit(value, 2, 1)
        value = exchange_bit(value, 1, 0)
        high, low = split(value.reshape(576, 128))
        rows_x[:, pl.ds(turn * 128, 128)] = high
        rows_x[:, pl.ds(N + turn * 128, 128)] = high
        rows_x[:, pl.ds(2 * N + turn * 128, 128)] = low

    cos = jnp.dot(rows_x[...], first_cos[...], preferred_element_type=F32)
    sin = jnp.dot(rows_x[...], first_sin[...], preferred_element_type=F32)
    real = (cos[:288] - sin[288:]).reshape(4, 3, 24, M)
    imag = (sin[:288] + cos[288:]).reshape(4, 3, 24, M)
    for b in range(4):
        for a in range(3):
            out[0, a * 4 + b] = real[b, a]
            out[1, a * 4 + b] = imag[b, a]

    for turn in range(ROUNDS):

        @pl.loop(1, COLS)
        def _(k):
            send_z(turn, lax.rem(gy + k, COLS), gy).wait_send()

        @pl.loop(1, ROWS)
        def _(k):
            send_y(turn, lax.rem(gx + k, ROWS), gx).wait_send()


    @pl.loop(1, DEVICES)
    def _(k):
        send_piece(lax.rem(me + k, DEVICES), me).wait_send()


def whole(owners, tile_ids, samples, kernel, offsets, third, second, first_cos, first_sin):
    operands = (owners, tile_ids, samples, kernel, offsets, third, second, first_cos, first_sin)
    held = [pltpu.VMEM(x.shape, x.dtype) for x in operands]
    return pl.pallas_call(
        whole_kernel,
        out_shape=jax.ShapeDtypeStruct((2, 12, 24, M), F32),
        in_specs=[pl.BlockSpec(memory_space=pl.ANY)] * len(operands),
        out_specs=pl.BlockSpec(memory_space=pltpu.VMEM),
        scratch_shapes=held
        + [
            pltpu.VMEM((BLOCKS + 1, 8, 128), F32),
            pltpu.VMEM((8, 128), F32),
            pltpu.VMEM((8, 128), jnp.int32),
            pltpu.SMEM((8, 128), jnp.int32),
            pltpu.VMEM((DEVICES, SLOT_ROWS, 128), F32),
            pltpu.VMEM((DEVICES, SLOT_ROWS, 128), F32),
            pltpu.VMEM((128, 128), F32),
            pltpu.VMEM((512, 1024), BF16),
            pltpu.VMEM((2, 6, N, 128), BF16),
            pltpu.VMEM((ROUNDS, 8, 2, 9, 8, 128), F32),
            pltpu.VMEM((ROUNDS, COLS, 9, 8, 128), F32),
            pltpu.VMEM((N, 3 * N), BF16),
            pltpu.VMEM((ROUNDS, ROWS, 3, 24, 128), F32),
            pltpu.VMEM((ROUNDS, ROWS, 3, 24, 128), F32),
            pltpu.VMEM((576, 3 * N), BF16),
            pltpu.SemaphoreType.DMA((len(operands),)),
            pltpu.SemaphoreType.DMA,
            pltpu.SemaphoreType.DMA((DEVICES,)),
            pltpu.SemaphoreType.DMA((DEVICES,)),
            pltpu.SemaphoreType.DMA((ROUNDS, COLS)),
            pltpu.SemaphoreType.DMA((ROUNDS, COLS)),
            pltpu.SemaphoreType.DMA((ROUNDS, ROWS)),
            pltpu.SemaphoreType.DMA((ROUNDS, ROWS)),
            pltpu.SemaphoreType.DMA((2, ROUNDS)),
        ],
        compiler_params=pltpu.CompilerParams(
            collective_id=0, has_side_effects=True, vmem_limit_bytes=62 << 20
        ),
        name="whole",
    )(*operands)


def solution(mesh):
    third, second, first_cos, first_sin = tables()

    def on_device(samples, kernel, offsets, owners, tile_ids, deapod_first, deapod_second, deapod_third):
        along_x = whole(
            owners.reshape(1, BLOCKS),
            tile_ids.reshape(1, BLOCKS),
            samples,
            kernel,
            offsets.transpose(1, 0, 2),
            third,
            second,
            first_cos,
            first_sin,
        )
        return (
            along_x
            * deapod_third[None, :, None, None]
            * deapod_second[None, None, :, None]
            * deapod_first[None, None, None, :]
        )

    in_specs = (
        P(("gx", "gy"), None, None),
        P(("gx", "gy"), None, None, None),
        P(("gx", "gy"), None, None),
        P(("gx", "gy"), None),
        P(("gx", "gy")),
        P(),
        P("gx"),
        P("gy"),
    )
    return jax.shard_map(
        on_device, mesh=mesh, in_specs=in_specs, out_specs=P(None, "gy", "gx", None), check_vma=False
    )
```

```python
import math

import jax
import jax.numpy as jnp
import ml_dtypes
import numpy as np
from jax import lax
from jax.experimental import pallas as pl
from jax.experimental.pallas import tpu as pltpu
from jax.sharding import PartitionSpec as P

N = 384
M = 192
DEVICES = 128
ROWS, COLS = 8, 16
BLOCKS = 128
TILES = 864
SLOT_ROWS = 17
ROUNDS = 3
MESH = pl.DeviceIdType.MESH
F32 = jnp.float32
BF16 = jnp.bfloat16


def angles(cells, images):
    steps = np.mod((cells[:, None] - N // 2) * (images[None, :] - M // 2), N)
    phases = steps.astype(np.float64) * (2.0 * math.pi / N)
    return np.cos(phases) / math.sqrt(N), np.sin(phases) / math.sqrt(N)


def halves(table):
    table = table.astype(np.float32)
    high = table.astype(ml_dtypes.bfloat16)
    low = (table - high.astype(np.float32)).astype(ml_dtypes.bfloat16)
    return high, low


def left_table(cells, images):
    cos, sin = angles(cells, images)
    return np.concatenate(halves(np.concatenate((cos.T, sin.T))), axis=1)


def tables():
    every = np.arange(M)
    a, pair, side, low = np.meshgrid(np.arange(3), np.arange(8), np.arange(2), np.arange(4), indexing="ij")
    order = (12 * (2 * pair + side) + 4 * a + low).reshape(-1)
    l, d = np.meshgrid(np.arange(8), np.arange(48), indexing="ij")
    third = left_table((d * 8 + l).reshape(-1), order)
    q, g, j = np.meshgrid(np.arange(3), np.arange(COLS), np.arange(8), indexing="ij")
    second = left_table((g * 24 + q * 8 + j).reshape(-1), every)
    turn, lane = np.meshgrid(np.arange(ROUNDS), np.arange(128), indexing="ij")
    source = (lane >> 6) * 4 + (lane & 3)
    cells = source * 48 + (2 * turn + ((lane >> 2) & 1)) * 8 + ((lane >> 3) & 7)
    firsts = []
    for part in angles(cells.reshape(-1), every):
        high, low = halves(part.reshape(ROUNDS, 128, M))
        firsts.append(np.concatenate((high, low), axis=1))
    return third, second, firsts[0], firsts[1]


def split(value):
    high = value.astype(BF16)
    return high, (value - high.astype(F32)).astype(BF16)


def exchange_bit(value, axis_low, lane_bit):
    count, rows, lanes = value.shape
    shift = 1 << lane_bit
    pairs = value.reshape(count // (2 * axis_low), 2, axis_low * rows, lanes)
    first = pairs[:, 0].reshape(-1, lanes)
    second = pairs[:, 1].reshape(-1, lanes)
    lane = lax.broadcasted_iota(jnp.int32, first.shape, 1)
    upper = (lane & shift) != 0
    new_first = jnp.where(upper, pltpu.roll(second, shift, 1), first)
    new_second = jnp.where(upper, second, pltpu.roll(first, lanes - shift, 1))
    shape = (count // (2 * axis_low), axis_low * rows, lanes)
    out = jnp.stack((new_first.reshape(shape), new_second.reshape(shape)), axis=1)
    return out.reshape(value.shape)


def combine(product):
    rows = product.shape[0] // 2
    lane = lax.broadcasted_iota(jnp.int32, (rows, 128), 1)
    turned = pltpu.roll(product[rows:], 64, 1)
    return product[:rows] + jnp.where(lane < 64, -turned, turned)


NT = (((1,), (1,)), ((), ()))


def whole_kernel(
    owners_in,
    tile_ids_in,
    samples_in,
    kernel_in,
    offsets_in,
    third_in,
    second_in,
    first_cos_in,
    first_sin_in,
    out,
    owners,
    tile_ids,
    samples,
    kernel,
    offsets,
    third,
    second,
    first_cos,
    first_sin,
    pieces,
    ids,
    source_of,
    slots,
    outbox,
    inbox,
    marks,
    arrived,
    cells,
    out_z,
    in_y,
    rows_y,
    out_y,
    in_x,
    sum_cos,
    sum_sin,
    settled,
    load_sem,
    slot_sem,
    p_send,
    p_recv,
    z_send,
    z_recv,
    y_send,
    y_recv,
):
    gx, gy = lax.axis_index("gx"), lax.axis_index("gy")
    me = gx * COLS + gy

    loads = [
        pltpu.make_async_copy(source, target, load_sem.at[i])
        for i, (source, target) in enumerate(
            (
                (owners_in, owners),
                (tile_ids_in, tile_ids),
                (offsets_in, offsets),
                (samples_in, samples),
                (kernel_in, kernel),
                (third_in, third.at[:, pl.ds(0, 2 * N)]),
                (third_in.at[:, pl.ds(0, N)], third.at[:, pl.ds(2 * N, N)]),
                (second_in, second.at[:, pl.ds(0, 2 * N)]),
                (second_in.at[:, pl.ds(0, N)], second.at[:, pl.ds(2 * N, N)]),
                (first_cos_in, first_cos.at[:, pl.ds(0, 256)]),
                (first_cos_in.at[:, pl.ds(0, 128)], first_cos.at[:, pl.ds(256, 128)]),
                (first_sin_in, first_sin.at[:, pl.ds(0, 256)]),
                (first_sin_in.at[:, pl.ds(0, 128)], first_sin.at[:, pl.ds(256, 128)]),
            )
        )
    ]
    for load in loads[:5]:
        load.start()
    barrier = pltpu.get_barrier_semaphore()

    def greet(semaphore, x, y):
        pl.semaphore_signal(semaphore, inc=1, device_id=(x, y), device_id_type=MESH)

    @pl.loop(1, COLS)
    def _(k):
        greet(barrier, gx, lax.rem(gy + k, COLS))

    @pl.loop(1, ROWS)
    def _(k):
        greet(barrier, lax.rem(gx + k, ROWS), gy)

    for load in loads[5:]:
        load.start()

    loads[0].wait()
    loads[1].wait()
    lane = lax.broadcasted_iota(jnp.int32, (128, 128), 1)
    block = lax.broadcasted_iota(jnp.int32, (128, 128), 0)
    named = jnp.transpose(jnp.broadcast_to(owners[...], (128, 128))) == lane
    tiles = jnp.transpose(jnp.broadcast_to(tile_ids[...], (128, 128)))
    first = jnp.min(jnp.where(named, block, BLOCKS), axis=0, keepdims=True)
    last = jnp.max(jnp.where(named, block, -1), axis=0, keepdims=True)
    last = jnp.where(last > first, last, BLOCKS)
    source_of[pl.ds(0, 1), :] = first
    source_of[pl.ds(1, 1), :] = last
    place_slots = pltpu.make_async_copy(source_of, slots, slot_sem)
    place_slots.start()
    found = []
    for chosen in (first, last):
        tile = jnp.sum(jnp.where(named & (block == chosen), tiles, 0), axis=0, keepdims=True)
        found.append(jnp.where(chosen < BLOCKS, tile, TILES).astype(F32))
    low_lane = lax.broadcasted_iota(jnp.int32, (1, 128), 1) < 64
    ids[pl.ds(0, 1), :] = jnp.where(low_lane, found[0], pltpu.roll(found[1], 64, 1))
    ids[pl.ds(1, 1), :] = jnp.where(low_lane, pltpu.roll(found[0], 64, 1), found[1])

    for load in loads[2:5]:
        load.wait()
    pieces[BLOCKS] = jnp.zeros((8, 128), F32)
    cell = lax.broadcasted_iota(jnp.int32, (8, 128), 0)

    def spread(step):
        starts = [offsets[dim, pl.ds(pl.multiple_of(step * 16, 16), 16), :] for dim in range(3)]
        for u in range(16):
            n = step * 16 + u

            placed = []
            for dim in range(3):
                away = cell - starts[dim][u : u + 1]
                total = jnp.zeros((8, 128), F32)
                for k in range(4):
                    total = jnp.where(away == k, kernel[n, dim, pl.ds(k, 1), :], total)
                placed.append(total)
            real = samples[n, pl.ds(0, 1), :] * placed[0]
            imag = samples[n, pl.ds(1, 1), :] * placed[0]
            plane = jnp.concatenate((real, imag), axis=0)
            weight = (plane[:, None, :] * placed[1][None, :, :]).reshape(128, 128)
            high, low = split(weight)
            depth_high, depth_low = split(placed[2])
            left = jnp.concatenate(
                (
                    jnp.concatenate((depth_high, depth_high), axis=1),
                    jnp.concatenate((depth_low, jnp.zeros_like(depth_low)), axis=1),
                ),
                axis=0,
            )
            right = jnp.concatenate((high, low), axis=1)
            both = lax.dot_general(left, right, NT, preferred_element_type=F32)
            pieces[n] = both[:8] + both[8:]

    pl.loop(0, BLOCKS // 32)(spread)
    pl.semaphore_wait(barrier, COLS + ROWS - 2)

    @pl.loop(1, COLS)
    def _(k):
        greet(settled, gx, lax.rem(gy + k, COLS))

    pl.loop(BLOCKS // 32, BLOCKS // 16)(spread)
    place_slots.wait()
    pl.semaphore_wait(settled, COLS - 1)

    def arrival(target, semaphore):
        pltpu.make_async_copy(target, target, semaphore).wait()

    def send_piece(peer, lands):
        return pltpu.make_async_remote_copy(
            src_ref=outbox.at[peer],
            dst_ref=inbox.at[lands],
            send_sem=p_send,
            recv_sem=p_recv.at[lands // COLS],
            device_id=(peer // COLS, lax.rem(peer, COLS)),
            device_id_type=MESH,
        )

    def fill(peer):
        outbox[peer, pl.ds(0, 8), :] = pieces[slots[0, peer]]
        outbox[peer, pl.ds(8, 8), :] = pieces[slots[1, peer]]
        outbox[peer, pl.ds(16, 1), :] = ids[pl.ds(peer // 64, 1), :]

    @pl.loop(1, DEVICES)
    def _(k):
        peer = lax.rem(me + k, DEVICES)
        fill(peer)
        send_piece(peer, me).start()

    fill(me)
    pltpu.make_async_copy(outbox.at[me], inbox.at[me], p_recv.at[gx]).start()

    @pl.loop(0, ROWS)
    def _(t):
        group = lax.rem(gx + ROWS - t, ROWS)

        base = pl.multiple_of(group * COLS, COLS)
        arrival(inbox.at[pl.ds(base, COLS)], p_recv.at[group])
        for slot in range(2):
            for l in range(8):
                high, low = split(inbox[pl.ds(base, COLS), slot * 8 + l, :])
                arrived[pl.ds(pl.multiple_of(base + slot * 128, 16), COLS), pl.ds(l * 128, 128)] = high
                arrived[pl.ds(pl.multiple_of(base + 256 + slot * 128, 16), COLS), pl.ds(l * 128, 128)] = low

    marks[...] = jnp.transpose(inbox[:, 16, :])
    mine = lax.rem(me, 64)
    tile_rows = [marks[pl.ds(mine + 64 * slot, 1), :] for slot in range(2)]
    for load in loads[5:]:
        load.wait()

    def tile_at(turn, q, a):
        return q * 3 + a if turn == 0 else a * 3 + q

    def part(turn, third_of):
        return pl.ds(0, 9) if turn == 1 else pl.ds(3 * third_of, 3)

    def send_z(turn, third_of):
        tiles_of = part(turn, third_of)
        count = turn * 3 + third_of

        @pl.loop(1, COLS)
        def _(k):
            peer = lax.rem(gy + k, COLS)
            pltpu.make_async_remote_copy(
                src_ref=out_z.at[turn, peer // 2, lax.rem(peer, 2), tiles_of],
                dst_ref=in_y.at[turn, gy, tiles_of],
                send_sem=z_send,
                recv_sem=z_recv.at[count],
                device_id=(gx, peer),
                device_id_type=MESH,
            ).start()

        pltpu.make_async_copy(
            out_z.at[turn, gy // 2, lax.rem(gy, 2), tiles_of], in_y.at[turn, gy, tiles_of], z_recv.at[count]
        ).start()

    def wait_z(turn, third_of):
        arrival(in_y.at[turn, :, part(turn, third_of)], z_recv.at[turn * 3 + third_of])

    def send_y(turn, thirds):
        count = turn * 3 + thirds.start

        @pl.loop(1, ROWS)
        def _(k):
            peer = lax.rem(gx + k, ROWS)
            pltpu.make_async_remote_copy(
                src_ref=out_y.at[turn, peer, thirds],
                dst_ref=in_x.at[turn, gx, thirds],
                send_sem=y_send,
                recv_sem=y_recv.at[count],
                device_id=(peer, gy),
                device_id_type=MESH,
            ).start()

        pltpu.make_async_copy(
            out_y.at[turn, gx, thirds], in_x.at[turn, gx, thirds], y_recv.at[count]
        ).start()

    def wait_y(turn, thirds):
        arrival(in_x.at[turn, :, thirds], y_recv.at[turn * 3 + thirds.start])

    row = lax.broadcasted_iota(jnp.int32, (24, 8, 128), 1)
    tile_of = lax.broadcasted_iota(jnp.int32, (48, 128), 0)

    def stage_z(turn, q):
        bases = [((2 * turn + r) * 3 + q) * 48 for r in range(2)]
        hits = [
            jnp.concatenate(
                [jnp.where((tile_of + base).astype(F32) == tile_row, 1.0, 0.0) for base in bases], axis=0
            ).astype(BF16)
            for tile_row in tile_rows
        ]
        hits = jnp.concatenate(hits + hits, axis=1)
        for pair in range(4):
            added = jnp.dot(hits, arrived[:, pl.ds(pair * 256, 256)], preferred_element_type=F32)
            for half, value in enumerate(split(added)):
                for l in range(2):
                    for r in range(2):
                        cells[half, pl.ds((2 * pair + l) * 48, 48), pl.ds(r * 128, 128)] = value[
                            r * 48 : r * 48 + 48, l * 128 : l * 128 + 128
                        ]
        high, low = cells[0], cells[1]
        product = jnp.dot(
            third[...], jnp.concatenate((high, high, low), axis=0), preferred_element_type=F32
        )
        near = combine(product[:, :128]).reshape(24, 8, 128)
        far = combine(product[:, 128:]).reshape(24, 8, 128)
        even = jnp.where(row < 4, near, pltpu.roll(far, 4, 1))
        odd = jnp.where(row < 4, pltpu.roll(near, 4, 1), far)
        for a in range(3):
            out_z[turn, :, 0, tile_at(turn, q, a)] = even[a * 8 : a * 8 + 8]
            out_z[turn, :, 1, tile_at(turn, q, a)] = odd[a * 8 : a * 8 + 8]

    def stage_y(turn, thirds):
        for a in range(thirds.start, thirds.start + thirds.size):
            for q in range(3):
                value = in_y[turn, :, tile_at(turn, q, a)]
                for bit in range(4):
                    value = exchange_bit(value, 1 << bit, 3 + bit)
                high, low = split(value.reshape(128, 128))
                rows_y[pl.ds(a * 128, 128), pl.ds(q * 128, 128)] = high
                rows_y[pl.ds(a * 128, 128), pl.ds(N + q * 128, 128)] = high
                rows_y[pl.ds(a * 128, 128), pl.ds(2 * N + q * 128, 128)] = low
        product = lax.dot_general(
            second[...],
            rows_y[pl.ds(thirds.start * 128, thirds.size * 128), :],
            NT,
            preferred_element_type=F32,
        )
        for a in range(thirds.size):
            done = combine(product[:, a * 128 : a * 128 + 128])
            out_y[turn, :, thirds.start + a] = done.reshape(ROWS, 24, 128)

    def stage_x(turn, thirds):
        values = []
        for a in range(thirds.start, thirds.start + thirds.size):
            value = in_x[turn, :, a]
            value = exchange_bit(value, 4, 6)
            value = exchange_bit(value, 2, 1)
            values.append(exchange_bit(value, 1, 0).reshape(192, 128))
        high, low = split(jnp.concatenate(values, axis=0))
        rows = jnp.concatenate((high, high, low), axis=1)
        return [
            jnp.dot(rows, table[turn], preferred_element_type=F32) for table in (first_cos, first_sin)
        ]

    for turn in range(ROUNDS):
        for q in range(3):
            stage_z(turn, q)
            if turn == 0:
                send_z(turn, q)
        if turn == 1:
            send_z(turn, 0)
    for a in range(3):
        send_z(2, a)

    everything = pl.ds(0, 3)
    for q in range(3):
        wait_z(0, q)
    stage_y(0, everything)
    send_y(0, everything)
    wait_z(1, 0)
    stage_y(1, everything)
    send_y(1, everything)
    wait_y(0, everything)
    cos, sin = stage_x(0, everything)
    sum_cos[...] = cos
    sum_sin[...] = sin
    for a in range(3):
        wait_z(2, a)
        stage_y(2, pl.ds(a, 1))
        send_y(2, pl.ds(a, 1))
        if a == 0:
            wait_y(1, everything)
            cos, sin = stage_x(1, everything)
            sum_cos[...] += cos
            sum_sin[...] += sin

    arrival(outbox.at[pl.ds(0, DEVICES - 1)], p_send)
    arrival(in_y.at[:, pl.ds(0, COLS - 1)], z_send)

    for a in range(3):
        wait_y(2, pl.ds(a, 1))
        cos, sin = stage_x(2, pl.ds(a, 1))
        cos = cos + sum_cos[pl.ds(a * 192, 192), :]
        sin = sin + sum_sin[pl.ds(a * 192, 192), :]
        out[0, pl.ds(a * 4, 4)] = (cos[:96] - sin[96:]).reshape(4, 24, M)
        out[1, pl.ds(a * 4, 4)] = (sin[:96] + cos[96:]).reshape(4, 24, M)
    arrival(in_x.at[:, pl.ds(0, ROWS - 1)], y_send)


def whole(owners, tile_ids, samples, kernel, offsets, third, second, first_cos, first_sin):
    operands = (owners, tile_ids, samples, kernel, offsets, third, second, first_cos, first_sin)
    held = [pltpu.VMEM(x.shape, x.dtype) for x in operands[:5]] + [
        pltpu.VMEM((N, 3 * N), BF16),
        pltpu.VMEM((N, 3 * N), BF16),
        pltpu.VMEM((ROUNDS, N, M), BF16),
        pltpu.VMEM((ROUNDS, N, M), BF16),
    ]
    return pl.pallas_call(
        whole_kernel,
        out_shape=jax.ShapeDtypeStruct((2, 12, 24, M), F32),
        in_specs=[pl.BlockSpec(memory_space=pl.ANY)] * len(operands),
        out_specs=pl.BlockSpec(memory_space=pltpu.VMEM),
        scratch_shapes=held
        + [
            pltpu.VMEM((BLOCKS + 1, 8, 128), F32),
            pltpu.VMEM((8, 128), F32),
            pltpu.VMEM((8, 128), jnp.int32),
            pltpu.SMEM((8, 128), jnp.int32),
            pltpu.VMEM((DEVICES, SLOT_ROWS, 128), F32),
            pltpu.VMEM((DEVICES, SLOT_ROWS, 128), F32),
            pltpu.VMEM((128, 128), F32),
            pltpu.VMEM((512, 1024), BF16),
            pltpu.VMEM((2, N, 256), BF16),
            pltpu.VMEM((ROUNDS, 8, 2, 9, 8, 128), F32),
            pltpu.VMEM((ROUNDS, COLS, 9, 8, 128), F32),
            pltpu.VMEM((N, 3 * N), BF16),
            pltpu.VMEM((ROUNDS, ROWS, 3, 24, 128), F32),
            pltpu.VMEM((ROUNDS, ROWS, 3, 24, 128), F32),
            pltpu.VMEM((576, M), F32),
            pltpu.VMEM((576, M), F32),
            pltpu.SemaphoreType.REGULAR,
            pltpu.SemaphoreType.DMA((13,)),
            pltpu.SemaphoreType.DMA,
            pltpu.SemaphoreType.DMA,
            pltpu.SemaphoreType.DMA((ROWS,)),
            pltpu.SemaphoreType.DMA,
            pltpu.SemaphoreType.DMA((3 * ROUNDS,)),
            pltpu.SemaphoreType.DMA,
            pltpu.SemaphoreType.DMA((3 * ROUNDS,)),
        ],
        compiler_params=pltpu.CompilerParams(
            collective_id=0, has_side_effects=True, vmem_limit_bytes=48 << 20
        ),
        name="whole",
    )(*[pltpu.with_memory_space_constraint(x, pltpu.HBM) for x in operands])


def solution(mesh):
    third, second, first_cos, first_sin = tables()

    def on_device(samples, kernel, offsets, owners, tile_ids, deapod_first, deapod_second, deapod_third):
        along_x = whole(
            owners.reshape(1, BLOCKS),
            tile_ids.reshape(1, BLOCKS),
            samples,
            kernel,
            offsets.transpose(1, 0, 2),
            third,
            second,
            first_cos,
            first_sin,
        )
        return (
            along_x
            * deapod_third[None, :, None, None]
            * deapod_second[None, None, :, None]
            * deapod_first[None, None, None, :]
        )

    in_specs = (
        P(("gx", "gy"), None, None),
        P(("gx", "gy"), None, None, None),
        P(("gx", "gy"), None, None),
        P(("gx", "gy"), None),
        P(("gx", "gy")),
        P(),
        P("gx"),
        P("gy"),
    )
    return jax.shard_map(
        on_device, mesh=mesh, in_specs=in_specs, out_specs=P(None, "gy", "gx", None), check_vma=False
    )
```

```python
import math

import jax
import jax.numpy as jnp
import ml_dtypes
import numpy as np
from jax import lax
from jax.experimental import pallas as pl
from jax.experimental.pallas import tpu as pltpu
from jax.sharding import PartitionSpec as P

N = 384
M = 192
DEVICES = 128
ROWS, COLS = 8, 16
BLOCKS = 128
TILES = 864
SLOT_ROWS = 17
ROUNDS = 3
MESH = pl.DeviceIdType.MESH
F32 = jnp.float32
BF16 = jnp.bfloat16


def angles(cells, images):
    steps = np.mod((cells[:, None] - N // 2) * (images[None, :] - M // 2), N)
    phases = steps.astype(np.float64) * (2.0 * math.pi / N)
    return np.cos(phases) / math.sqrt(N), np.sin(phases) / math.sqrt(N)


def halves(table):
    table = table.astype(np.float32)
    high = table.astype(ml_dtypes.bfloat16)
    low = (table - high.astype(np.float32)).astype(ml_dtypes.bfloat16)
    return high, low


def left_table(cells, images):
    cos, sin = angles(cells, images)
    return np.concatenate(halves(np.concatenate((cos.T, sin.T))), axis=1)


def tables():
    every = np.arange(M)
    a, pair, side, low = np.meshgrid(np.arange(3), np.arange(8), np.arange(2), np.arange(4), indexing="ij")
    order = (12 * (2 * pair + side) + 4 * a + low).reshape(-1)
    l, d = np.meshgrid(np.arange(8), np.arange(48), indexing="ij")
    third = left_table((d * 8 + l).reshape(-1), order)
    q, g, j = np.meshgrid(np.arange(3), np.arange(COLS), np.arange(8), indexing="ij")
    second = left_table((g * 24 + q * 8 + j).reshape(-1), every)
    turn, lane = np.meshgrid(np.arange(ROUNDS), np.arange(128), indexing="ij")
    source = (lane >> 6) * 4 + (lane & 3)
    cells = source * 48 + (2 * turn + ((lane >> 2) & 1)) * 8 + ((lane >> 3) & 7)
    firsts = []
    for part in angles(cells.reshape(-1), every):
        high, low = halves(part.reshape(ROUNDS, 128, M))
        firsts.append(np.concatenate((high, low), axis=1))
    return third, second, firsts[0], firsts[1]


def split(value):
    high = value.astype(BF16)
    return high, (value - high.astype(F32)).astype(BF16)


def exchange_bit(value, axis_low, lane_bit):
    count, rows, lanes = value.shape
    shift = 1 << lane_bit
    pairs = value.reshape(count // (2 * axis_low), 2, axis_low * rows, lanes)
    first = pairs[:, 0].reshape(-1, lanes)
    second = pairs[:, 1].reshape(-1, lanes)
    lane = lax.broadcasted_iota(jnp.int32, first.shape, 1)
    upper = (lane & shift) != 0
    new_first = jnp.where(upper, pltpu.roll(second, shift, 1), first)
    new_second = jnp.where(upper, second, pltpu.roll(first, lanes - shift, 1))
    shape = (count // (2 * axis_low), axis_low * rows, lanes)
    out = jnp.stack((new_first.reshape(shape), new_second.reshape(shape)), axis=1)
    return out.reshape(value.shape)


def combine(product):
    rows = product.shape[0] // 2
    lane = lax.broadcasted_iota(jnp.int32, (rows, 128), 1)
    turned = pltpu.roll(product[rows:], 64, 1)
    return product[:rows] + jnp.where(lane < 64, -turned, turned)


NT = (((1,), (1,)), ((), ()))


def whole_kernel(
    owners_in,
    tile_ids_in,
    samples_in,
    kernel_in,
    offsets_in,
    third_in,
    second_in,
    first_cos_in,
    first_sin_in,
    out,
    owners,
    tile_ids,
    samples,
    kernel,
    offsets,
    third,
    second,
    first_cos,
    first_sin,
    pieces,
    ids,
    source_of,
    slots,
    outbox,
    inbox,
    marks,
    arrived,
    cells,
    out_z,
    in_y,
    rows_y,
    out_y,
    in_x,
    sum_cos,
    sum_sin,
    settled,
    load_sem,
    slot_sem,
    p_send,
    p_recv,
    z_send,
    z_recv,
    y_send,
    y_recv,
):
    gx, gy = lax.axis_index("gx"), lax.axis_index("gy")
    me = gx * COLS + gy

    loads = [
        pltpu.make_async_copy(source, target, load_sem.at[i])
        for i, (source, target) in enumerate(
            (
                (owners_in, owners),
                (tile_ids_in, tile_ids),
                (offsets_in, offsets),
                (samples_in, samples),
                (kernel_in, kernel),
                (third_in, third.at[:, pl.ds(0, 2 * N)]),
                (third_in.at[:, pl.ds(0, N)], third.at[:, pl.ds(2 * N, N)]),
                (second_in, second.at[:, pl.ds(0, 2 * N)]),
                (second_in.at[:, pl.ds(0, N)], second.at[:, pl.ds(2 * N, N)]),
                (first_cos_in, first_cos.at[:, pl.ds(0, 256)]),
                (first_cos_in.at[:, pl.ds(0, 128)], first_cos.at[:, pl.ds(256, 128)]),
                (first_sin_in, first_sin.at[:, pl.ds(0, 256)]),
                (first_sin_in.at[:, pl.ds(0, 128)], first_sin.at[:, pl.ds(256, 128)]),
            )
        )
    ]
    for load in loads[:5]:
        load.start()
    barrier = pltpu.get_barrier_semaphore()

    def greet(semaphore, x, y):
        pl.semaphore_signal(semaphore, inc=1, device_id=(x, y), device_id_type=MESH)

    @pl.loop(1, COLS)
    def _(k):
        greet(barrier, gx, lax.rem(gy + k, COLS))

    @pl.loop(1, ROWS)
    def _(k):
        greet(barrier, lax.rem(gx + k, ROWS), gy)

    for load in loads[5:]:
        load.start()

    loads[0].wait()
    loads[1].wait()
    lane = lax.broadcasted_iota(jnp.int32, (128, 128), 1)
    block = lax.broadcasted_iota(jnp.int32, (128, 128), 0)
    named = jnp.transpose(jnp.broadcast_to(owners[...], (128, 128))) == lane
    tiles = jnp.transpose(jnp.broadcast_to(tile_ids[...], (128, 128)))
    first = jnp.min(jnp.where(named, block, BLOCKS), axis=0, keepdims=True)
    last = jnp.max(jnp.where(named, block, -1), axis=0, keepdims=True)
    last = jnp.where(last > first, last, BLOCKS)
    source_of[pl.ds(0, 1), :] = first
    source_of[pl.ds(1, 1), :] = last
    place_slots = pltpu.make_async_copy(source_of, slots, slot_sem)
    place_slots.start()
    found = []
    for chosen in (first, last):
        tile = jnp.sum(jnp.where(named & (block == chosen), tiles, 0), axis=0, keepdims=True)
        found.append(jnp.where(chosen < BLOCKS, tile, TILES).astype(F32))
    low_lane = lax.broadcasted_iota(jnp.int32, (1, 128), 1) < 64
    ids[pl.ds(0, 1), :] = jnp.where(low_lane, found[0], pltpu.roll(found[1], 64, 1))
    ids[pl.ds(1, 1), :] = jnp.where(low_lane, pltpu.roll(found[0], 64, 1), found[1])

    for load in loads[2:5]:
        load.wait()
    pieces[BLOCKS] = jnp.zeros((8, 128), F32)
    cell = lax.broadcasted_iota(jnp.int32, (8, 128), 0)

    def spread(step):
        starts = [offsets[dim, pl.ds(pl.multiple_of(step * 16, 16), 16), :] for dim in range(3)]
        for u in range(16):
            n = step * 16 + u

            placed = []
            for dim in range(3):
                away = cell - starts[dim][u : u + 1]
                total = jnp.zeros((8, 128), F32)
                for k in range(4):
                    total = jnp.where(away == k, kernel[n, dim, pl.ds(k, 1), :], total)
                placed.append(total)
            real = samples[n, pl.ds(0, 1), :] * placed[0]
            imag = samples[n, pl.ds(1, 1), :] * placed[0]
            plane = jnp.concatenate((real, imag), axis=0)
            weight = (plane[:, None, :] * placed[1][None, :, :]).reshape(128, 128)
            high, low = split(weight)
            depth_high, depth_low = split(placed[2])
            left = jnp.concatenate(
                (
                    jnp.concatenate((depth_high, depth_high), axis=1),
                    jnp.concatenate((depth_low, jnp.zeros_like(depth_low)), axis=1),
                ),
                axis=0,
            )
            right = jnp.concatenate((high, low), axis=1)
            both = lax.dot_general(left, right, NT, preferred_element_type=F32)
            pieces[n] = both[:8] + both[8:]

    pl.loop(0, BLOCKS // 32)(spread)
    pl.semaphore_wait(barrier, COLS + ROWS - 2)

    @pl.loop(1, COLS)
    def _(k):
        greet(settled, gx, lax.rem(gy + k, COLS))

    pl.loop(BLOCKS // 32, BLOCKS // 16)(spread)
    place_slots.wait()
    pl.semaphore_wait(settled, COLS - 1)

    def arrival(target, semaphore):
        pltpu.make_async_copy(target, target, semaphore).wait()

    def send_piece(peer, lands):
        return pltpu.make_async_remote_copy(
            src_ref=outbox.at[peer],
            dst_ref=inbox.at[lands],
            send_sem=p_send,
            recv_sem=p_recv.at[lands // COLS],
            device_id=(peer // COLS, lax.rem(peer, COLS)),
            device_id_type=MESH,
        )

    def fill(peer):
        outbox[peer, pl.ds(0, 8), :] = pieces[slots[0, peer]]
        outbox[peer, pl.ds(8, 8), :] = pieces[slots[1, peer]]
        outbox[peer, pl.ds(16, 1), :] = ids[pl.ds(peer // 64, 1), :]

    @pl.loop(1, DEVICES)
    def _(k):
        peer = lax.rem(me + k, DEVICES)
        fill(peer)
        send_piece(peer, me).start()

    fill(me)
    pltpu.make_async_copy(outbox.at[me], inbox.at[me], p_recv.at[gx]).start()

    @pl.loop(0, ROWS)
    def _(t):
        group = lax.rem(gx + ROWS - t, ROWS)

        base = pl.multiple_of(group * COLS, COLS)
        arrival(inbox.at[pl.ds(base, COLS)], p_recv.at[group])
        for slot in range(2):
            for l in range(8):
                high, low = split(inbox[pl.ds(base, COLS), slot * 8 + l, :])
                arrived[pl.ds(pl.multiple_of(base + slot * 128, 16), COLS), pl.ds(l * 128, 128)] = high
                arrived[pl.ds(pl.multiple_of(base + 256 + slot * 128, 16), COLS), pl.ds(l * 128, 128)] = low

    marks[...] = jnp.transpose(inbox[:, 16, :])
    mine = lax.rem(me, 64)
    tile_rows = [marks[pl.ds(mine + 64 * slot, 1), :] for slot in range(2)]
    for load in loads[5:]:
        load.wait()

    def tile_at(turn, q, a):
        return q * 3 + a if turn == 0 else a * 3 + q

    def part(third_of):
        return pl.ds(3 * third_of, 3)

    def send_z(turn, third_of):
        tiles_of = part(third_of)
        count = turn * 3 + third_of

        @pl.loop(1, COLS)
        def _(k):
            peer = lax.rem(gy + k, COLS)
            pltpu.make_async_remote_copy(
                src_ref=out_z.at[turn, peer // 2, lax.rem(peer, 2), tiles_of],
                dst_ref=in_y.at[turn, gy, tiles_of],
                send_sem=z_send,
                recv_sem=z_recv.at[count],
                device_id=(gx, peer),
                device_id_type=MESH,
            ).start()

        pltpu.make_async_copy(
            out_z.at[turn, gy // 2, lax.rem(gy, 2), tiles_of], in_y.at[turn, gy, tiles_of], z_recv.at[count]
        ).start()

    def wait_z(turn, third_of):
        arrival(in_y.at[turn, :, part(third_of)], z_recv.at[turn * 3 + third_of])

    def send_y(turn, thirds):
        count = turn * 3 + thirds.start

        @pl.loop(1, ROWS)
        def _(k):
            peer = lax.rem(gx + k, ROWS)
            pltpu.make_async_remote_copy(
                src_ref=out_y.at[turn, peer, thirds],
                dst_ref=in_x.at[turn, gx, thirds],
                send_sem=y_send,
                recv_sem=y_recv.at[count],
                device_id=(peer, gy),
                device_id_type=MESH,
            ).start()

        pltpu.make_async_copy(
            out_y.at[turn, gx, thirds], in_x.at[turn, gx, thirds], y_recv.at[count]
        ).start()

    def wait_y(turn, thirds):
        arrival(in_x.at[turn, :, thirds], y_recv.at[turn * 3 + thirds.start])

    row = lax.broadcasted_iota(jnp.int32, (24, 8, 128), 1)
    tile_of = lax.broadcasted_iota(jnp.int32, (48, 128), 0)

    def add_pieces(turn, columns):
        bases = [((2 * turn + r) * 3 + q) * 48 for q in columns for r in range(2)]
        hits = [
            jnp.concatenate(
                [jnp.where((tile_of + base).astype(F32) == tile_row, 1.0, 0.0) for base in bases], axis=0
            ).astype(BF16)
            for tile_row in tile_rows
        ]
        hits = jnp.concatenate(hits + hits, axis=1)
        for pair in range(4):
            added = jnp.dot(hits, arrived[:, pl.ds(pair * 256, 256)], preferred_element_type=F32)
            for half, value in enumerate(split(added)):
                for l in range(2):
                    for i in range(len(bases)):
                        cells[columns[i // 2], half, pl.ds((2 * pair + l) * 48, 48), pl.ds(i % 2 * 128, 128)] = (
                            value[i * 48 : i * 48 + 48, l * 128 : l * 128 + 128]
                        )

    def stage_z(turn, q):
        high, low = cells[q, 0], cells[q, 1]
        product = jnp.dot(
            third[...], jnp.concatenate((high, high, low), axis=0), preferred_element_type=F32
        )
        near = combine(product[:, :128]).reshape(24, 8, 128)
        far = combine(product[:, 128:]).reshape(24, 8, 128)
        even = jnp.where(row < 4, near, pltpu.roll(far, 4, 1))
        odd = jnp.where(row < 4, pltpu.roll(near, 4, 1), far)
        for a in range(3):
            out_z[turn, :, 0, tile_at(turn, q, a)] = even[a * 8 : a * 8 + 8]
            out_z[turn, :, 1, tile_at(turn, q, a)] = odd[a * 8 : a * 8 + 8]

    def stage_y(parts):
        for i, (turn, a) in enumerate(parts):
            for q in range(3):
                value = in_y[turn, :, tile_at(turn, q, a)]
                for bit in range(4):
                    value = exchange_bit(value, 1 << bit, 3 + bit)
                high, low = split(value.reshape(128, 128))
                rows_y[pl.ds(i * 128, 128), pl.ds(q * 128, 128)] = high
                rows_y[pl.ds(i * 128, 128), pl.ds(N + q * 128, 128)] = high
                rows_y[pl.ds(i * 128, 128), pl.ds(2 * N + q * 128, 128)] = low
        product = lax.dot_general(
            second[...], rows_y[pl.ds(0, len(parts) * 128), :], NT, preferred_element_type=F32
        )
        for i, (turn, a) in enumerate(parts):
            done = combine(product[:, i * 128 : i * 128 + 128])
            out_y[turn, :, a] = done.reshape(ROWS, 24, 128)
            send_y(turn, pl.ds(a, 1))

    def stage_x(turn, thirds):
        values = []
        for a in range(thirds.start, thirds.start + thirds.size):
            value = in_x[turn, :, a]
            value = exchange_bit(value, 4, 6)
            value = exchange_bit(value, 2, 1)
            values.append(exchange_bit(value, 1, 0).reshape(192, 128))
        high, low = split(jnp.concatenate(values, axis=0))
        rows = jnp.concatenate((high, high, low), axis=1)
        return [
            jnp.dot(rows, table[turn], preferred_element_type=F32) for table in (first_cos, first_sin)
        ]

    def add_x(turn):
        for a in range(3):
            wait_y(turn, pl.ds(a, 1))
        return stage_x(turn, pl.ds(0, 3))

    for q in range(3):
        add_pieces(0, (q,))
        stage_z(0, q)
        send_z(0, q)
    add_pieces(1, (0, 1, 2))
    for q in range(3):
        stage_z(1, q)
    send_z(1, 0)
    send_z(1, 1)
    add_pieces(2, (0, 1, 2))
    for q in range(3):
        stage_z(2, q)
    send_z(1, 2)
    for q in range(3):
        wait_z(0, q)
    stage_y(((0, 0), (0, 1)))
    send_z(2, 0)
    wait_z(1, 0)
    stage_y(((0, 2), (1, 0)))
    send_z(2, 1)
    wait_z(1, 1)
    wait_z(1, 2)
    stage_y(((1, 1), (1, 2)))
    send_z(2, 2)
    sum_cos[...], sum_sin[...] = add_x(0)
    wait_z(2, 0)
    wait_z(2, 1)
    stage_y(((2, 0), (2, 1)))
    cos, sin = add_x(1)
    sum_cos[...] += cos
    sum_sin[...] += sin
    wait_z(2, 2)
    stage_y(((2, 2),))

    arrival(outbox.at[pl.ds(0, DEVICES - 1)], p_send)
    arrival(in_y.at[:, pl.ds(0, COLS - 1)], z_send)

    for a in range(3):
        wait_y(2, pl.ds(a, 1))
        cos, sin = stage_x(2, pl.ds(a, 1))
        cos = cos + sum_cos[pl.ds(a * 192, 192), :]
        sin = sin + sum_sin[pl.ds(a * 192, 192), :]
        out[0, pl.ds(a * 4, 4)] = (cos[:96] - sin[96:]).reshape(4, 24, M)
        out[1, pl.ds(a * 4, 4)] = (sin[:96] + cos[96:]).reshape(4, 24, M)
    arrival(in_x.at[:, pl.ds(0, ROWS - 1)], y_send)


def whole(owners, tile_ids, samples, kernel, offsets, third, second, first_cos, first_sin):
    operands = (owners, tile_ids, samples, kernel, offsets, third, second, first_cos, first_sin)
    held = [pltpu.VMEM(x.shape, x.dtype) for x in operands[:5]] + [
        pltpu.VMEM((N, 3 * N), BF16),
        pltpu.VMEM((N, 3 * N), BF16),
        pltpu.VMEM((ROUNDS, N, M), BF16),
        pltpu.VMEM((ROUNDS, N, M), BF16),
    ]
    return pl.pallas_call(
        whole_kernel,
        out_shape=jax.ShapeDtypeStruct((2, 12, 24, M), F32),
        in_specs=[pl.BlockSpec(memory_space=pl.ANY)] * len(operands),
        out_specs=pl.BlockSpec(memory_space=pltpu.VMEM),
        scratch_shapes=held
        + [
            pltpu.VMEM((BLOCKS + 1, 8, 128), F32),
            pltpu.VMEM((8, 128), F32),
            pltpu.VMEM((8, 128), jnp.int32),
            pltpu.SMEM((8, 128), jnp.int32),
            pltpu.VMEM((DEVICES, SLOT_ROWS, 128), F32),
            pltpu.VMEM((DEVICES, SLOT_ROWS, 128), F32),
            pltpu.VMEM((128, 128), F32),
            pltpu.VMEM((512, 1024), BF16),
            pltpu.VMEM((3, 2, N, 256), BF16),
            pltpu.VMEM((ROUNDS, 8, 2, 9, 8, 128), F32),
            pltpu.VMEM((ROUNDS, COLS, 9, 8, 128), F32),
            pltpu.VMEM((256, 3 * N), BF16),
            pltpu.VMEM((ROUNDS, ROWS, 3, 24, 128), F32),
            pltpu.VMEM((ROUNDS, ROWS, 3, 24, 128), F32),
            pltpu.VMEM((576, M), F32),
            pltpu.VMEM((576, M), F32),
            pltpu.SemaphoreType.REGULAR,
            pltpu.SemaphoreType.DMA((13,)),
            pltpu.SemaphoreType.DMA,
            pltpu.SemaphoreType.DMA,
            pltpu.SemaphoreType.DMA((ROWS,)),
            pltpu.SemaphoreType.DMA,
            pltpu.SemaphoreType.DMA((3 * ROUNDS,)),
            pltpu.SemaphoreType.DMA,
            pltpu.SemaphoreType.DMA((3 * ROUNDS,)),
        ],
        compiler_params=pltpu.CompilerParams(
            collective_id=0, has_side_effects=True, vmem_limit_bytes=48 << 20
        ),
        name="whole",
    )(*[pltpu.with_memory_space_constraint(x, pltpu.HBM) for x in operands])


def solution(mesh):
    third, second, first_cos, first_sin = tables()

    def on_device(samples, kernel, offsets, owners, tile_ids, deapod_first, deapod_second, deapod_third):
        along_x = whole(
            owners.reshape(1, BLOCKS),
            tile_ids.reshape(1, BLOCKS),
            samples,
            kernel,
            offsets.transpose(1, 0, 2),
            third,
            second,
            first_cos,
            first_sin,
        )
        return (
            along_x
            * deapod_third[None, :, None, None]
            * deapod_second[None, None, :, None]
            * deapod_first[None, None, None, :]
        )

    in_specs = (
        P(("gx", "gy"), None, None),
        P(("gx", "gy"), None, None, None),
        P(("gx", "gy"), None, None),
        P(("gx", "gy"), None),
        P(("gx", "gy")),
        P(),
        P("gx"),
        P("gy"),
    )
    return jax.shard_map(
        on_device, mesh=mesh, in_specs=in_specs, out_specs=P(None, "gy", "gx", None), check_vma=False
    )
```

```python
import math

import jax
import jax.numpy as jnp
import ml_dtypes
import numpy as np
from jax import lax
from jax.experimental import pallas as pl
from jax.experimental.pallas import tpu as pltpu
from jax.sharding import PartitionSpec as P

N = 384
M = 192
DEVICES = 128
ROWS, COLS = 8, 16
BLOCKS = 128
TILES = 864
SLOT_ROWS = 17
ROUNDS = 3
MESH = pl.DeviceIdType.MESH
F32 = jnp.float32
BF16 = jnp.bfloat16


def angles(cells, images):
    steps = np.mod((cells[:, None] - N // 2) * (images[None, :] - M // 2), N)
    phases = steps.astype(np.float64) * (2.0 * math.pi / N)
    return np.cos(phases) / math.sqrt(N), np.sin(phases) / math.sqrt(N)


def halves(table):
    table = table.astype(np.float32)
    high = table.astype(ml_dtypes.bfloat16)
    low = (table - high.astype(np.float32)).astype(ml_dtypes.bfloat16)
    return high, low


def left_table(cells, images):
    cos, sin = angles(cells, images)
    return np.concatenate(halves(np.concatenate((cos.T, sin.T))), axis=1)


def tables():
    every = np.arange(M)
    a, pair, side, low = np.meshgrid(np.arange(3), np.arange(8), np.arange(2), np.arange(4), indexing="ij")
    order = (12 * (2 * pair + side) + 4 * a + low).reshape(-1)
    l, d = np.meshgrid(np.arange(8), np.arange(48), indexing="ij")
    third = left_table((d * 8 + l).reshape(-1), order)
    q, g, j = np.meshgrid(np.arange(3), np.arange(COLS), np.arange(8), indexing="ij")
    second = left_table((g * 24 + q * 8 + j).reshape(-1), every)
    turn, lane = np.meshgrid(np.arange(ROUNDS), np.arange(128), indexing="ij")
    source = (lane >> 6) * 4 + (lane & 3)
    cells = source * 48 + (2 * turn + ((lane >> 2) & 1)) * 8 + ((lane >> 3) & 7)
    firsts = []
    for part in angles(cells.reshape(-1), every):
        high, low = halves(part.reshape(ROUNDS, 128, M))
        firsts.append(np.concatenate((high, low), axis=1))
    return third, second, firsts[0], firsts[1]


def split(value):
    high = value.astype(BF16)
    return high, (value - high.astype(F32)).astype(BF16)


def exchange_bit(value, axis_low, lane_bit):
    count, rows, lanes = value.shape
    shift = 1 << lane_bit
    pairs = value.reshape(count // (2 * axis_low), 2, axis_low * rows, lanes)
    first = pairs[:, 0].reshape(-1, lanes)
    second = pairs[:, 1].reshape(-1, lanes)
    lane = lax.broadcasted_iota(jnp.int32, first.shape, 1)
    upper = (lane & shift) != 0
    new_first = jnp.where(upper, pltpu.roll(second, shift, 1), first)
    new_second = jnp.where(upper, second, pltpu.roll(first, lanes - shift, 1))
    shape = (count // (2 * axis_low), axis_low * rows, lanes)
    out = jnp.stack((new_first.reshape(shape), new_second.reshape(shape)), axis=1)
    return out.reshape(value.shape)


def combine(product):
    rows = product.shape[0] // 2
    lane = lax.broadcasted_iota(jnp.int32, (rows, 128), 1)
    turned = pltpu.roll(product[rows:], 64, 1)
    return product[:rows] + jnp.where(lane < 64, -turned, turned)


NT = (((1,), (1,)), ((), ()))


def whole_kernel(
    owners_in,
    tile_ids_in,
    samples_in,
    kernel_in,
    offsets_in,
    third_in,
    second_in,
    first_cos_in,
    first_sin_in,
    out,
    owners,
    tile_ids,
    samples,
    kernel,
    offsets,
    third,
    second,
    first_cos,
    first_sin,
    pieces,
    ids,
    source_of,
    slots,
    outbox,
    inbox,
    marks,
    arrived,
    cells,
    out_z,
    in_y,
    rows_y,
    out_y,
    in_x,
    sum_cos,
    sum_sin,
    settled,
    load_sem,
    slot_sem,
    p_send,
    p_recv,
    z_send,
    z_recv,
    y_send,
    y_recv,
):
    gx, gy = lax.axis_index("gx"), lax.axis_index("gy")
    me = gx * COLS + gy

    loads = [
        pltpu.make_async_copy(source, target, load_sem.at[i])
        for i, (source, target) in enumerate(
            (
                (owners_in, owners),
                (tile_ids_in, tile_ids),
                (offsets_in, offsets),
                (samples_in, samples),
                (kernel_in, kernel),
                (third_in, third.at[:, pl.ds(0, 2 * N)]),
                (third_in.at[:, pl.ds(0, N)], third.at[:, pl.ds(2 * N, N)]),
                (second_in, second.at[:, pl.ds(0, 2 * N)]),
                (second_in.at[:, pl.ds(0, N)], second.at[:, pl.ds(2 * N, N)]),
                (first_cos_in, first_cos.at[:, pl.ds(0, 256)]),
                (first_cos_in.at[:, pl.ds(0, 128)], first_cos.at[:, pl.ds(256, 128)]),
                (first_sin_in, first_sin.at[:, pl.ds(0, 256)]),
                (first_sin_in.at[:, pl.ds(0, 128)], first_sin.at[:, pl.ds(256, 128)]),
            )
        )
    ]
    for load in loads[:5]:
        load.start()
    barrier = pltpu.get_barrier_semaphore()

    def greet(semaphore, x, y):
        pl.semaphore_signal(semaphore, inc=1, device_id=(x, y), device_id_type=MESH)

    def in_column(k):
        return jnp.where(gy + k >= COLS, gy + k - COLS, gy + k)

    def in_row(k):
        return jnp.where(gx + k >= ROWS, gx + k - ROWS, gx + k)

    for k in range(1, COLS):
        greet(barrier, gx, in_column(k))
    for k in range(1, ROWS):
        greet(barrier, in_row(k), gy)

    loads[0].wait()
    loads[1].wait()
    lane = lax.broadcasted_iota(jnp.int32, (128, 128), 1)
    block = lax.broadcasted_iota(jnp.int32, (128, 128), 0)
    named = jnp.transpose(jnp.broadcast_to(owners[...], (128, 128))) == lane
    tiles = jnp.transpose(jnp.broadcast_to(tile_ids[...], (128, 128)))
    first = jnp.min(jnp.where(named, block, BLOCKS), axis=0, keepdims=True)
    last = jnp.max(jnp.where(named, block, -1), axis=0, keepdims=True)
    last = jnp.where(last > first, last, BLOCKS)
    source_of[pl.ds(0, 1), :] = first
    source_of[pl.ds(1, 1), :] = last
    place_slots = pltpu.make_async_copy(source_of, slots, slot_sem)
    place_slots.start()
    found = []
    for chosen in (first, last):
        tile = jnp.sum(jnp.where(named & (block == chosen), tiles, 0), axis=0, keepdims=True)
        found.append(jnp.where(chosen < BLOCKS, tile, TILES).astype(F32))
    low_lane = lax.broadcasted_iota(jnp.int32, (1, 128), 1) < 64
    ids[pl.ds(0, 1), :] = jnp.where(low_lane, found[0], pltpu.roll(found[1], 64, 1))
    ids[pl.ds(1, 1), :] = jnp.where(low_lane, pltpu.roll(found[0], 64, 1), found[1])

    for load in loads[2:5]:
        load.wait()
    pieces[BLOCKS] = jnp.zeros((8, 128), F32)
    cell = lax.broadcasted_iota(jnp.int32, (8, 128), 0)

    def spread(step):
        starts = [offsets[dim, pl.ds(pl.multiple_of(step * 32, 32), 32), :] for dim in range(3)]
        for u in range(32):
            n = step * 32 + u

            placed = []
            for dim in range(3):
                away = cell - starts[dim][u : u + 1]
                total = jnp.zeros((8, 128), F32)
                for k in range(4):
                    total = jnp.where(away == k, kernel[n, dim, pl.ds(k, 1), :], total)
                placed.append(total)
            real = samples[n, pl.ds(0, 1), :] * placed[0]
            imag = samples[n, pl.ds(1, 1), :] * placed[0]
            plane = jnp.concatenate((real, imag), axis=0)
            weight = (plane[:, None, :] * placed[1][None, :, :]).reshape(128, 128)
            high, low = split(weight)
            depth_high, depth_low = split(placed[2])
            left = jnp.concatenate(
                (
                    jnp.concatenate((depth_high, depth_high), axis=1),
                    jnp.concatenate((depth_low, jnp.zeros_like(depth_low)), axis=1),
                ),
                axis=0,
            )
            right = jnp.concatenate((high, low), axis=1)
            both = lax.dot_general(left, right, NT, preferred_element_type=F32)
            pieces[n] = both[:8] + both[8:]

    pl.loop(0, BLOCKS // 64)(spread)
    pl.semaphore_wait(barrier, COLS + ROWS - 2)
    for k in range(1, COLS):
        greet(settled, gx, in_column(k))
    pl.loop(BLOCKS // 64, BLOCKS // 32)(spread)
    place_slots.wait()

    def arrival(target, semaphore):
        pltpu.make_async_copy(target, target, semaphore).wait()

    def send_piece(peer, lands):
        return pltpu.make_async_remote_copy(
            src_ref=outbox.at[peer],
            dst_ref=inbox.at[lands],
            send_sem=p_send,
            recv_sem=p_recv.at[lands // COLS],
            device_id=(peer // COLS, lax.rem(peer, COLS)),
            device_id_type=MESH,
        )

    def fill(peer):
        outbox[peer, pl.ds(0, 8), :] = pieces[slots[0, peer]]
        outbox[peer, pl.ds(8, 8), :] = pieces[slots[1, peer]]
        outbox[peer, pl.ds(16, 1), :] = ids[pl.ds(peer // 64, 1), :]

    def send_to(x, y):
        peer = x * COLS + y
        fill(peer)
        send_piece(peer, me).start()

    @pl.loop(1, COLS)
    def _(k):
        send_to(gx, in_column(k))

    @pl.loop(1, ROWS)
    def _(k):
        send_to(in_row(k), gy)

    pl.semaphore_wait(settled, COLS - 1)

    @pl.loop(1, ROWS)
    def _(i):
        @pl.loop(1, COLS)
        def _(k):
            send_to(in_row(i), in_column(k))

    for load in loads[5:]:
        load.start()
    fill(me)
    pltpu.make_async_copy(outbox.at[me], inbox.at[me], p_recv.at[gx]).start()

    @pl.loop(0, ROWS)
    def _(t):
        group = lax.rem(gx + ROWS - t, ROWS)

        base = pl.multiple_of(group * COLS, COLS)
        arrival(inbox.at[pl.ds(base, COLS)], p_recv.at[group])
        for slot in range(2):
            for l in range(8):
                high, low = split(inbox[pl.ds(base, COLS), slot * 8 + l, :])
                arrived[pl.ds(pl.multiple_of(base + slot * 128, 16), COLS), pl.ds(l * 128, 128)] = high
                arrived[pl.ds(pl.multiple_of(base + 256 + slot * 128, 16), COLS), pl.ds(l * 128, 128)] = low

    marks[...] = jnp.transpose(inbox[:, 16, :])
    mine = lax.rem(me, 64)
    tile_rows = [marks[pl.ds(mine + 64 * slot, 1), :] for slot in range(2)]
    for load in loads[5:]:
        load.wait()

    def tile_at(turn, q, a):
        return q * 3 + a if turn == 0 else a * 3 + q

    def part(third_of):
        return pl.ds(3 * third_of, 3)

    def send_z(turn, third_of):
        tiles_of = part(third_of)
        count = turn * 3 + third_of

        @pl.loop(1, COLS)
        def _(k):
            peer = lax.rem(gy + k, COLS)
            pltpu.make_async_remote_copy(
                src_ref=out_z.at[turn, peer // 2, lax.rem(peer, 2), tiles_of],
                dst_ref=in_y.at[turn, gy, tiles_of],
                send_sem=z_send,
                recv_sem=z_recv.at[count],
                device_id=(gx, peer),
                device_id_type=MESH,
            ).start()

        pltpu.make_async_copy(
            out_z.at[turn, gy // 2, lax.rem(gy, 2), tiles_of], in_y.at[turn, gy, tiles_of], z_recv.at[count]
        ).start()

    def wait_z(turn, third_of):
        arrival(in_y.at[turn, :, part(third_of)], z_recv.at[turn * 3 + third_of])

    def send_y(turn, thirds):
        count = turn * 3 + thirds.start

        @pl.loop(1, ROWS)
        def _(k):
            peer = lax.rem(gx + k, ROWS)
            pltpu.make_async_remote_copy(
                src_ref=out_y.at[turn, peer, thirds],
                dst_ref=in_x.at[turn, gx, thirds],
                send_sem=y_send,
                recv_sem=y_recv.at[count],
                device_id=(peer, gy),
                device_id_type=MESH,
            ).start()

        pltpu.make_async_copy(
            out_y.at[turn, gx, thirds], in_x.at[turn, gx, thirds], y_recv.at[count]
        ).start()

    def wait_y(turn, thirds):
        arrival(in_x.at[turn, :, thirds], y_recv.at[turn * 3 + thirds.start])

    row = lax.broadcasted_iota(jnp.int32, (24, 8, 128), 1)
    tile_of = lax.broadcasted_iota(jnp.int32, (48, 128), 0)

    def add_pieces(turn, columns):
        bases = [((2 * turn + r) * 3 + q) * 48 for q in columns for r in range(2)]
        hits = [
            jnp.concatenate(
                [jnp.where((tile_of + base).astype(F32) == tile_row, 1.0, 0.0) for base in bases], axis=0
            ).astype(BF16)
            for tile_row in tile_rows
        ]
        hits = jnp.concatenate(hits + hits, axis=1)
        for pair in range(4):
            added = jnp.dot(hits, arrived[:, pl.ds(pair * 256, 256)], preferred_element_type=F32)
            for half, value in enumerate(split(added)):
                for l in range(2):
                    for i in range(len(bases)):
                        cells[columns[i // 2], half, pl.ds((2 * pair + l) * 48, 48), pl.ds(i % 2 * 128, 128)] = (
                            value[i * 48 : i * 48 + 48, l * 128 : l * 128 + 128]
                        )

    def stage_z(turn, q):
        high, low = cells[q, 0], cells[q, 1]
        product = jnp.dot(
            third[...], jnp.concatenate((high, high, low), axis=0), preferred_element_type=F32
        )
        near = combine(product[:, :128]).reshape(24, 8, 128)
        far = combine(product[:, 128:]).reshape(24, 8, 128)
        even = jnp.where(row < 4, near, pltpu.roll(far, 4, 1))
        odd = jnp.where(row < 4, pltpu.roll(near, 4, 1), far)
        for a in range(3):
            out_z[turn, :, 0, tile_at(turn, q, a)] = even[a * 8 : a * 8 + 8]
            out_z[turn, :, 1, tile_at(turn, q, a)] = odd[a * 8 : a * 8 + 8]

    def stage_y(parts):
        for i, (turn, a) in enumerate(parts):
            for q in range(3):
                value = in_y[turn, :, tile_at(turn, q, a)]
                for bit in range(4):
                    value = exchange_bit(value, 1 << bit, 3 + bit)
                high, low = split(value.reshape(128, 128))
                rows_y[pl.ds(i * 128, 128), pl.ds(q * 128, 128)] = high
                rows_y[pl.ds(i * 128, 128), pl.ds(N + q * 128, 128)] = high
                rows_y[pl.ds(i * 128, 128), pl.ds(2 * N + q * 128, 128)] = low
        product = lax.dot_general(
            second[...], rows_y[pl.ds(0, len(parts) * 128), :], NT, preferred_element_type=F32
        )
        for i, (turn, a) in enumerate(parts):
            done = combine(product[:, i * 128 : i * 128 + 128])
            out_y[turn, :, a] = done.reshape(ROWS, 24, 128)
            send_y(turn, pl.ds(a, 1))

    def stage_x(turn, thirds):
        values = []
        for a in range(thirds.start, thirds.start + thirds.size):
            value = in_x[turn, :, a]
            value = exchange_bit(value, 4, 6)
            value = exchange_bit(value, 2, 1)
            values.append(exchange_bit(value, 1, 0).reshape(192, 128))
        high, low = split(jnp.concatenate(values, axis=0))
        rows = jnp.concatenate((high, high, low), axis=1)
        return [
            jnp.dot(rows, table[turn], preferred_element_type=F32) for table in (first_cos, first_sin)
        ]

    def add_x(turn):
        for a in range(3):
            wait_y(turn, pl.ds(a, 1))
        return stage_x(turn, pl.ds(0, 3))

    for q in range(3):
        add_pieces(0, (q,))
        stage_z(0, q)
        send_z(0, q)
    add_pieces(1, (0, 1, 2))
    for q in range(3):
        stage_z(1, q)
    send_z(1, 0)
    send_z(1, 1)
    add_pieces(2, (0, 1, 2))
    for q in range(3):
        stage_z(2, q)
    send_z(1, 2)
    for q in range(3):
        wait_z(0, q)
    stage_y(((0, 0), (0, 1)))
    send_z(2, 0)
    wait_z(1, 0)
    stage_y(((0, 2), (1, 0)))
    send_z(2, 1)
    wait_z(1, 1)
    wait_z(1, 2)
    stage_y(((1, 1), (1, 2)))
    send_z(2, 2)
    sum_cos[...], sum_sin[...] = add_x(0)
    wait_z(2, 0)
    wait_z(2, 1)
    stage_y(((2, 0), (2, 1)))
    cos, sin = add_x(1)
    sum_cos[...] += cos
    sum_sin[...] += sin
    wait_z(2, 2)
    stage_y(((2, 2),))

    arrival(outbox.at[pl.ds(0, DEVICES - 1)], p_send)
    arrival(in_y.at[:, pl.ds(0, COLS - 1)], z_send)

    for a in range(3):
        wait_y(2, pl.ds(a, 1))
        cos, sin = stage_x(2, pl.ds(a, 1))
        cos = cos + sum_cos[pl.ds(a * 192, 192), :]
        sin = sin + sum_sin[pl.ds(a * 192, 192), :]
        out[0, pl.ds(a * 4, 4)] = (cos[:96] - sin[96:]).reshape(4, 24, M)
        out[1, pl.ds(a * 4, 4)] = (sin[:96] + cos[96:]).reshape(4, 24, M)
    arrival(in_x.at[:, pl.ds(0, ROWS - 1)], y_send)


def whole(owners, tile_ids, samples, kernel, offsets, third, second, first_cos, first_sin):
    operands = (owners, tile_ids, samples, kernel, offsets, third, second, first_cos, first_sin)
    held = [pltpu.VMEM(x.shape, x.dtype) for x in operands[:5]] + [
        pltpu.VMEM((N, 3 * N), BF16),
        pltpu.VMEM((N, 3 * N), BF16),
        pltpu.VMEM((ROUNDS, N, M), BF16),
        pltpu.VMEM((ROUNDS, N, M), BF16),
    ]
    return pl.pallas_call(
        whole_kernel,
        out_shape=jax.ShapeDtypeStruct((2, 12, 24, M), F32),
        in_specs=[pl.BlockSpec(memory_space=pl.ANY)] * len(operands),
        out_specs=pl.BlockSpec(memory_space=pltpu.VMEM),
        scratch_shapes=held
        + [
            pltpu.VMEM((BLOCKS + 1, 8, 128), F32),
            pltpu.VMEM((8, 128), F32),
            pltpu.VMEM((8, 128), jnp.int32),
            pltpu.SMEM((8, 128), jnp.int32),
            pltpu.VMEM((DEVICES, SLOT_ROWS, 128), F32),
            pltpu.VMEM((DEVICES, SLOT_ROWS, 128), F32),
            pltpu.VMEM((128, 128), F32),
            pltpu.VMEM((512, 1024), BF16),
            pltpu.VMEM((3, 2, N, 256), BF16),
            pltpu.VMEM((ROUNDS, 8, 2, 9, 8, 128), F32),
            pltpu.VMEM((ROUNDS, COLS, 9, 8, 128), F32),
            pltpu.VMEM((256, 3 * N), BF16),
            pltpu.VMEM((ROUNDS, ROWS, 3, 24, 128), F32),
            pltpu.VMEM((ROUNDS, ROWS, 3, 24, 128), F32),
            pltpu.VMEM((576, M), F32),
            pltpu.VMEM((576, M), F32),
            pltpu.SemaphoreType.REGULAR,
            pltpu.SemaphoreType.DMA((13,)),
            pltpu.SemaphoreType.DMA,
            pltpu.SemaphoreType.DMA,
            pltpu.SemaphoreType.DMA((ROWS,)),
            pltpu.SemaphoreType.DMA,
            pltpu.SemaphoreType.DMA((3 * ROUNDS,)),
            pltpu.SemaphoreType.DMA,
            pltpu.SemaphoreType.DMA((3 * ROUNDS,)),
        ],
        compiler_params=pltpu.CompilerParams(
            collective_id=0, has_side_effects=True, vmem_limit_bytes=48 << 20
        ),
        name="whole",
    )(*[pltpu.with_memory_space_constraint(x, pltpu.HBM) for x in operands])


def solution(mesh):
    third, second, first_cos, first_sin = tables()

    def on_device(samples, kernel, offsets, owners, tile_ids, deapod_first, deapod_second, deapod_third):
        along_x = whole(
            owners.reshape(1, BLOCKS),
            tile_ids.reshape(1, BLOCKS),
            samples,
            kernel,
            offsets.transpose(1, 0, 2),
            third,
            second,
            first_cos,
            first_sin,
        )
        return (
            along_x
            * deapod_third[None, :, None, None]
            * deapod_second[None, None, :, None]
            * deapod_first[None, None, None, :]
        )

    in_specs = (
        P(("gx", "gy"), None, None),
        P(("gx", "gy"), None, None, None),
        P(("gx", "gy"), None, None),
        P(("gx", "gy"), None),
        P(("gx", "gy")),
        P(),
        P("gx"),
        P("gy"),
    )
    return jax.shard_map(
        on_device, mesh=mesh, in_specs=in_specs, out_specs=P(None, "gy", "gx", None), check_vma=False
    )
```

```python
import math

import jax
import jax.numpy as jnp
import ml_dtypes
import numpy as np
from jax import lax
from jax.experimental import pallas as pl
from jax.experimental.pallas import tpu as pltpu
from jax.sharding import PartitionSpec as P

N = 384
M = 192
DEVICES = 128
ROWS, COLS = 8, 16
BLOCKS = 128
TILES = 864
SLOT_ROWS = 17
ROUNDS = 3
MESH = pl.DeviceIdType.MESH
F32 = jnp.float32
BF16 = jnp.bfloat16


def angles(cells, images):
    steps = np.mod((cells[:, None] - N // 2) * (images[None, :] - M // 2), N)
    phases = steps.astype(np.float64) * (2.0 * math.pi / N)
    return np.cos(phases) / math.sqrt(N), np.sin(phases) / math.sqrt(N)


def halves(table):
    table = table.astype(np.float32)
    high = table.astype(ml_dtypes.bfloat16)
    low = (table - high.astype(np.float32)).astype(ml_dtypes.bfloat16)
    return high, low


def left_table(cells, images):
    cos, sin = angles(cells, images)
    return np.concatenate(halves(np.concatenate((cos.T, sin.T))), axis=1)


def tables():
    every = np.arange(M)
    a, pair, side, low = np.meshgrid(np.arange(3), np.arange(8), np.arange(2), np.arange(4), indexing="ij")
    order = (12 * (2 * pair + side) + 4 * a + low).reshape(-1)
    l, d = np.meshgrid(np.arange(8), np.arange(48), indexing="ij")
    third = left_table((d * 8 + l).reshape(-1), order)
    q, g, j = np.meshgrid(np.arange(3), np.arange(COLS), np.arange(8), indexing="ij")
    second = left_table((g * 24 + q * 8 + j).reshape(-1), every)
    turn, lane = np.meshgrid(np.arange(ROUNDS), np.arange(128), indexing="ij")
    source = (lane >> 6) * 4 + (lane & 3)
    cells = source * 48 + (2 * turn + ((lane >> 2) & 1)) * 8 + ((lane >> 3) & 7)
    firsts = []
    for part in angles(cells.reshape(-1), every):
        high, low = halves(part.reshape(ROUNDS, 128, M))
        firsts.append(np.concatenate((high, low), axis=1))
    return third, second, firsts[0], firsts[1]


def split(value):
    high = value.astype(BF16)
    return high, (value - high.astype(F32)).astype(BF16)


def exchange_bit(value, axis_low, lane_bit):
    count, rows, lanes = value.shape
    shift = 1 << lane_bit
    pairs = value.reshape(count // (2 * axis_low), 2, axis_low * rows, lanes)
    first = pairs[:, 0].reshape(-1, lanes)
    second = pairs[:, 1].reshape(-1, lanes)
    lane = lax.broadcasted_iota(jnp.int32, first.shape, 1)
    upper = (lane & shift) != 0
    new_first = jnp.where(upper, pltpu.roll(second, shift, 1), first)
    new_second = jnp.where(upper, second, pltpu.roll(first, lanes - shift, 1))
    shape = (count // (2 * axis_low), axis_low * rows, lanes)
    out = jnp.stack((new_first.reshape(shape), new_second.reshape(shape)), axis=1)
    return out.reshape(value.shape)


def combine(product):
    rows = product.shape[0] // 2
    lane = lax.broadcasted_iota(jnp.int32, (rows, 128), 1)
    turned = pltpu.roll(product[rows:], 64, 1)
    return product[:rows] + jnp.where(lane < 64, -turned, turned)


NT = (((1,), (1,)), ((), ()))


def whole_kernel(
    owners_in,
    tile_ids_in,
    samples_in,
    kernel_in,
    offsets_in,
    third_in,
    second_in,
    first_cos_in,
    first_sin_in,
    scale_first_in,
    scale_second_in,
    scale_third_in,
    out,
    owners,
    tile_ids,
    samples,
    kernel,
    offsets,
    third,
    second,
    first_cos,
    first_sin,
    scale_first,
    scale_second,
    scale_third,
    pieces,
    ids,
    source_of,
    slots,
    outbox,
    inbox,
    marks,
    arrived,
    cells,
    out_z,
    in_y,
    rows_y,
    out_y,
    in_x,
    sum_cos,
    sum_sin,
    settled,
    load_sem,
    slot_sem,
    p_send,
    p_recv,
    z_send,
    z_recv,
    y_send,
    y_recv,
):
    gx, gy = lax.axis_index("gx"), lax.axis_index("gy")
    me = gx * COLS + gy

    loads = [
        pltpu.make_async_copy(source, target, load_sem.at[i])
        for i, (source, target) in enumerate(
            (
                (owners_in, owners),
                (tile_ids_in, tile_ids),
                (offsets_in, offsets),
                (samples_in, samples),
                (kernel_in, kernel),
                (third_in, third.at[:, pl.ds(0, 2 * N)]),
                (third_in.at[:, pl.ds(0, N)], third.at[:, pl.ds(2 * N, N)]),
                (second_in, second.at[:, pl.ds(0, 2 * N)]),
                (second_in.at[:, pl.ds(0, N)], second.at[:, pl.ds(2 * N, N)]),
                (first_cos_in, first_cos.at[:, pl.ds(0, 256)]),
                (first_cos_in.at[:, pl.ds(0, 128)], first_cos.at[:, pl.ds(256, 128)]),
                (first_sin_in, first_sin.at[:, pl.ds(0, 256)]),
                (first_sin_in.at[:, pl.ds(0, 128)], first_sin.at[:, pl.ds(256, 128)]),
                (scale_first_in, scale_first),
                (scale_second_in, scale_second),
                (scale_third_in, scale_third),
            )
        )
    ]
    for load in loads[:5]:
        load.start()
    barrier = pltpu.get_barrier_semaphore()

    def greet(semaphore, x, y):
        pl.semaphore_signal(semaphore, inc=1, device_id=(x, y), device_id_type=MESH)

    def in_column(k):
        return jnp.where(gy + k >= COLS, gy + k - COLS, gy + k)

    def in_row(k):
        return jnp.where(gx + k >= ROWS, gx + k - ROWS, gx + k)

    for k in range(1, COLS):
        greet(barrier, gx, in_column(k))
    for k in range(1, ROWS):
        greet(barrier, in_row(k), gy)

    loads[0].wait()
    loads[1].wait()
    lane = lax.broadcasted_iota(jnp.int32, (128, 128), 1)
    block = lax.broadcasted_iota(jnp.int32, (128, 128), 0)
    named = jnp.transpose(jnp.broadcast_to(owners[...], (128, 128))) == lane
    tiles = jnp.transpose(jnp.broadcast_to(tile_ids[...], (128, 128)))
    first = jnp.min(jnp.where(named, block, BLOCKS), axis=0, keepdims=True)
    last = jnp.max(jnp.where(named, block, -1), axis=0, keepdims=True)
    last = jnp.where(last > first, last, BLOCKS)
    source_of[pl.ds(0, 1), :] = first
    source_of[pl.ds(1, 1), :] = last
    place_slots = pltpu.make_async_copy(source_of, slots, slot_sem)
    place_slots.start()
    found = []
    for chosen in (first, last):
        tile = jnp.sum(jnp.where(named & (block == chosen), tiles, 0), axis=0, keepdims=True)
        found.append(jnp.where(chosen < BLOCKS, tile, TILES).astype(F32))
    low_lane = lax.broadcasted_iota(jnp.int32, (1, 128), 1) < 64
    ids[pl.ds(0, 1), :] = jnp.where(low_lane, found[0], pltpu.roll(found[1], 64, 1))
    ids[pl.ds(1, 1), :] = jnp.where(low_lane, pltpu.roll(found[0], 64, 1), found[1])

    for load in loads[2:5]:
        load.wait()
    pieces[BLOCKS] = jnp.zeros((8, 128), F32)
    cell = lax.broadcasted_iota(jnp.int32, (8, 128), 0)

    def spread(step):
        starts = [offsets[dim, pl.ds(pl.multiple_of(step * 32, 32), 32), :] for dim in range(3)]
        for u in range(32):
            n = step * 32 + u

            placed = []
            for dim in range(3):
                away = cell - starts[dim][u : u + 1]
                total = jnp.zeros((8, 128), F32)
                for k in range(4):
                    total = jnp.where(away == k, kernel[n, dim, pl.ds(k, 1), :], total)
                placed.append(total)
            real = samples[n, pl.ds(0, 1), :] * placed[0]
            imag = samples[n, pl.ds(1, 1), :] * placed[0]
            plane = jnp.concatenate((real, imag), axis=0)
            weight = (plane[:, None, :] * placed[1][None, :, :]).reshape(128, 128)
            high, low = split(weight)
            depth_high, depth_low = split(placed[2])
            left = jnp.concatenate(
                (
                    jnp.concatenate((depth_high, depth_high), axis=1),
                    jnp.concatenate((depth_low, jnp.zeros_like(depth_low)), axis=1),
                ),
                axis=0,
            )
            right = jnp.concatenate((high, low), axis=1)
            both = lax.dot_general(left, right, NT, preferred_element_type=F32)
            pieces[n] = both[:8] + both[8:]

    pl.loop(0, BLOCKS // 64)(spread)
    pl.semaphore_wait(barrier, COLS + ROWS - 2)
    for k in range(1, COLS):
        greet(settled, gx, in_column(k))
    pl.loop(BLOCKS // 64, BLOCKS // 32)(spread)
    place_slots.wait()

    def arrival(target, semaphore):
        pltpu.make_async_copy(target, target, semaphore).wait()

    def send_piece(peer, lands):
        return pltpu.make_async_remote_copy(
            src_ref=outbox.at[peer],
            dst_ref=inbox.at[lands],
            send_sem=p_send,
            recv_sem=p_recv.at[lands // COLS],
            device_id=(peer // COLS, lax.rem(peer, COLS)),
            device_id_type=MESH,
        )

    def fill(peer):
        outbox[peer, pl.ds(0, 8), :] = pieces[slots[0, peer]]
        outbox[peer, pl.ds(8, 8), :] = pieces[slots[1, peer]]
        outbox[peer, pl.ds(16, 1), :] = ids[pl.ds(peer // 64, 1), :]

    def send_to(x, y):
        peer = x * COLS + y
        fill(peer)
        send_piece(peer, me).start()

    @pl.loop(1, COLS)
    def _(k):
        send_to(gx, in_column(k))

    @pl.loop(1, ROWS)
    def _(k):
        send_to(in_row(k), gy)

    pl.semaphore_wait(settled, COLS - 1)

    @pl.loop(1, ROWS)
    def _(i):
        @pl.loop(1, COLS)
        def _(k):
            send_to(in_row(i), in_column(k))

    for load in loads[5:]:
        load.start()
    fill(me)
    pltpu.make_async_copy(outbox.at[me], inbox.at[me], p_recv.at[gx]).start()

    @pl.loop(0, ROWS)
    def _(t):
        group = lax.rem(gx + ROWS - t, ROWS)

        base = pl.multiple_of(group * COLS, COLS)
        arrival(inbox.at[pl.ds(base, COLS)], p_recv.at[group])
        for slot in range(2):
            for l in range(8):
                high, low = split(inbox[pl.ds(base, COLS), slot * 8 + l, :])
                arrived[pl.ds(pl.multiple_of(base + slot * 128, 16), COLS), pl.ds(l * 128, 128)] = high
                arrived[pl.ds(pl.multiple_of(base + 256 + slot * 128, 16), COLS), pl.ds(l * 128, 128)] = low

    marks[...] = jnp.transpose(inbox[:, 16, :])
    mine = lax.rem(me, 64)
    tile_rows = [marks[pl.ds(mine + 64 * slot, 1), :] for slot in range(2)]
    for load in loads[5:]:
        load.wait()

    def tile_at(turn, q, a):
        return q * 3 + a if turn == 0 else a * 3 + q

    def part(third_of):
        return pl.ds(3 * third_of, 3)

    def send_z(turn, third_of, single=None):
        tiles_of = part(third_of) if single is None else pl.ds(3 * third_of + single, 1)
        count = turn * 3 + third_of if single is None else 3 * ROUNDS + single

        @pl.loop(1, COLS)
        def _(k):
            peer = lax.rem(gy + k, COLS)
            pltpu.make_async_remote_copy(
                src_ref=out_z.at[turn, peer // 2, lax.rem(peer, 2), tiles_of],
                dst_ref=in_y.at[turn, gy, tiles_of],
                send_sem=z_send,
                recv_sem=z_recv.at[count],
                device_id=(gx, peer),
                device_id_type=MESH,
            ).start()

        pltpu.make_async_copy(
            out_z.at[turn, gy // 2, lax.rem(gy, 2), tiles_of], in_y.at[turn, gy, tiles_of], z_recv.at[count]
        ).start()

    def wait_z(turn, third_of):
        if turn == 0 and third_of == 0:
            for single in range(3):
                arrival(in_y.at[0, :, pl.ds(single, 1)], z_recv.at[3 * ROUNDS + single])
        else:
            arrival(in_y.at[turn, :, part(third_of)], z_recv.at[turn * 3 + third_of])

    def send_y(turn, thirds):
        count = turn * 3 + thirds.start

        @pl.loop(1, ROWS)
        def _(k):
            peer = lax.rem(gx + k, ROWS)
            pltpu.make_async_remote_copy(
                src_ref=out_y.at[turn, peer, thirds],
                dst_ref=in_x.at[turn, gx, thirds],
                send_sem=y_send,
                recv_sem=y_recv.at[count],
                device_id=(peer, gy),
                device_id_type=MESH,
            ).start()

        pltpu.make_async_copy(
            out_y.at[turn, gx, thirds], in_x.at[turn, gx, thirds], y_recv.at[count]
        ).start()

    def wait_y(turn, thirds):
        arrival(in_x.at[turn, :, thirds], y_recv.at[turn * 3 + thirds.start])

    tile_of = lax.broadcasted_iota(jnp.int32, (48, 128), 0)

    def add_pieces(turn, columns):
        bases = [((2 * turn + r) * 3 + q) * 48 for q in columns for r in range(2)]
        hits = [
            jnp.concatenate(
                [jnp.where((tile_of + base).astype(F32) == tile_row, 1.0, 0.0) for base in bases], axis=0
            ).astype(BF16)
            for tile_row in tile_rows
        ]
        hits = jnp.concatenate(hits + hits, axis=1)
        for pair in range(4):
            added = jnp.dot(hits, arrived[:, pl.ds(pair * 256, 256)], preferred_element_type=F32)
            for half, value in enumerate(split(added)):
                for l in range(2):
                    for i in range(len(bases)):
                        cells[columns[i // 2], half, pl.ds((2 * pair + l) * 48, 48), pl.ds(i % 2 * 128, 128)] = (
                            value[i * 48 : i * 48 + 48, l * 128 : l * 128 + 128]
                        )

    def place_z(product, turn, q, thirds):
        count = 8 * len(thirds)
        near = combine(product[:, :128]).reshape(count, 8, 128)
        far = combine(product[:, 128:]).reshape(count, 8, 128)
        row = lax.broadcasted_iota(jnp.int32, (count, 8, 128), 1)
        even = jnp.where(row < 4, near, pltpu.roll(far, 4, 1))
        odd = jnp.where(row < 4, pltpu.roll(near, 4, 1), far)
        for i, a in enumerate(thirds):
            out_z[turn, :, 0, tile_at(turn, q, a)] = even[i * 8 : i * 8 + 8]
            out_z[turn, :, 1, tile_at(turn, q, a)] = odd[i * 8 : i * 8 + 8]

    def stage_z(turn, q):
        high, low = cells[q, 0], cells[q, 1]
        product = jnp.dot(
            third[...], jnp.concatenate((high, high, low), axis=0), preferred_element_type=F32
        )
        place_z(product, turn, q, range(3))

    def first_stage_z():
        high, low = cells[0, 0], cells[0, 1]
        right = jnp.concatenate((high, high, low), axis=0)
        for a in range(3):
            left = jnp.concatenate((third[pl.ds(64 * a, 64), :], third[pl.ds(M + 64 * a, 64), :]), axis=0)
            place_z(jnp.dot(left, right, preferred_element_type=F32), 0, 0, (a,))
            send_z(0, 0, a)

    def stage_y(parts):
        for i, (turn, a) in enumerate(parts):
            for q in range(3):
                value = in_y[turn, :, tile_at(turn, q, a)]
                for bit in range(4):
                    value = exchange_bit(value, 1 << bit, 3 + bit)
                high, low = split(value.reshape(128, 128))
                rows_y[pl.ds(i * 128, 128), pl.ds(q * 128, 128)] = high
                rows_y[pl.ds(i * 128, 128), pl.ds(N + q * 128, 128)] = high
                rows_y[pl.ds(i * 128, 128), pl.ds(2 * N + q * 128, 128)] = low
        product = lax.dot_general(
            second[...], rows_y[pl.ds(0, len(parts) * 128), :], NT, preferred_element_type=F32
        )
        for i, (turn, a) in enumerate(parts):
            done = combine(product[:, i * 128 : i * 128 + 128])
            out_y[turn, :, a] = done.reshape(ROWS, 24, 128)
            send_y(turn, pl.ds(a, 1))

    def stage_x(turn, thirds):
        values = []
        for a in range(thirds.start, thirds.start + thirds.size):
            value = in_x[turn, :, a]
            value = exchange_bit(value, 4, 6)
            value = exchange_bit(value, 2, 1)
            values.append(exchange_bit(value, 1, 0).reshape(192, 128))
        high, low = split(jnp.concatenate(values, axis=0))
        rows = jnp.concatenate((high, high, low), axis=1)
        return [
            jnp.dot(rows, table[turn], preferred_element_type=F32) for table in (first_cos, first_sin)
        ]

    def add_x(turn):
        for a in range(3):
            wait_y(turn, pl.ds(a, 1))
        return stage_x(turn, pl.ds(0, 3))

    add_pieces(0, (0,))
    first_stage_z()
    for q in range(1, 3):
        add_pieces(0, (q,))
        stage_z(0, q)
        send_z(0, q)
    add_pieces(1, (0, 1, 2))
    for q in range(3):
        stage_z(1, q)
    send_z(1, 0)
    send_z(1, 1)
    add_pieces(2, (0, 1, 2))
    for q in range(3):
        stage_z(2, q)
    send_z(1, 2)
    for q in range(3):
        wait_z(0, q)
    stage_y(((0, 0), (0, 1)))
    send_z(2, 0)
    wait_z(1, 0)
    stage_y(((0, 2), (1, 0)))
    send_z(2, 1)
    wait_z(1, 1)
    wait_z(1, 2)
    stage_y(((1, 1), (1, 2)))
    send_z(2, 2)
    sum_cos[...], sum_sin[...] = add_x(0)
    wait_z(2, 0)
    wait_z(2, 1)
    stage_y(((2, 0), (2, 1)))
    cos, sin = add_x(1)
    sum_cos[...] += cos
    sum_sin[...] += sin
    wait_z(2, 2)
    stage_y(((2, 2),))

    diagonal = lax.broadcasted_iota(jnp.int32, (24, 24), 0) == lax.broadcasted_iota(jnp.int32, (24, 24), 1)
    column = jnp.sum(jnp.where(diagonal, scale_second[...], 0.0), axis=1, keepdims=True)
    plane = column * scale_first[...]

    arrival(outbox.at[pl.ds(0, DEVICES - 1)], p_send)
    arrival(in_y.at[:, pl.ds(0, COLS - 1)], z_send)

    for a in range(3):
        wait_y(2, pl.ds(a, 1))
        cos, sin = stage_x(2, pl.ds(a, 1))
        cos = cos + sum_cos[pl.ds(a * 192, 192), :]
        sin = sin + sum_sin[pl.ds(a * 192, 192), :]
        real = (cos[:96] - sin[96:]).reshape(4, 24, M)
        imag = (sin[:96] + cos[96:]).reshape(4, 24, M)
        for b in range(4):
            scale = plane * scale_third[0, a * 4 + b]
            out[0, a * 4 + b] = real[b] * scale
            out[1, a * 4 + b] = imag[b] * scale
    arrival(in_x.at[:, pl.ds(0, ROWS - 1)], y_send)


def whole(*operands):
    held = [pltpu.VMEM(x.shape, x.dtype) for x in operands[:5]] + [
        pltpu.VMEM((N, 3 * N), BF16),
        pltpu.VMEM((N, 3 * N), BF16),
        pltpu.VMEM((ROUNDS, N, M), BF16),
        pltpu.VMEM((ROUNDS, N, M), BF16),
        pltpu.VMEM((1, M), F32),
        pltpu.VMEM((1, 24), F32),
        pltpu.SMEM((1, 12), F32),
    ]
    return pl.pallas_call(
        whole_kernel,
        out_shape=jax.ShapeDtypeStruct((2, 12, 24, M), F32),
        in_specs=[pl.BlockSpec(memory_space=pl.ANY)] * len(operands),
        out_specs=pl.BlockSpec(memory_space=pltpu.VMEM),
        scratch_shapes=held
        + [
            pltpu.VMEM((BLOCKS + 1, 8, 128), F32),
            pltpu.VMEM((8, 128), F32),
            pltpu.VMEM((8, 128), jnp.int32),
            pltpu.SMEM((8, 128), jnp.int32),
            pltpu.VMEM((DEVICES, SLOT_ROWS, 128), F32),
            pltpu.VMEM((DEVICES, SLOT_ROWS, 128), F32),
            pltpu.VMEM((128, 128), F32),
            pltpu.VMEM((512, 1024), BF16),
            pltpu.VMEM((3, 2, N, 256), BF16),
            pltpu.VMEM((ROUNDS, 8, 2, 9, 8, 128), F32),
            pltpu.VMEM((ROUNDS, COLS, 9, 8, 128), F32),
            pltpu.VMEM((256, 3 * N), BF16),
            pltpu.VMEM((ROUNDS, ROWS, 3, 24, 128), F32),
            pltpu.VMEM((ROUNDS, ROWS, 3, 24, 128), F32),
            pltpu.VMEM((576, M), F32),
            pltpu.VMEM((576, M), F32),
            pltpu.SemaphoreType.REGULAR,
            pltpu.SemaphoreType.DMA((16,)),
            pltpu.SemaphoreType.DMA,
            pltpu.SemaphoreType.DMA,
            pltpu.SemaphoreType.DMA((ROWS,)),
            pltpu.SemaphoreType.DMA,
            pltpu.SemaphoreType.DMA((3 * ROUNDS + 3,)),
            pltpu.SemaphoreType.DMA,
            pltpu.SemaphoreType.DMA((3 * ROUNDS,)),
        ],
        compiler_params=pltpu.CompilerParams(
            collective_id=0, has_side_effects=True, vmem_limit_bytes=48 << 20
        ),
        name="whole",
    )(*[pltpu.with_memory_space_constraint(x, pltpu.HBM) for x in operands])


def solution(mesh):
    third, second, first_cos, first_sin = tables()

    def on_device(samples, kernel, offsets, owners, tile_ids, deapod_first, deapod_second, deapod_third):
        return whole(
            owners.reshape(1, BLOCKS),
            tile_ids.reshape(1, BLOCKS),
            samples,
            kernel,
            offsets.transpose(1, 0, 2),
            third,
            second,
            first_cos,
            first_sin,
            deapod_first.reshape(1, M),
            deapod_second.reshape(1, 24),
            deapod_third.reshape(1, 12),
        )

    in_specs = (
        P(("gx", "gy"), None, None),
        P(("gx", "gy"), None, None, None),
        P(("gx", "gy"), None, None),
        P(("gx", "gy"), None),
        P(("gx", "gy")),
        P(),
        P("gx"),
        P("gy"),
    )
    return jax.shard_map(
        on_device, mesh=mesh, in_specs=in_specs, out_specs=P(None, "gy", "gx", None), check_vma=False
    )
```

```python
import math

import jax
import jax.numpy as jnp
import ml_dtypes
import numpy as np
from jax import lax
from jax.experimental import pallas as pl
from jax.experimental.pallas import tpu as pltpu
from jax.sharding import PartitionSpec as P

N = 384
M = 192
DEVICES = 128
ROWS, COLS = 8, 16
BLOCKS = 128
TILES = 864
SLOT_ROWS = 17
ROUNDS = 3
MESH = pl.DeviceIdType.MESH
F32 = jnp.float32
BF16 = jnp.bfloat16


def angles(cells, images):
    steps = np.mod((cells[:, None] - N // 2) * (images[None, :] - M // 2), N)
    phases = steps.astype(np.float64) * (2.0 * math.pi / N)
    return np.cos(phases) / math.sqrt(N), np.sin(phases) / math.sqrt(N)


def halves(table):
    table = table.astype(np.float32)
    high = table.astype(ml_dtypes.bfloat16)
    low = (table - high.astype(np.float32)).astype(ml_dtypes.bfloat16)
    return high, low


def left_table(cells, images):
    cos, sin = angles(cells, images)
    return np.concatenate(halves(np.concatenate((cos.T, sin.T))), axis=1)


def tables():
    every = np.arange(M)
    a, pair, side, low = np.meshgrid(np.arange(3), np.arange(8), np.arange(2), np.arange(4), indexing="ij")
    order = (12 * (2 * pair + side) + 4 * a + low).reshape(-1)
    l, d = np.meshgrid(np.arange(8), np.arange(48), indexing="ij")
    third = left_table((d * 8 + l).reshape(-1), order)
    q, g, j = np.meshgrid(np.arange(3), np.arange(COLS), np.arange(8), indexing="ij")
    second = left_table((g * 24 + q * 8 + j).reshape(-1), every)
    turn, lane = np.meshgrid(np.arange(ROUNDS), np.arange(128), indexing="ij")
    source = (lane >> 6) * 4 + (lane & 3)
    cells = source * 48 + (2 * turn + ((lane >> 2) & 1)) * 8 + ((lane >> 3) & 7)
    firsts = []
    for part in angles(cells.reshape(-1), every):
        high, low = halves(part.reshape(ROUNDS, 128, M))
        firsts.append(np.concatenate((high, low), axis=1))
    return third, second, firsts[0], firsts[1]


def split(value):
    high = value.astype(BF16)
    return high, (value - high.astype(F32)).astype(BF16)


def exchange_bit(value, axis_low, lane_bit):
    count, rows, lanes = value.shape
    shift = 1 << lane_bit
    pairs = value.reshape(count // (2 * axis_low), 2, axis_low * rows, lanes)
    first = pairs[:, 0].reshape(-1, lanes)
    second = pairs[:, 1].reshape(-1, lanes)
    lane = lax.broadcasted_iota(jnp.int32, first.shape, 1)
    upper = (lane & shift) != 0
    new_first = jnp.where(upper, pltpu.roll(second, shift, 1), first)
    new_second = jnp.where(upper, second, pltpu.roll(first, lanes - shift, 1))
    shape = (count // (2 * axis_low), axis_low * rows, lanes)
    out = jnp.stack((new_first.reshape(shape), new_second.reshape(shape)), axis=1)
    return out.reshape(value.shape)


def combine(product):
    rows = product.shape[0] // 2
    lane = lax.broadcasted_iota(jnp.int32, (rows, 128), 1)
    turned = pltpu.roll(product[rows:], 64, 1)
    return product[:rows] + jnp.where(lane < 64, -turned, turned)


NT = (((1,), (1,)), ((), ()))


def whole_kernel(
    owners_in,
    tile_ids_in,
    samples_in,
    kernel_in,
    offsets_in,
    third_in,
    second_in,
    first_cos_in,
    first_sin_in,
    out,
    owners,
    tile_ids,
    samples,
    kernel,
    offsets,
    third,
    second,
    first_cos,
    first_sin,
    pieces,
    ids,
    source_of,
    slots,
    outbox,
    inbox,
    marks,
    arrived,
    cells,
    out_z,
    in_y,
    rows_y,
    out_y,
    in_x,
    sum_cos,
    sum_sin,
    settled,
    load_sem,
    slot_sem,
    p_send,
    p_recv,
    z_send,
    z_recv,
    y_send,
    y_recv,
):
    gx, gy = lax.axis_index("gx"), lax.axis_index("gy")
    me = gx * COLS + gy

    loads = [
        pltpu.make_async_copy(source, target, load_sem.at[i])
        for i, (source, target) in enumerate(
            (
                (owners_in, owners),
                (tile_ids_in, tile_ids),
                (offsets_in, offsets),
                (samples_in, samples),
                (kernel_in, kernel),
                (third_in, third.at[:, pl.ds(0, 2 * N)]),
                (third_in.at[:, pl.ds(0, N)], third.at[:, pl.ds(2 * N, N)]),
                (second_in, second.at[:, pl.ds(0, 2 * N)]),
                (second_in.at[:, pl.ds(0, N)], second.at[:, pl.ds(2 * N, N)]),
                (first_cos_in, first_cos.at[:, pl.ds(0, 256)]),
                (first_cos_in.at[:, pl.ds(0, 128)], first_cos.at[:, pl.ds(256, 128)]),
                (first_sin_in, first_sin.at[:, pl.ds(0, 256)]),
                (first_sin_in.at[:, pl.ds(0, 128)], first_sin.at[:, pl.ds(256, 128)]),
            )
        )
    ]
    for load in loads[:5]:
        load.start()
    barrier = pltpu.get_barrier_semaphore()

    def greet(semaphore, x, y):
        pl.semaphore_signal(semaphore, inc=1, device_id=(x, y), device_id_type=MESH)

    def in_column(k):
        return jnp.where(gy + k >= COLS, gy + k - COLS, gy + k)

    def in_row(k):
        return jnp.where(gx + k >= ROWS, gx + k - ROWS, gx + k)

    for k in range(1, COLS):
        greet(barrier, gx, in_column(k))
    for k in range(1, ROWS):
        greet(barrier, in_row(k), gy)

    loads[0].wait()
    loads[1].wait()
    lane = lax.broadcasted_iota(jnp.int32, (128, 128), 1)
    block = lax.broadcasted_iota(jnp.int32, (128, 128), 0)
    named = jnp.transpose(jnp.broadcast_to(owners[...], (128, 128))) == lane
    tiles = jnp.transpose(jnp.broadcast_to(tile_ids[...], (128, 128)))
    first = jnp.min(jnp.where(named, block, BLOCKS), axis=0, keepdims=True)
    last = jnp.max(jnp.where(named, block, -1), axis=0, keepdims=True)
    last = jnp.where(last > first, last, BLOCKS)
    source_of[pl.ds(0, 1), :] = first
    source_of[pl.ds(1, 1), :] = last
    place_slots = pltpu.make_async_copy(source_of, slots, slot_sem)
    place_slots.start()
    found = []
    for chosen in (first, last):
        tile = jnp.sum(jnp.where(named & (block == chosen), tiles, 0), axis=0, keepdims=True)
        found.append(jnp.where(chosen < BLOCKS, tile, TILES).astype(F32))
    low_lane = lax.broadcasted_iota(jnp.int32, (1, 128), 1) < 64
    ids[pl.ds(0, 1), :] = jnp.where(low_lane, found[0], pltpu.roll(found[1], 64, 1))
    ids[pl.ds(1, 1), :] = jnp.where(low_lane, pltpu.roll(found[0], 64, 1), found[1])

    for load in loads[2:5]:
        load.wait()
    pieces[BLOCKS] = jnp.zeros((8, 128), F32)
    cell = lax.broadcasted_iota(jnp.int32, (8, 128), 0)

    def spread(step):
        starts = [offsets[dim, pl.ds(pl.multiple_of(step * 32, 32), 32), :] for dim in range(3)]
        for u in range(32):
            n = step * 32 + u

            placed = []
            for dim in range(3):
                away = cell - starts[dim][u : u + 1]
                total = jnp.zeros((8, 128), F32)
                for k in range(4):
                    total = jnp.where(away == k, kernel[n, dim, pl.ds(k, 1), :], total)
                placed.append(total)
            real = samples[n, pl.ds(0, 1), :] * placed[0]
            imag = samples[n, pl.ds(1, 1), :] * placed[0]
            plane = jnp.concatenate((real, imag), axis=0)
            weight = (plane[:, None, :] * placed[1][None, :, :]).reshape(128, 128)
            high, low = split(weight)
            depth_high, depth_low = split(placed[2])
            left = jnp.concatenate(
                (
                    jnp.concatenate((depth_high, depth_high), axis=1),
                    jnp.concatenate((depth_low, jnp.zeros_like(depth_low)), axis=1),
                ),
                axis=0,
            )
            right = jnp.concatenate((high, low), axis=1)
            both = lax.dot_general(left, right, NT, preferred_element_type=F32)
            pieces[n] = both[:8] + both[8:]

    pl.loop(0, 1)(spread)
    pl.semaphore_wait(barrier, COLS + ROWS - 2)
    for k in range(1, COLS):
        greet(settled, gx, in_column(k))
    pl.loop(1, BLOCKS // 32)(spread)
    place_slots.wait()

    def arrival(target, semaphore):
        pltpu.make_async_copy(target, target, semaphore).wait()

    def send_piece(peer, lands):
        return pltpu.make_async_remote_copy(
            src_ref=outbox.at[peer],
            dst_ref=inbox.at[lands],
            send_sem=p_send,
            recv_sem=p_recv.at[lands // COLS],
            device_id=(peer // COLS, lax.rem(peer, COLS)),
            device_id_type=MESH,
        )

    def fill(peer):
        outbox[peer, pl.ds(0, 8), :] = pieces[slots[0, peer]]
        outbox[peer, pl.ds(8, 8), :] = pieces[slots[1, peer]]
        outbox[peer, pl.ds(16, 1), :] = ids[pl.ds(peer // 64, 1), :]

    def send_to(x, y):
        peer = x * COLS + y
        fill(peer)
        send_piece(peer, me).start()

    @pl.loop(1, COLS)
    def _(k):
        send_to(gx, in_column(k))

    @pl.loop(1, ROWS)
    def _(k):
        send_to(in_row(k), gy)

    pl.semaphore_wait(settled, COLS - 1)

    @pl.loop(1, ROWS)
    def _(i):
        @pl.loop(1, COLS)
        def _(k):
            send_to(in_row(i), in_column(k))

    for load in loads[5:]:
        load.start()
    fill(me)
    pltpu.make_async_copy(outbox.at[me], inbox.at[me], p_recv.at[gx]).start()

    @pl.loop(0, ROWS)
    def _(t):
        group = lax.rem(gx + ROWS - t, ROWS)

        base = pl.multiple_of(group * COLS, COLS)
        arrival(inbox.at[pl.ds(base, COLS)], p_recv.at[group])
        for slot in range(2):
            for l in range(8):
                high, low = split(inbox[pl.ds(base, COLS), slot * 8 + l, :])
                arrived[pl.ds(pl.multiple_of(base + slot * 128, 16), COLS), pl.ds(l * 128, 128)] = high
                arrived[pl.ds(pl.multiple_of(base + 256 + slot * 128, 16), COLS), pl.ds(l * 128, 128)] = low

    marks[...] = jnp.transpose(inbox[:, 16, :])
    mine = lax.rem(me, 64)
    tile_rows = [marks[pl.ds(mine + 64 * slot, 1), :] for slot in range(2)]
    for load in loads[5:]:
        load.wait()

    def tile_at(turn, q, a):
        return q * 3 + a if turn == 0 else a * 3 + q

    def part(third_of):
        return pl.ds(3 * third_of, 3)

    def send_z(turn, third_of):
        tiles_of = part(third_of)
        count = turn * 3 + third_of

        @pl.loop(1, COLS)
        def _(k):
            peer = lax.rem(gy + k, COLS)
            pltpu.make_async_remote_copy(
                src_ref=out_z.at[turn, peer // 2, lax.rem(peer, 2), tiles_of],
                dst_ref=in_y.at[turn, gy, tiles_of],
                send_sem=z_send,
                recv_sem=z_recv.at[count],
                device_id=(gx, peer),
                device_id_type=MESH,
            ).start()

        pltpu.make_async_copy(
            out_z.at[turn, gy // 2, lax.rem(gy, 2), tiles_of], in_y.at[turn, gy, tiles_of], z_recv.at[count]
        ).start()

    def wait_z(turn, third_of):
        arrival(in_y.at[turn, :, part(third_of)], z_recv.at[turn * 3 + third_of])

    def send_y(turn, thirds):
        count = turn * 3 + thirds.start

        @pl.loop(1, ROWS)
        def _(k):
            peer = lax.rem(gx + k, ROWS)
            pltpu.make_async_remote_copy(
                src_ref=out_y.at[turn, peer, thirds],
                dst_ref=in_x.at[turn, gx, thirds],
                send_sem=y_send,
                recv_sem=y_recv.at[count],
                device_id=(peer, gy),
                device_id_type=MESH,
            ).start()

        pltpu.make_async_copy(
            out_y.at[turn, gx, thirds], in_x.at[turn, gx, thirds], y_recv.at[count]
        ).start()

    def wait_y(turn, thirds):
        arrival(in_x.at[turn, :, thirds], y_recv.at[turn * 3 + thirds.start])

    row = lax.broadcasted_iota(jnp.int32, (24, 8, 128), 1)
    tile_of = lax.broadcasted_iota(jnp.int32, (48, 128), 0)

    def add_pieces(turn, columns):
        bases = [((2 * turn + r) * 3 + q) * 48 for q in columns for r in range(2)]
        hits = [
            jnp.concatenate(
                [jnp.where((tile_of + base).astype(F32) == tile_row, 1.0, 0.0) for base in bases], axis=0
            ).astype(BF16)
            for tile_row in tile_rows
        ]
        hits = jnp.concatenate(hits + hits, axis=1)
        for pair in range(4):
            added = jnp.dot(hits, arrived[:, pl.ds(pair * 256, 256)], preferred_element_type=F32)
            for half, value in enumerate(split(added)):
                for l in range(2):
                    for i in range(len(bases)):
                        cells[columns[i // 2], half, pl.ds((2 * pair + l) * 48, 48), pl.ds(i % 2 * 128, 128)] = (
                            value[i * 48 : i * 48 + 48, l * 128 : l * 128 + 128]
                        )

    def stage_z(turn, q):
        high, low = cells[q, 0], cells[q, 1]
        product = jnp.dot(
            third[...], jnp.concatenate((high, high, low), axis=0), preferred_element_type=F32
        )
        near = combine(product[:, :128]).reshape(24, 8, 128)
        far = combine(product[:, 128:]).reshape(24, 8, 128)
        even = jnp.where(row < 4, near, pltpu.roll(far, 4, 1))
        odd = jnp.where(row < 4, pltpu.roll(near, 4, 1), far)
        for a in range(3):
            out_z[turn, :, 0, tile_at(turn, q, a)] = even[a * 8 : a * 8 + 8]
            out_z[turn, :, 1, tile_at(turn, q, a)] = odd[a * 8 : a * 8 + 8]

    def stage_y(parts):
        for i, (turn, a) in enumerate(parts):
            for q in range(3):
                value = in_y[turn, :, tile_at(turn, q, a)]
                for bit in range(4):
                    value = exchange_bit(value, 1 << bit, 3 + bit)
                high, low = split(value.reshape(128, 128))
                rows_y[pl.ds(i * 128, 128), pl.ds(q * 128, 128)] = high
                rows_y[pl.ds(i * 128, 128), pl.ds(N + q * 128, 128)] = high
                rows_y[pl.ds(i * 128, 128), pl.ds(2 * N + q * 128, 128)] = low
        product = lax.dot_general(
            second[...], rows_y[pl.ds(0, len(parts) * 128), :], NT, preferred_element_type=F32
        )
        for i, (turn, a) in enumerate(parts):
            done = combine(product[:, i * 128 : i * 128 + 128])
            out_y[turn, :, a] = done.reshape(ROWS, 24, 128)
            send_y(turn, pl.ds(a, 1))

    def stage_x(turn, thirds):
        values = []
        for a in range(thirds.start, thirds.start + thirds.size):
            value = in_x[turn, :, a]
            value = exchange_bit(value, 4, 6)
            value = exchange_bit(value, 2, 1)
            values.append(exchange_bit(value, 1, 0).reshape(192, 128))
        high, low = split(jnp.concatenate(values, axis=0))
        rows = jnp.concatenate((high, high, low), axis=1)
        return [
            jnp.dot(rows, table[turn], preferred_element_type=F32) for table in (first_cos, first_sin)
        ]

    def add_x(turn):
        for a in range(3):
            wait_y(turn, pl.ds(a, 1))
        return stage_x(turn, pl.ds(0, 3))

    for q in range(3):
        add_pieces(0, (q,))
        stage_z(0, q)
        send_z(0, q)
    add_pieces(1, (0, 1, 2))
    for q in range(3):
        stage_z(1, q)
    send_z(1, 0)
    send_z(1, 1)
    add_pieces(2, (0, 1, 2))
    for q in range(3):
        stage_z(2, q)
    send_z(1, 2)
    for q in range(3):
        wait_z(0, q)
    stage_y(((0, 0), (0, 1)))
    send_z(2, 0)
    wait_z(1, 0)
    stage_y(((0, 2), (1, 0)))
    send_z(2, 1)
    wait_z(1, 1)
    wait_z(1, 2)
    stage_y(((1, 1), (1, 2)))
    send_z(2, 2)
    sum_cos[...], sum_sin[...] = add_x(0)
    wait_z(2, 0)
    wait_z(2, 1)
    stage_y(((2, 0), (2, 1)))
    cos, sin = add_x(1)
    sum_cos[...] += cos
    sum_sin[...] += sin
    wait_z(2, 2)
    stage_y(((2, 2),))

    arrival(outbox.at[pl.ds(0, DEVICES - 1)], p_send)
    arrival(in_y.at[:, pl.ds(0, COLS - 1)], z_send)

    for a in range(3):
        wait_y(2, pl.ds(a, 1))
        cos, sin = stage_x(2, pl.ds(a, 1))
        cos = cos + sum_cos[pl.ds(a * 192, 192), :]
        sin = sin + sum_sin[pl.ds(a * 192, 192), :]
        out[0, pl.ds(a * 4, 4)] = (cos[:96] - sin[96:]).reshape(4, 24, M)
        out[1, pl.ds(a * 4, 4)] = (sin[:96] + cos[96:]).reshape(4, 24, M)
    arrival(in_x.at[:, pl.ds(0, ROWS - 1)], y_send)


def whole(owners, tile_ids, samples, kernel, offsets, third, second, first_cos, first_sin):
    operands = (owners, tile_ids, samples, kernel, offsets, third, second, first_cos, first_sin)
    held = [pltpu.VMEM(x.shape, x.dtype) for x in operands[:5]] + [
        pltpu.VMEM((N, 3 * N), BF16),
        pltpu.VMEM((N, 3 * N), BF16),
        pltpu.VMEM((ROUNDS, N, M), BF16),
        pltpu.VMEM((ROUNDS, N, M), BF16),
    ]
    return pl.pallas_call(
        whole_kernel,
        out_shape=jax.ShapeDtypeStruct((2, 12, 24, M), F32),
        in_specs=[pl.BlockSpec(memory_space=pl.ANY)] * len(operands),
        out_specs=pl.BlockSpec(memory_space=pltpu.VMEM),
        scratch_shapes=held
        + [
            pltpu.VMEM((BLOCKS + 1, 8, 128), F32),
            pltpu.VMEM((8, 128), F32),
            pltpu.VMEM((8, 128), jnp.int32),
            pltpu.SMEM((8, 128), jnp.int32),
            pltpu.VMEM((DEVICES, SLOT_ROWS, 128), F32),
            pltpu.VMEM((DEVICES, SLOT_ROWS, 128), F32),
            pltpu.VMEM((128, 128), F32),
            pltpu.VMEM((512, 1024), BF16),
            pltpu.VMEM((3, 2, N, 256), BF16),
            pltpu.VMEM((ROUNDS, 8, 2, 9, 8, 128), F32),
            pltpu.VMEM((ROUNDS, COLS, 9, 8, 128), F32),
            pltpu.VMEM((256, 3 * N), BF16),
            pltpu.VMEM((ROUNDS, ROWS, 3, 24, 128), F32),
            pltpu.VMEM((ROUNDS, ROWS, 3, 24, 128), F32),
            pltpu.VMEM((576, M), F32),
            pltpu.VMEM((576, M), F32),
            pltpu.SemaphoreType.REGULAR,
            pltpu.SemaphoreType.DMA((13,)),
            pltpu.SemaphoreType.DMA,
            pltpu.SemaphoreType.DMA,
            pltpu.SemaphoreType.DMA((ROWS,)),
            pltpu.SemaphoreType.DMA,
            pltpu.SemaphoreType.DMA((3 * ROUNDS,)),
            pltpu.SemaphoreType.DMA,
            pltpu.SemaphoreType.DMA((3 * ROUNDS,)),
        ],
        compiler_params=pltpu.CompilerParams(
            collective_id=0, has_side_effects=True, vmem_limit_bytes=48 << 20
        ),
        name="whole",
    )(*[pltpu.with_memory_space_constraint(x, pltpu.HBM) for x in operands])


def solution(mesh):
    third, second, first_cos, first_sin = tables()

    def on_device(samples, kernel, offsets, owners, tile_ids, deapod_first, deapod_second, deapod_third):
        along_x = whole(
            owners.reshape(1, BLOCKS),
            tile_ids.reshape(1, BLOCKS),
            samples,
            kernel,
            offsets.transpose(1, 0, 2),
            third,
            second,
            first_cos,
            first_sin,
        )
        return (
            along_x
            * deapod_third[None, :, None, None]
            * deapod_second[None, None, :, None]
            * deapod_first[None, None, None, :]
        )

    in_specs = (
        P(("gx", "gy"), None, None),
        P(("gx", "gy"), None, None, None),
        P(("gx", "gy"), None, None),
        P(("gx", "gy"), None),
        P(("gx", "gy")),
        P(),
        P("gx"),
        P("gy"),
    )
    return jax.shard_map(
        on_device, mesh=mesh, in_specs=in_specs, out_specs=P(None, "gy", "gx", None), check_vma=False
    )
```

```python
import math

import jax
import jax.numpy as jnp
import ml_dtypes
import numpy as np
from jax import lax
from jax.experimental import pallas as pl
from jax.experimental.pallas import tpu as pltpu
from jax.sharding import PartitionSpec as P

N = 384
M = 192
DEVICES = 128
ROWS, COLS = 8, 16
BLOCKS = 128
TILES = 864
SLOT_ROWS = 17
ROUNDS = 3
MESH = pl.DeviceIdType.MESH
F32 = jnp.float32
BF16 = jnp.bfloat16


def angles(cells, images):
    steps = np.mod((cells[:, None] - N // 2) * (images[None, :] - M // 2), N)
    phases = steps.astype(np.float64) * (2.0 * math.pi / N)
    return np.cos(phases) / math.sqrt(N), np.sin(phases) / math.sqrt(N)


def halves(table):
    table = table.astype(np.float32)
    high = table.astype(ml_dtypes.bfloat16)
    low = (table - high.astype(np.float32)).astype(ml_dtypes.bfloat16)
    return high, low


def left_table(cells, images):
    cos, sin = angles(cells, images)
    return np.concatenate(halves(np.concatenate((cos.T, sin.T))), axis=1)


def tables():
    every = np.arange(M)
    a, pair, side, low = np.meshgrid(np.arange(3), np.arange(8), np.arange(2), np.arange(4), indexing="ij")
    order = (12 * (2 * pair + side) + 4 * a + low).reshape(-1)
    l, d = np.meshgrid(np.arange(8), np.arange(48), indexing="ij")
    third = left_table((d * 8 + l).reshape(-1), order)
    q, g, j = np.meshgrid(np.arange(3), np.arange(COLS), np.arange(8), indexing="ij")
    second = left_table((g * 24 + q * 8 + j).reshape(-1), every)
    turn, lane = np.meshgrid(np.arange(ROUNDS), np.arange(128), indexing="ij")
    source = (lane >> 6) * 4 + (lane & 3)
    cells = source * 48 + (2 * turn + ((lane >> 2) & 1)) * 8 + ((lane >> 3) & 7)
    firsts = []
    for part in angles(cells.reshape(-1), every):
        high, low = halves(part.reshape(ROUNDS, 128, M))
        firsts.append(np.concatenate((high, low), axis=1))
    return third, second, firsts[0], firsts[1]


def split(value):
    high = value.astype(BF16)
    return high, (value - high.astype(F32)).astype(BF16)


def exchange_bit(value, axis_low, lane_bit):
    count, rows, lanes = value.shape
    shift = 1 << lane_bit
    pairs = value.reshape(count // (2 * axis_low), 2, axis_low * rows, lanes)
    first = pairs[:, 0].reshape(-1, lanes)
    second = pairs[:, 1].reshape(-1, lanes)
    lane = lax.broadcasted_iota(jnp.int32, first.shape, 1)
    upper = (lane & shift) != 0
    new_first = jnp.where(upper, pltpu.roll(second, shift, 1), first)
    new_second = jnp.where(upper, second, pltpu.roll(first, lanes - shift, 1))
    shape = (count // (2 * axis_low), axis_low * rows, lanes)
    out = jnp.stack((new_first.reshape(shape), new_second.reshape(shape)), axis=1)
    return out.reshape(value.shape)


def combine(product):
    rows = product.shape[0] // 2
    lane = lax.broadcasted_iota(jnp.int32, (rows, 128), 1)
    turned = pltpu.roll(product[rows:], 64, 1)
    return product[:rows] + jnp.where(lane < 64, -turned, turned)


NT = (((1,), (1,)), ((), ()))


def whole_kernel(
    owners_in,
    tile_ids_in,
    samples_in,
    kernel_in,
    offsets_in,
    third_in,
    second_in,
    first_cos_in,
    first_sin_in,
    scale_first_in,
    scale_second_in,
    scale_third_in,
    out,
    owners,
    tile_ids,
    samples,
    kernel,
    offsets,
    third,
    second,
    first_cos,
    first_sin,
    scale_first,
    scale_second,
    scale_third,
    pieces,
    ids,
    source_of,
    slots,
    outbox,
    inbox,
    marks,
    arrived,
    cells,
    out_z,
    in_y,
    rows_y,
    out_y,
    in_x,
    sum_cos,
    sum_sin,
    settled,
    load_sem,
    slot_sem,
    p_send,
    p_recv,
    z_send,
    z_recv,
    y_send,
    y_recv,
):
    gx, gy = lax.axis_index("gx"), lax.axis_index("gy")
    me = gx * COLS + gy

    loads = [
        pltpu.make_async_copy(source, target, load_sem.at[i])
        for i, (source, target) in enumerate(
            (
                (owners_in, owners),
                (tile_ids_in, tile_ids),
                (offsets_in, offsets),
                (samples_in, samples),
                (kernel_in, kernel),
                (third_in, third.at[:, pl.ds(0, 2 * N)]),
                (third_in.at[:, pl.ds(0, N)], third.at[:, pl.ds(2 * N, N)]),
                (second_in, second.at[:, pl.ds(0, 2 * N)]),
                (second_in.at[:, pl.ds(0, N)], second.at[:, pl.ds(2 * N, N)]),
                (first_cos_in, first_cos.at[:, pl.ds(0, 256)]),
                (first_cos_in.at[:, pl.ds(0, 128)], first_cos.at[:, pl.ds(256, 128)]),
                (first_sin_in, first_sin.at[:, pl.ds(0, 256)]),
                (first_sin_in.at[:, pl.ds(0, 128)], first_sin.at[:, pl.ds(256, 128)]),
                (scale_first_in, scale_first),
                (scale_second_in, scale_second),
                (scale_third_in, scale_third),
            )
        )
    ]
    for load in loads[:5]:
        load.start()
    barrier = pltpu.get_barrier_semaphore()

    def greet(semaphore, x, y):
        pl.semaphore_signal(semaphore, inc=1, device_id=(x, y), device_id_type=MESH)

    def in_column(k):
        return jnp.where(gy + k >= COLS, gy + k - COLS, gy + k)

    def in_row(k):
        return jnp.where(gx + k >= ROWS, gx + k - ROWS, gx + k)

    for k in range(1, COLS):
        greet(barrier, gx, in_column(k))
    for k in range(1, ROWS):
        greet(barrier, in_row(k), gy)

    loads[0].wait()
    loads[1].wait()
    lane = lax.broadcasted_iota(jnp.int32, (128, 128), 1)
    block = lax.broadcasted_iota(jnp.int32, (128, 128), 0)
    named = jnp.transpose(jnp.broadcast_to(owners[...], (128, 128))) == lane
    tiles = jnp.transpose(jnp.broadcast_to(tile_ids[...], (128, 128)))
    first = jnp.min(jnp.where(named, block, BLOCKS), axis=0, keepdims=True)
    last = jnp.max(jnp.where(named, block, -1), axis=0, keepdims=True)
    last = jnp.where(last > first, last, BLOCKS)
    source_of[pl.ds(0, 1), :] = first
    source_of[pl.ds(1, 1), :] = last
    place_slots = pltpu.make_async_copy(source_of, slots, slot_sem)
    place_slots.start()
    found = []
    for chosen in (first, last):
        tile = jnp.sum(jnp.where(named & (block == chosen), tiles, 0), axis=0, keepdims=True)
        found.append(jnp.where(chosen < BLOCKS, tile, TILES).astype(F32))
    low_lane = lax.broadcasted_iota(jnp.int32, (1, 128), 1) < 64
    ids[pl.ds(0, 1), :] = jnp.where(low_lane, found[0], pltpu.roll(found[1], 64, 1))
    ids[pl.ds(1, 1), :] = jnp.where(low_lane, pltpu.roll(found[0], 64, 1), found[1])

    for load in loads[2:5]:
        load.wait()
    pieces[BLOCKS] = jnp.zeros((8, 128), F32)
    cell = lax.broadcasted_iota(jnp.int32, (8, 128), 0)

    def spread(step):
        starts = [offsets[dim, pl.ds(pl.multiple_of(step * 32, 32), 32), :] for dim in range(3)]
        for u in range(32):
            n = step * 32 + u

            placed = []
            for dim in range(3):
                away = cell - starts[dim][u : u + 1]
                total = jnp.zeros((8, 128), F32)
                for k in range(4):
                    total = jnp.where(away == k, kernel[n, dim, pl.ds(k, 1), :], total)
                placed.append(total)
            real = samples[n, pl.ds(0, 1), :] * placed[0]
            imag = samples[n, pl.ds(1, 1), :] * placed[0]
            plane = jnp.concatenate((real, imag), axis=0)
            weight = (plane[:, None, :] * placed[1][None, :, :]).reshape(128, 128)
            high, low = split(weight)
            depth_high, depth_low = split(placed[2])
            left = jnp.concatenate(
                (
                    jnp.concatenate((depth_high, depth_high), axis=1),
                    jnp.concatenate((depth_low, jnp.zeros_like(depth_low)), axis=1),
                ),
                axis=0,
            )
            right = jnp.concatenate((high, low), axis=1)
            both = lax.dot_general(left, right, NT, preferred_element_type=F32)
            pieces[n] = both[:8] + both[8:]

    pl.loop(0, BLOCKS // 64)(spread)
    pl.semaphore_wait(barrier, COLS + ROWS - 2)
    for k in range(1, COLS):
        greet(settled, gx, in_column(k))
    pl.loop(BLOCKS // 64, BLOCKS // 32)(spread)
    place_slots.wait()

    def arrival(target, semaphore):
        pltpu.make_async_copy(target, target, semaphore).wait()

    def send_piece(peer, lands):
        return pltpu.make_async_remote_copy(
            src_ref=outbox.at[peer],
            dst_ref=inbox.at[lands],
            send_sem=p_send,
            recv_sem=p_recv.at[lands // COLS],
            device_id=(peer // COLS, lax.rem(peer, COLS)),
            device_id_type=MESH,
        )

    def fill(peer):
        outbox[peer, pl.ds(0, 8), :] = pieces[slots[0, peer]]
        outbox[peer, pl.ds(8, 8), :] = pieces[slots[1, peer]]
        outbox[peer, pl.ds(16, 1), :] = ids[pl.ds(peer // 64, 1), :]

    def send_to(x, y):
        peer = x * COLS + y
        fill(peer)
        send_piece(peer, me).start()

    @pl.loop(1, COLS)
    def _(k):
        send_to(gx, in_column(k))

    @pl.loop(1, ROWS)
    def _(k):
        send_to(in_row(k), gy)

    pl.semaphore_wait(settled, COLS - 1)

    @pl.loop(1, ROWS)
    def _(i):
        @pl.loop(1, COLS)
        def _(k):
            send_to(in_row(i), in_column(k))

    for load in loads[5:]:
        load.start()
    fill(me)
    pltpu.make_async_copy(outbox.at[me], inbox.at[me], p_recv.at[gx]).start()

    @pl.loop(0, ROWS)
    def _(t):
        group = lax.rem(gx + ROWS - t, ROWS)

        base = pl.multiple_of(group * COLS, COLS)
        arrival(inbox.at[pl.ds(base, COLS)], p_recv.at[group])
        for slot in range(2):
            for l in range(8):
                high, low = split(inbox[pl.ds(base, COLS), slot * 8 + l, :])
                arrived[pl.ds(pl.multiple_of(base + slot * 128, 16), COLS), pl.ds(l * 128, 128)] = high
                arrived[pl.ds(pl.multiple_of(base + 256 + slot * 128, 16), COLS), pl.ds(l * 128, 128)] = low

    marks[...] = jnp.transpose(inbox[:, 16, :])
    mine = lax.rem(me, 64)
    tile_rows = [marks[pl.ds(mine + 64 * slot, 1), :] for slot in range(2)]
    for load in loads[5:]:
        load.wait()

    def tile_at(turn, q, a):
        return q * 3 + a if turn == 0 else a * 3 + q

    def part(third_of):
        return pl.ds(3 * third_of, 3)

    def send_z(turn, third_of):
        tiles_of = part(third_of)
        count = turn * 3 + third_of

        @pl.loop(1, COLS)
        def _(k):
            peer = lax.rem(gy + k, COLS)
            pltpu.make_async_remote_copy(
                src_ref=out_z.at[turn, peer // 2, lax.rem(peer, 2), tiles_of],
                dst_ref=in_y.at[turn, gy, tiles_of],
                send_sem=z_send,
                recv_sem=z_recv.at[count],
                device_id=(gx, peer),
                device_id_type=MESH,
            ).start()

        pltpu.make_async_copy(
            out_z.at[turn, gy // 2, lax.rem(gy, 2), tiles_of], in_y.at[turn, gy, tiles_of], z_recv.at[count]
        ).start()

    def wait_z(turn, third_of):
        arrival(in_y.at[turn, :, part(third_of)], z_recv.at[turn * 3 + third_of])

    def send_y(turn, thirds):
        count = turn * 3 + thirds.start

        @pl.loop(1, ROWS)
        def _(k):
            peer = lax.rem(gx + k, ROWS)
            pltpu.make_async_remote_copy(
                src_ref=out_y.at[turn, peer, thirds],
                dst_ref=in_x.at[turn, gx, thirds],
                send_sem=y_send,
                recv_sem=y_recv.at[count],
                device_id=(peer, gy),
                device_id_type=MESH,
            ).start()

        pltpu.make_async_copy(
            out_y.at[turn, gx, thirds], in_x.at[turn, gx, thirds], y_recv.at[count]
        ).start()

    def wait_y(turn, thirds):
        arrival(in_x.at[turn, :, thirds], y_recv.at[turn * 3 + thirds.start])

    tile_of = lax.broadcasted_iota(jnp.int32, (48, 128), 0)

    def add_pieces(turn, columns):
        bases = [((2 * turn + r) * 3 + q) * 48 for q in columns for r in range(2)]
        hits = [
            jnp.concatenate(
                [jnp.where((tile_of + base).astype(F32) == tile_row, 1.0, 0.0) for base in bases], axis=0
            ).astype(BF16)
            for tile_row in tile_rows
        ]
        hits = jnp.concatenate(hits + hits, axis=1)
        for pair in range(4):
            added = jnp.dot(hits, arrived[:, pl.ds(pair * 256, 256)], preferred_element_type=F32)
            for half, value in enumerate(split(added)):
                for l in range(2):
                    for i in range(len(bases)):
                        cells[columns[i // 2], half, pl.ds((2 * pair + l) * 48, 48), pl.ds(i % 2 * 128, 128)] = (
                            value[i * 48 : i * 48 + 48, l * 128 : l * 128 + 128]
                        )

    def place_z(product, turn, q, thirds):
        count = 8 * len(thirds)
        near = combine(product[:, :128]).reshape(count, 8, 128)
        far = combine(product[:, 128:]).reshape(count, 8, 128)
        row = lax.broadcasted_iota(jnp.int32, (count, 8, 128), 1)
        even = jnp.where(row < 4, near, pltpu.roll(far, 4, 1))
        odd = jnp.where(row < 4, pltpu.roll(near, 4, 1), far)
        for i, a in enumerate(thirds):
            out_z[turn, :, 0, tile_at(turn, q, a)] = even[i * 8 : i * 8 + 8]
            out_z[turn, :, 1, tile_at(turn, q, a)] = odd[i * 8 : i * 8 + 8]

    def stage_z(turn, q):
        high, low = cells[q, 0], cells[q, 1]
        product = jnp.dot(
            third[...], jnp.concatenate((high, high, low), axis=0), preferred_element_type=F32
        )
        place_z(product, turn, q, range(3))

    def stage_y(parts):
        for i, (turn, a) in enumerate(parts):
            for q in range(3):
                value = in_y[turn, :, tile_at(turn, q, a)]
                for bit in range(4):
                    value = exchange_bit(value, 1 << bit, 3 + bit)
                high, low = split(value.reshape(128, 128))
                rows_y[pl.ds(i * 128, 128), pl.ds(q * 128, 128)] = high
                rows_y[pl.ds(i * 128, 128), pl.ds(N + q * 128, 128)] = high
                rows_y[pl.ds(i * 128, 128), pl.ds(2 * N + q * 128, 128)] = low
        product = lax.dot_general(
            second[...], rows_y[pl.ds(0, len(parts) * 128), :], NT, preferred_element_type=F32
        )
        for i, (turn, a) in enumerate(parts):
            done = combine(product[:, i * 128 : i * 128 + 128])
            out_y[turn, :, a] = done.reshape(ROWS, 24, 128)
            send_y(turn, pl.ds(a, 1))

    def stage_x(turn, thirds):
        values = []
        for a in range(thirds.start, thirds.start + thirds.size):
            value = in_x[turn, :, a]
            value = exchange_bit(value, 4, 6)
            value = exchange_bit(value, 2, 1)
            values.append(exchange_bit(value, 1, 0).reshape(192, 128))
        high, low = split(jnp.concatenate(values, axis=0))
        rows = jnp.concatenate((high, high, low), axis=1)
        return [
            jnp.dot(rows, table[turn], preferred_element_type=F32) for table in (first_cos, first_sin)
        ]

    def add_x(turn):
        for a in range(3):
            wait_y(turn, pl.ds(a, 1))
        return stage_x(turn, pl.ds(0, 3))

    for q in range(3):
        add_pieces(0, (q,))
        stage_z(0, q)
        send_z(0, q)
    add_pieces(1, (0, 1, 2))
    for q in range(3):
        stage_z(1, q)
    send_z(1, 0)
    send_z(1, 1)
    add_pieces(2, (0, 1, 2))
    for q in range(3):
        stage_z(2, q)
    send_z(1, 2)
    for q in range(3):
        wait_z(0, q)
    stage_y(((0, 0), (0, 1)))
    send_z(2, 0)
    wait_z(1, 0)
    stage_y(((0, 2), (1, 0)))
    send_z(2, 1)
    wait_z(1, 1)
    wait_z(1, 2)
    stage_y(((1, 1), (1, 2)))
    send_z(2, 2)
    wait_z(2, 0)
    wait_z(2, 1)
    stage_y(((2, 0), (2, 1)))
    wait_z(2, 2)
    stage_y(((2, 2),))
    sum_cos[...], sum_sin[...] = add_x(0)
    cos, sin = add_x(1)
    sum_cos[...] += cos
    sum_sin[...] += sin

    diagonal = lax.broadcasted_iota(jnp.int32, (24, 24), 0) == lax.broadcasted_iota(jnp.int32, (24, 24), 1)
    column = jnp.sum(jnp.where(diagonal, scale_second[...], 0.0), axis=1, keepdims=True)
    plane = column * scale_first[...]

    arrival(outbox.at[pl.ds(0, DEVICES - 1)], p_send)
    arrival(in_y.at[:, pl.ds(0, COLS - 1)], z_send)

    for a in range(3):
        wait_y(2, pl.ds(a, 1))
        cos, sin = stage_x(2, pl.ds(a, 1))
        cos = cos + sum_cos[pl.ds(a * 192, 192), :]
        sin = sin + sum_sin[pl.ds(a * 192, 192), :]
        real = (cos[:96] - sin[96:]).reshape(4, 24, M)
        imag = (sin[:96] + cos[96:]).reshape(4, 24, M)
        for b in range(4):
            scale = plane * scale_third[0, a * 4 + b]
            out[0, a * 4 + b] = real[b] * scale
            out[1, a * 4 + b] = imag[b] * scale
    arrival(in_x.at[:, pl.ds(0, ROWS - 1)], y_send)


def whole(*operands):
    held = [pltpu.VMEM(x.shape, x.dtype) for x in operands[:5]] + [
        pltpu.VMEM((N, 3 * N), BF16),
        pltpu.VMEM((N, 3 * N), BF16),
        pltpu.VMEM((ROUNDS, N, M), BF16),
        pltpu.VMEM((ROUNDS, N, M), BF16),
        pltpu.VMEM((1, M), F32),
        pltpu.VMEM((1, 24), F32),
        pltpu.SMEM((1, 12), F32),
    ]
    return pl.pallas_call(
        whole_kernel,
        out_shape=jax.ShapeDtypeStruct((2, 12, 24, M), F32),
        in_specs=[pl.BlockSpec(memory_space=pl.ANY)] * len(operands),
        out_specs=pl.BlockSpec(memory_space=pltpu.VMEM),
        scratch_shapes=held
        + [
            pltpu.VMEM((BLOCKS + 1, 8, 128), F32),
            pltpu.VMEM((8, 128), F32),
            pltpu.VMEM((8, 128), jnp.int32),
            pltpu.SMEM((8, 128), jnp.int32),
            pltpu.VMEM((DEVICES, SLOT_ROWS, 128), F32),
            pltpu.VMEM((DEVICES, SLOT_ROWS, 128), F32),
            pltpu.VMEM((128, 128), F32),
            pltpu.VMEM((512, 1024), BF16),
            pltpu.VMEM((3, 2, N, 256), BF16),
            pltpu.VMEM((ROUNDS, 8, 2, 9, 8, 128), F32),
            pltpu.VMEM((ROUNDS, COLS, 9, 8, 128), F32),
            pltpu.VMEM((256, 3 * N), BF16),
            pltpu.VMEM((ROUNDS, ROWS, 3, 24, 128), F32),
            pltpu.VMEM((ROUNDS, ROWS, 3, 24, 128), F32),
            pltpu.VMEM((576, M), F32),
            pltpu.VMEM((576, M), F32),
            pltpu.SemaphoreType.REGULAR,
            pltpu.SemaphoreType.DMA((16,)),
            pltpu.SemaphoreType.DMA,
            pltpu.SemaphoreType.DMA,
            pltpu.SemaphoreType.DMA((ROWS,)),
            pltpu.SemaphoreType.DMA,
            pltpu.SemaphoreType.DMA((3 * ROUNDS,)),
            pltpu.SemaphoreType.DMA,
            pltpu.SemaphoreType.DMA((3 * ROUNDS,)),
        ],
        compiler_params=pltpu.CompilerParams(
            collective_id=0, has_side_effects=True, vmem_limit_bytes=48 << 20
        ),
        name="whole",
    )(*[pltpu.with_memory_space_constraint(x, pltpu.HBM) for x in operands])


def solution(mesh):
    third, second, first_cos, first_sin = tables()

    def on_device(samples, kernel, offsets, owners, tile_ids, deapod_first, deapod_second, deapod_third):
        return whole(
            owners.reshape(1, BLOCKS),
            tile_ids.reshape(1, BLOCKS),
            samples,
            kernel,
            offsets.transpose(1, 0, 2),
            third,
            second,
            first_cos,
            first_sin,
            deapod_first.reshape(1, M),
            deapod_second.reshape(1, 24),
            deapod_third.reshape(1, 12),
        )

    in_specs = (
        P(("gx", "gy"), None, None),
        P(("gx", "gy"), None, None, None),
        P(("gx", "gy"), None, None),
        P(("gx", "gy"), None),
        P(("gx", "gy")),
        P(),
        P("gx"),
        P("gy"),
    )
    return jax.shard_map(
        on_device, mesh=mesh, in_specs=in_specs, out_specs=P(None, "gy", "gx", None), check_vma=False
    )
```

```python
import math

import jax
import jax.numpy as jnp
import ml_dtypes
import numpy as np
from jax import lax
from jax.experimental import pallas as pl
from jax.experimental.pallas import tpu as pltpu
from jax.sharding import PartitionSpec as P

N = 384
M = 192
DEVICES = 128
ROWS, COLS = 8, 16
BLOCKS = 128
TILES = 864
SLOT_ROWS = 17
ROUNDS = 3
MESH = pl.DeviceIdType.MESH
F32 = jnp.float32
BF16 = jnp.bfloat16


def angles(cells, images):
    steps = np.mod((cells[:, None] - N // 2) * (images[None, :] - M // 2), N)
    phases = steps.astype(np.float64) * (2.0 * math.pi / N)
    return np.cos(phases) / math.sqrt(N), np.sin(phases) / math.sqrt(N)


def halves(table):
    table = table.astype(np.float32)
    high = table.astype(ml_dtypes.bfloat16)
    low = (table - high.astype(np.float32)).astype(ml_dtypes.bfloat16)
    return high, low


def left_table(cells, images):
    cos, sin = angles(cells, images)
    return np.concatenate(halves(np.concatenate((cos.T, sin.T))), axis=1)


def tables():
    every = np.arange(M)
    a, pair, side, low = np.meshgrid(np.arange(3), np.arange(8), np.arange(2), np.arange(4), indexing="ij")
    order = (12 * (2 * pair + side) + 4 * a + low).reshape(-1)
    l, d = np.meshgrid(np.arange(8), np.arange(48), indexing="ij")
    third = left_table((d * 8 + l).reshape(-1), order)
    q, g, j = np.meshgrid(np.arange(3), np.arange(COLS), np.arange(8), indexing="ij")
    second = left_table((g * 24 + q * 8 + j).reshape(-1), every)
    turn, lane = np.meshgrid(np.arange(ROUNDS), np.arange(128), indexing="ij")
    source = (lane >> 6) * 4 + (lane & 3)
    cells = source * 48 + (2 * turn + ((lane >> 2) & 1)) * 8 + ((lane >> 3) & 7)
    firsts = []
    for part in angles(cells.reshape(-1), every):
        high, low = halves(part.reshape(ROUNDS, 128, M))
        firsts.append(np.concatenate((high, low), axis=1))
    return third, second, firsts[0], firsts[1]


def split(value):
    high = value.astype(BF16)
    return high, (value - high.astype(F32)).astype(BF16)


def exchange_bit(value, axis_low, lane_bit):
    count, rows, lanes = value.shape
    shift = 1 << lane_bit
    pairs = value.reshape(count // (2 * axis_low), 2, axis_low * rows, lanes)
    first = pairs[:, 0].reshape(-1, lanes)
    second = pairs[:, 1].reshape(-1, lanes)
    lane = lax.broadcasted_iota(jnp.int32, first.shape, 1)
    upper = (lane & shift) != 0
    new_first = jnp.where(upper, pltpu.roll(second, shift, 1), first)
    new_second = jnp.where(upper, second, pltpu.roll(first, lanes - shift, 1))
    shape = (count // (2 * axis_low), axis_low * rows, lanes)
    out = jnp.stack((new_first.reshape(shape), new_second.reshape(shape)), axis=1)
    return out.reshape(value.shape)


def combine(product):
    rows = product.shape[0] // 2
    lane = lax.broadcasted_iota(jnp.int32, (rows, 128), 1)
    turned = pltpu.roll(product[rows:], 64, 1)
    return product[:rows] + jnp.where(lane < 64, -turned, turned)


NT = (((1,), (1,)), ((), ()))


def whole_kernel(
    owners_in,
    tile_ids_in,
    samples_in,
    kernel_in,
    offsets_in,
    third_in,
    second_in,
    first_cos_in,
    first_sin_in,
    scale_first_in,
    scale_second_in,
    scale_third_in,
    out,
    owners,
    tile_ids,
    samples,
    kernel,
    offsets,
    third,
    second,
    first_cos,
    first_sin,
    scale_first,
    scale_second,
    scale_third,
    pieces,
    ids,
    source_of,
    slots,
    outbox,
    inbox,
    marks,
    arrived,
    cells,
    out_z,
    in_y,
    rows_y,
    out_y,
    in_x,
    sum_cos,
    sum_sin,
    settled,
    load_sem,
    slot_sem,
    p_send,
    p_recv,
    z_send,
    z_recv,
    y_send,
    y_recv,
):
    gx, gy = lax.axis_index("gx"), lax.axis_index("gy")
    me = gx * COLS + gy

    loads = [
        pltpu.make_async_copy(source, target, load_sem.at[i])
        for i, (source, target) in enumerate(
            (
                (owners_in, owners),
                (tile_ids_in, tile_ids),
                (offsets_in, offsets),
                (samples_in, samples),
                (kernel_in, kernel),
                (third_in, third.at[:, pl.ds(0, 2 * N)]),
                (third_in.at[:, pl.ds(0, N)], third.at[:, pl.ds(2 * N, N)]),
                (second_in, second.at[:, pl.ds(0, 2 * N)]),
                (second_in.at[:, pl.ds(0, N)], second.at[:, pl.ds(2 * N, N)]),
                (first_cos_in, first_cos.at[:, pl.ds(0, 256)]),
                (first_cos_in.at[:, pl.ds(0, 128)], first_cos.at[:, pl.ds(256, 128)]),
                (first_sin_in, first_sin.at[:, pl.ds(0, 256)]),
                (first_sin_in.at[:, pl.ds(0, 128)], first_sin.at[:, pl.ds(256, 128)]),
                (scale_first_in, scale_first),
                (scale_second_in, scale_second),
                (scale_third_in, scale_third),
            )
        )
    ]
    for load in loads[:5]:
        load.start()
    barrier = pltpu.get_barrier_semaphore()

    def greet(semaphore, x, y):
        pl.semaphore_signal(semaphore, inc=1, device_id=(x, y), device_id_type=MESH)

    def in_column(k):
        return jnp.where(gy + k >= COLS, gy + k - COLS, gy + k)

    def in_row(k):
        return jnp.where(gx + k >= ROWS, gx + k - ROWS, gx + k)

    for k in range(1, COLS):
        greet(barrier, gx, in_column(k))
    for k in range(1, ROWS):
        greet(barrier, in_row(k), gy)

    loads[0].wait()
    loads[1].wait()
    lane = lax.broadcasted_iota(jnp.int32, (128, 128), 1)
    block = lax.broadcasted_iota(jnp.int32, (128, 128), 0)
    named = jnp.transpose(jnp.broadcast_to(owners[...], (128, 128))) == lane
    tiles = jnp.transpose(jnp.broadcast_to(tile_ids[...], (128, 128)))
    first = jnp.min(jnp.where(named, block, BLOCKS), axis=0, keepdims=True)
    last = jnp.max(jnp.where(named, block, -1), axis=0, keepdims=True)
    last = jnp.where(last > first, last, BLOCKS)
    source_of[pl.ds(0, 1), :] = first
    source_of[pl.ds(1, 1), :] = last
    place_slots = pltpu.make_async_copy(source_of, slots, slot_sem)
    place_slots.start()
    found = []
    for chosen in (first, last):
        tile = jnp.sum(jnp.where(named & (block == chosen), tiles, 0), axis=0, keepdims=True)
        found.append(jnp.where(chosen < BLOCKS, tile, TILES).astype(F32))
    low_lane = lax.broadcasted_iota(jnp.int32, (1, 128), 1) < 64
    ids[pl.ds(0, 1), :] = jnp.where(low_lane, found[0], pltpu.roll(found[1], 64, 1))
    ids[pl.ds(1, 1), :] = jnp.where(low_lane, pltpu.roll(found[0], 64, 1), found[1])

    for load in loads[2:5]:
        load.wait()
    pieces[BLOCKS] = jnp.zeros((8, 128), F32)
    cell = lax.broadcasted_iota(jnp.int32, (8, 128), 0)

    def spread(step):
        starts = [offsets[dim, pl.ds(pl.multiple_of(step * 32, 32), 32), :] for dim in range(3)]
        for u in range(32):
            n = step * 32 + u

            placed = []
            for dim in range(3):
                away = cell - starts[dim][u : u + 1]
                total = jnp.zeros((8, 128), F32)
                for k in range(4):
                    total = jnp.where(away == k, kernel[n, dim, pl.ds(k, 1), :], total)
                placed.append(total)
            real = samples[n, pl.ds(0, 1), :] * placed[0]
            imag = samples[n, pl.ds(1, 1), :] * placed[0]
            plane = jnp.concatenate((real, imag), axis=0)
            weight = (plane[:, None, :] * placed[1][None, :, :]).reshape(128, 128)
            high, low = split(weight)
            depth_high, depth_low = split(placed[2])
            left = jnp.concatenate(
                (
                    jnp.concatenate((depth_high, depth_high), axis=1),
                    jnp.concatenate((depth_low, jnp.zeros_like(depth_low)), axis=1),
                ),
                axis=0,
            )
            right = jnp.concatenate((high, low), axis=1)
            both = lax.dot_general(left, right, NT, preferred_element_type=F32)
            pieces[n] = both[:8] + both[8:]

    pl.loop(0, BLOCKS // 64)(spread)
    pl.semaphore_wait(barrier, COLS + ROWS - 2)
    for k in range(1, COLS):
        greet(settled, gx, in_column(k))
    pl.loop(BLOCKS // 64, BLOCKS // 32)(spread)
    place_slots.wait()

    def arrival(target, semaphore):
        pltpu.make_async_copy(target, target, semaphore).wait()

    def send_piece(peer, lands):
        return pltpu.make_async_remote_copy(
            src_ref=outbox.at[peer],
            dst_ref=inbox.at[lands],
            send_sem=p_send,
            recv_sem=p_recv.at[lands // COLS],
            device_id=(peer // COLS, lax.rem(peer, COLS)),
            device_id_type=MESH,
        )

    def fill(peer):
        outbox[peer, pl.ds(0, 8), :] = pieces[slots[0, peer]]
        outbox[peer, pl.ds(8, 8), :] = pieces[slots[1, peer]]
        outbox[peer, pl.ds(16, 1), :] = ids[pl.ds(peer // 64, 1), :]

    def send_to(x, y):
        peer = x * COLS + y
        fill(peer)
        send_piece(peer, me).start()

    @pl.loop(1, COLS)
    def _(k):
        send_to(gx, in_column(k))

    @pl.loop(1, ROWS)
    def _(k):
        send_to(in_row(k), gy)

    pl.semaphore_wait(settled, COLS - 1)

    @pl.loop(1, ROWS)
    def _(i):
        @pl.loop(1, COLS)
        def _(k):
            send_to(in_row(i), in_column(k))

    for load in loads[5:]:
        load.start()
    fill(me)
    pltpu.make_async_copy(outbox.at[me], inbox.at[me], p_recv.at[gx]).start()

    @pl.loop(0, ROWS)
    def _(t):
        group = lax.rem(gx + ROWS - t, ROWS)

        base = pl.multiple_of(group * COLS, COLS)
        arrival(inbox.at[pl.ds(base, COLS)], p_recv.at[group])
        for slot in range(2):
            for l in range(8):
                high, low = split(inbox[pl.ds(base, COLS), slot * 8 + l, :])
                arrived[pl.ds(pl.multiple_of(base + slot * 128, 16), COLS), pl.ds(l * 128, 128)] = high
                arrived[pl.ds(pl.multiple_of(base + 256 + slot * 128, 16), COLS), pl.ds(l * 128, 128)] = low

    marks[...] = jnp.transpose(inbox[:, 16, :])
    mine = lax.rem(me, 64)
    tile_rows = [marks[pl.ds(mine + 64 * slot, 1), :] for slot in range(2)]
    for load in loads[5:]:
        load.wait()

    def tile_at(turn, q, a):
        return q * 3 + a if turn == 0 else a * 3 + q

    def part(third_of):
        return pl.ds(3 * third_of, 3)

    def send_z(turn, third_of):
        tiles_of = part(third_of)
        count = turn * 3 + third_of

        @pl.loop(1, COLS, unroll=3)
        def _(k):
            peer = in_column(k)
            pltpu.make_async_remote_copy(
                src_ref=out_z.at[turn, peer // 2, lax.rem(peer, 2), tiles_of],
                dst_ref=in_y.at[turn, gy, tiles_of],
                send_sem=z_send,
                recv_sem=z_recv.at[count],
                device_id=(gx, peer),
                device_id_type=MESH,
            ).start()

        pltpu.make_async_copy(
            out_z.at[turn, gy // 2, lax.rem(gy, 2), tiles_of], in_y.at[turn, gy, tiles_of], z_recv.at[count]
        ).start()

    def wait_z(turn, third_of):
        arrival(in_y.at[turn, :, part(third_of)], z_recv.at[turn * 3 + third_of])

    def send_y(turn, thirds):
        count = turn * 3 + thirds.start

        @pl.loop(1, ROWS, unroll=7)
        def _(k):
            peer = in_row(k)
            pltpu.make_async_remote_copy(
                src_ref=out_y.at[turn, peer, thirds],
                dst_ref=in_x.at[turn, gx, thirds],
                send_sem=y_send,
                recv_sem=y_recv.at[count],
                device_id=(peer, gy),
                device_id_type=MESH,
            ).start()

        pltpu.make_async_copy(
            out_y.at[turn, gx, thirds], in_x.at[turn, gx, thirds], y_recv.at[count]
        ).start()

    def wait_y(turn, thirds):
        arrival(in_x.at[turn, :, thirds], y_recv.at[turn * 3 + thirds.start])

    tile_of = lax.broadcasted_iota(jnp.int32, (48, 128), 0)

    def add_pieces(turn, columns):
        bases = [((2 * turn + r) * 3 + q) * 48 for q in columns for r in range(2)]
        hits = [
            jnp.concatenate(
                [jnp.where((tile_of + base).astype(F32) == tile_row, 1.0, 0.0) for base in bases], axis=0
            ).astype(BF16)
            for tile_row in tile_rows
        ]
        hits = jnp.concatenate(hits + hits, axis=1)
        for pair in range(4):
            added = jnp.dot(hits, arrived[:, pl.ds(pair * 256, 256)], preferred_element_type=F32)
            for half, value in enumerate(split(added)):
                for l in range(2):
                    for i in range(len(bases)):
                        cells[columns[i // 2], half, pl.ds((2 * pair + l) * 48, 48), pl.ds(i % 2 * 128, 128)] = (
                            value[i * 48 : i * 48 + 48, l * 128 : l * 128 + 128]
                        )

    def place_z(product, turn, q, thirds):
        count = 8 * len(thirds)
        near = combine(product[:, :128]).reshape(count, 8, 128)
        far = combine(product[:, 128:]).reshape(count, 8, 128)
        row = lax.broadcasted_iota(jnp.int32, (count, 8, 128), 1)
        even = jnp.where(row < 4, near, pltpu.roll(far, 4, 1))
        odd = jnp.where(row < 4, pltpu.roll(near, 4, 1), far)
        for i, a in enumerate(thirds):
            out_z[turn, :, 0, tile_at(turn, q, a)] = even[i * 8 : i * 8 + 8]
            out_z[turn, :, 1, tile_at(turn, q, a)] = odd[i * 8 : i * 8 + 8]

    def stage_z(turn, q):
        high, low = cells[q, 0], cells[q, 1]
        product = jnp.dot(
            third[...], jnp.concatenate((high, high, low), axis=0), preferred_element_type=F32
        )
        place_z(product, turn, q, range(3))

    def stage_y(parts):
        for i, (turn, a) in enumerate(parts):
            for q in range(3):
                value = in_y[turn, :, tile_at(turn, q, a)]
                for bit in range(4):
                    value = exchange_bit(value, 1 << bit, 3 + bit)
                high, low = split(value.reshape(128, 128))
                rows_y[pl.ds(i * 128, 128), pl.ds(q * 128, 128)] = high
                rows_y[pl.ds(i * 128, 128), pl.ds(N + q * 128, 128)] = high
                rows_y[pl.ds(i * 128, 128), pl.ds(2 * N + q * 128, 128)] = low
        product = lax.dot_general(
            second[...], rows_y[pl.ds(0, len(parts) * 128), :], NT, preferred_element_type=F32
        )
        for i, (turn, a) in enumerate(parts):
            done = combine(product[:, i * 128 : i * 128 + 128])
            out_y[turn, :, a] = done.reshape(ROWS, 24, 128)
            send_y(turn, pl.ds(a, 1))

    def stage_x(turn, thirds):
        values = []
        for a in range(thirds.start, thirds.start + thirds.size):
            value = in_x[turn, :, a]
            value = exchange_bit(value, 4, 6)
            value = exchange_bit(value, 2, 1)
            values.append(exchange_bit(value, 1, 0).reshape(192, 128))
        high, low = split(jnp.concatenate(values, axis=0))
        rows = jnp.concatenate((high, high, low), axis=1)
        return [
            jnp.dot(rows, table[turn], preferred_element_type=F32) for table in (first_cos, first_sin)
        ]

    def add_x(turn):
        for a in range(3):
            wait_y(turn, pl.ds(a, 1))
        return stage_x(turn, pl.ds(0, 3))

    for q in range(3):
        add_pieces(0, (q,))
        stage_z(0, q)
        send_z(0, q)
    add_pieces(1, (0, 1, 2))
    for q in range(3):
        stage_z(1, q)
    send_z(1, 0)
    send_z(1, 1)
    add_pieces(2, (0, 1, 2))
    for q in range(3):
        stage_z(2, q)
    send_z(1, 2)
    for q in range(3):
        wait_z(0, q)
    stage_y(((0, 0), (0, 1)))
    send_z(2, 0)
    wait_z(1, 0)
    stage_y(((0, 2), (1, 0)))
    send_z(2, 1)
    wait_z(1, 1)
    wait_z(1, 2)
    stage_y(((1, 1), (1, 2)))
    send_z(2, 2)
    wait_z(2, 0)
    wait_z(2, 1)
    stage_y(((2, 0), (2, 1)))
    wait_z(2, 2)
    stage_y(((2, 2),))
    sum_cos[...], sum_sin[...] = add_x(0)
    cos, sin = add_x(1)
    sum_cos[...] += cos
    sum_sin[...] += sin

    diagonal = lax.broadcasted_iota(jnp.int32, (24, 24), 0) == lax.broadcasted_iota(jnp.int32, (24, 24), 1)
    column = jnp.sum(jnp.where(diagonal, scale_second[...], 0.0), axis=1, keepdims=True)
    plane = column * scale_first[...]

    arrival(outbox.at[pl.ds(0, DEVICES - 1)], p_send)
    arrival(in_y.at[:, pl.ds(0, COLS - 1)], z_send)

    for a in range(3):
        wait_y(2, pl.ds(a, 1))
        cos, sin = stage_x(2, pl.ds(a, 1))
        cos = cos + sum_cos[pl.ds(a * 192, 192), :]
        sin = sin + sum_sin[pl.ds(a * 192, 192), :]
        real = (cos[:96] - sin[96:]).reshape(4, 24, M)
        imag = (sin[:96] + cos[96:]).reshape(4, 24, M)
        for b in range(4):
            scale = plane * scale_third[0, a * 4 + b]
            out[0, a * 4 + b] = real[b] * scale
            out[1, a * 4 + b] = imag[b] * scale
    arrival(in_x.at[:, pl.ds(0, ROWS - 1)], y_send)


def whole(*operands):
    held = [pltpu.VMEM(x.shape, x.dtype) for x in operands[:5]] + [
        pltpu.VMEM((N, 3 * N), BF16),
        pltpu.VMEM((N, 3 * N), BF16),
        pltpu.VMEM((ROUNDS, N, M), BF16),
        pltpu.VMEM((ROUNDS, N, M), BF16),
        pltpu.VMEM((1, M), F32),
        pltpu.VMEM((1, 24), F32),
        pltpu.SMEM((1, 12), F32),
    ]
    return pl.pallas_call(
        whole_kernel,
        out_shape=jax.ShapeDtypeStruct((2, 12, 24, M), F32),
        in_specs=[pl.BlockSpec(memory_space=pl.ANY)] * len(operands),
        out_specs=pl.BlockSpec(memory_space=pltpu.VMEM),
        scratch_shapes=held
        + [
            pltpu.VMEM((BLOCKS + 1, 8, 128), F32),
            pltpu.VMEM((8, 128), F32),
            pltpu.VMEM((8, 128), jnp.int32),
            pltpu.SMEM((8, 128), jnp.int32),
            pltpu.VMEM((DEVICES, SLOT_ROWS, 128), F32),
            pltpu.VMEM((DEVICES, SLOT_ROWS, 128), F32),
            pltpu.VMEM((128, 128), F32),
            pltpu.VMEM((512, 1024), BF16),
            pltpu.VMEM((3, 2, N, 256), BF16),
            pltpu.VMEM((ROUNDS, 8, 2, 9, 8, 128), F32),
            pltpu.VMEM((ROUNDS, COLS, 9, 8, 128), F32),
            pltpu.VMEM((256, 3 * N), BF16),
            pltpu.VMEM((ROUNDS, ROWS, 3, 24, 128), F32),
            pltpu.VMEM((ROUNDS, ROWS, 3, 24, 128), F32),
            pltpu.VMEM((576, M), F32),
            pltpu.VMEM((576, M), F32),
            pltpu.SemaphoreType.REGULAR,
            pltpu.SemaphoreType.DMA((16,)),
            pltpu.SemaphoreType.DMA,
            pltpu.SemaphoreType.DMA,
            pltpu.SemaphoreType.DMA((ROWS,)),
            pltpu.SemaphoreType.DMA,
            pltpu.SemaphoreType.DMA((3 * ROUNDS,)),
            pltpu.SemaphoreType.DMA,
            pltpu.SemaphoreType.DMA((3 * ROUNDS,)),
        ],
        compiler_params=pltpu.CompilerParams(
            collective_id=0, has_side_effects=True, vmem_limit_bytes=48 << 20
        ),
        name="whole",
    )(*[pltpu.with_memory_space_constraint(x, pltpu.HBM) for x in operands])


def solution(mesh):
    third, second, first_cos, first_sin = tables()

    def on_device(samples, kernel, offsets, owners, tile_ids, deapod_first, deapod_second, deapod_third):
        return whole(
            owners.reshape(1, BLOCKS),
            tile_ids.reshape(1, BLOCKS),
            samples,
            kernel,
            offsets.transpose(1, 0, 2),
            third,
            second,
            first_cos,
            first_sin,
            deapod_first.reshape(1, M),
            deapod_second.reshape(1, 24),
            deapod_third.reshape(1, 12),
        )

    in_specs = (
        P(("gx", "gy"), None, None),
        P(("gx", "gy"), None, None, None),
        P(("gx", "gy"), None, None),
        P(("gx", "gy"), None),
        P(("gx", "gy")),
        P(),
        P("gx"),
        P("gy"),
    )
    return jax.shard_map(
        on_device, mesh=mesh, in_specs=in_specs, out_specs=P(None, "gy", "gx", None), check_vma=False
    )
```
